32 devices in a mesh: dp: 4 (over y, core), row: 2 (over x), col: 4 (over z).
Axes of the slice: x: 2, y: 2, z: 4, core: 2. Of those that a mesh axis runs over, the one named last changes fastest.
Arguments:
- inputs: bfloat16 [4096, 2048], P(('dp', 'col'), 'row'), may hold values from -6 to 6
- first_gain: float32 [1, 2048], P(None, 'row'), may hold values from 0.25 to 1.75
- first_shift: float32 [1, 2048], P(None, 'row'), may hold values from -3 to 3
- project_in: bfloat16 [1, 2048, 3, 2048], P(None, 'row', None, 'col'), may hold values from -0.125 to 0.125
- project_bias: float32 [1, 3, 2048], P(None, None, 'col'), may hold values from -3 to 3
- project_out: bfloat16 [1, 2048, 2048], P(None, 'col', 'row'), may hold values from -0.75 to 0.75
- second_gain: float32 [1, 2048], P(None, 'row'), may hold values from 0.25 to 1.75
- second_shift: float32 [1, 2048], P(None, 'row'), may hold values from -3 to 3
- gate_weight: bfloat16 [1, 2048, 2, 5632], P(None, 'row', None, 'col'), may hold values from -0.125 to 0.125
- down_weight: bfloat16 [1, 5632, 2048], P(None, 'col', 'row'), may hold values from -0.078125 to 0.078125
- cotangent: bfloat16 [4096, 2048], P(('dp', 'col'), 'row'), may hold values from -6 to 6
Outputs:
- layer_outputs: bfloat16 [1, 4096, 2048], P(None, ('dp', 'col'), 'row')
- input_grad: float32 [4096, 2048], P(('dp', 'col'), 'row')
- first_gain_grad: float32 [1, 2048], P(None, 'row')
- first_shift_grad: float32 [1, 2048], P(None, 'row')
- project_in_grad: float32 [1, 2048, 3, 2048], P(None, 'row', None, 'col')
- project_bias_grad: float32 [1, 3, 2048], P(None, None, 'col')
- project_out_grad: float32 [1, 2048, 2048], P(None, 'col', 'row')
- second_gain_grad: float32 [1, 2048], P(None, 'row')
- second_shift_grad: float32 [1, 2048], P(None, 'row')
- gate_weight_grad: float32 [1, 2048, 2, 5632], P(None, 'row', None, 'col')
- down_weight_grad: float32 [1, 5632, 2048], P(None, 'col', 'row')
The draws below stay inside these ranges and needn't reach their ends.
All inputs are finite; a program needn't handle non-finite values.
Results may differ from the reference program's by a relative error of at most 0.015.
Values may be sent and summed in bfloat16 or wider, within the bound.
No kernel may reach another device: no remote copies, remote signals or barrier semaphores. Data moves between devices by JAX's collectives and lax.ppermute only.
A program may use at most 192 MiB of HBM per device.

```python
import math
import jax
import jax.numpy as jnp
from jax import lax

D = 2048
HEADS = 32
HEAD_DIM = 64
ROT = 16
FF = 5632
LENGTH = 1024
SEQS = 1
LAYERS = 1
TOKENS = 4096
N_DP = 4


def block_levels(rng, shape, shards, low, top_value):
    factor_of = 1.0
    for dim, shards_of in shards:
        heights = jax.random.uniform(jax.random.fold_in(jax.random.fold_in(rng, 6), dim), (shards_of,), jnp.float32, low / len(shards), top_value / len(shards))
        factor_of = factor_of * jnp.repeat(jnp.exp(heights), shape[dim] // shards_of).reshape((-1,) + (1,) * (len(shape) - 1 - dim))
    return factor_of


def noise(own_key, extent, width, limit, cuts=(), kind=jnp.bfloat16):
    entries = jax.random.normal(own_key, extent, jnp.float32) * width
    if len(cuts) > 0:
        entries = block_levels(own_key, extent, cuts, -0.22, 0.18) * entries
    return jnp.clip(entries, min=-limit, max=limit).astype(kind)


def setup_inputs(seed: int = 0) -> dict:
    arg_keys = jax.random.split(jax.random.key(seed), 12)
    inputs = noise(arg_keys[0], (TOKENS, D), 1.0, 6.0, ((0, 16), (1, 2)))
    first_gain = jnp.clip(1.0 + 0.15 * jax.random.normal(arg_keys[1], (LAYERS, D), jnp.float32), 0.25, 1.75)
    first_shift = noise(arg_keys[2], (LAYERS, D), 0.5, 3.0, ((1, 2),), jnp.float32)
    project_in = noise(arg_keys[3], (LAYERS, D, 3, D), D ** -0.5, 0.125, ((1, 2), (3, 4)))
    project_bias = noise(arg_keys[4], (LAYERS, 3, D), 0.5, 3.0, ((2, 4),), jnp.float32)
    project_out = noise(arg_keys[5], (LAYERS, D, D), (D // 32) ** -0.5, 0.75, ((1, 4), (2, 2)))
    second_gain = jnp.clip(1.0 + 0.15 * jax.random.normal(arg_keys[6], (LAYERS, D), jnp.float32), 0.25, 1.75)
    second_shift = noise(arg_keys[7], (LAYERS, D), 0.5, 3.0, ((1, 2),), jnp.float32)
    gate_weight = noise(arg_keys[8], (LAYERS, D, 2, FF), D ** -0.5, 0.125, ((1, 2), (3, 4)))
    down_weight = noise(arg_keys[9], (LAYERS, FF, D), FF ** -0.5, 0.078125, ((1, 4), (2, 2)))
    cotangent = noise(arg_keys[10], (TOKENS, D), 1.0, 6.0, ((0, 16), (1, 2)))
    return {"inputs": inputs, "first_gain": first_gain, "first_shift": first_shift, "project_in": project_in, "project_bias": project_bias, "project_out": project_out, "second_gain": second_gain, "second_shift": second_shift, "gate_weight": gate_weight, "down_weight": down_weight, "cotangent": cotangent}


EPSILON = 1e-05
HIGHEST = lax.Precision.HIGHEST

@jax.custom_vjp
def low(v):
    return lax.optimization_barrier(v.astype(jnp.bfloat16)).astype(jnp.float32)

@jax.custom_vjp
def low_back(v):
    return v

def low_keep(v):
    return (low(v), None)

def low_pass(kept, grad):
    return (grad,)

def back_keep(v):
    return (v, None)

def back_low(kept, grad):
    return (low(grad),)
low.defvjp(low_keep, low_pass)
low_back.defvjp(back_keep, back_low)

def layer_norm(stream, gain_row, shift_row):
    average = lax.optimization_barrier(jnp.mean(stream, axis=-1, keepdims=True))
    variance = lax.optimization_barrier(jnp.mean(jnp.square(stream - average), axis=-1, keepdims=True))
    return (stream - average) * lax.rsqrt(variance + EPSILON) * gain_row + shift_row

def rotary_tables(tokens):
    position = (jnp.arange(tokens) % LENGTH).astype(jnp.float32)
    frequency = 10000.0 ** (-(jnp.arange(ROT // 2).astype(jnp.float32) * 2.0 / ROT))
    angles = position[:, None] * frequency[None, :]
    return (jnp.cos(angles), jnp.sin(angles))

def rotate(tensor, cosine_table, sine_table):
    half_rot = ROT // 2
    front_half = tensor[..., :half_rot]
    back_half = tensor[..., half_rot:ROT]
    cosine = cosine_table[:, None, :]
    sine = sine_table[:, None, :]
    return jnp.concatenate([front_half * cosine - back_half * sine, back_half * cosine + front_half * sine, tensor[..., ROT:]], axis=-1)

def attend(triple):
    query_heads, key_heads, value_heads = triple
    factor = 1.0 / math.sqrt(HEAD_DIM)
    scores = low_back(jnp.einsum('qhd,khd->hqk', query_heads, key_heads, precision=HIGHEST) * factor)
    position = jnp.arange(LENGTH)
    causal = position[:, None] >= position[None, :]
    scores = jnp.where(causal[None], scores, -jnp.inf)
    highest = lax.optimization_barrier(jnp.max(scores, axis=-1, keepdims=True))
    exponent = jnp.exp(scores - highest)
    softmax_probs = exponent / lax.optimization_barrier(jnp.sum(exponent, axis=-1, keepdims=True))
    return jnp.einsum('hqk,khd->qhd', low(softmax_probs), value_heads, precision=HIGHEST)

def decoder_layer(stream, params, cosine_table, sine_table):
    first_gain, first_shift, project_in, project_bias, project_out, second_gain, second_shift, gate_weight, down_weight = params
    tokens = stream.shape[0]
    normed_a = low(layer_norm(stream, first_gain, first_shift))
    mixed = low_back(jnp.einsum('sd,dtk->stk', normed_a, project_in, precision=HIGHEST) + project_bias)
    mixed = mixed.reshape(tokens, 3, HEADS, HEAD_DIM)
    query_heads = low(rotate(mixed[:, 0], cosine_table, sine_table))
    key_heads = low(rotate(mixed[:, 1], cosine_table, sine_table))
    value_heads = low(mixed[:, 2])
    shape = (tokens // LENGTH, LENGTH, HEADS, HEAD_DIM)
    attended = lax.map(jax.checkpoint(attend), (query_heads.reshape(shape), key_heads.reshape(shape), value_heads.reshape(shape)))
    attended = low_back(low(attended.reshape(tokens, D)))
    residual = stream + low_back(jnp.dot(attended, project_out, precision=HIGHEST))
    normed_b = low(layer_norm(residual, second_gain, second_shift))
    gate_up = low_back(jnp.einsum('sd,dtf->stf', normed_b, gate_weight, precision=HIGHEST))
    hidden = low(jax.nn.silu(gate_up[:, 0]) * gate_up[:, 1])
    return low(residual + low_back(jnp.dot(hidden, down_weight, precision=HIGHEST)))

def replica_layers(group, params):
    cosine_table, sine_table = rotary_tables(group.shape[0])
    results = []
    stream = group
    for layer_index in range(LAYERS):
        stream = decoder_layer(stream, [tensor[layer_index] for tensor in params], cosine_table, sine_table)
        results.append(stream)
    return jnp.stack(results)

def reference(inputs, first_gain, first_shift, project_in, project_bias, project_out, second_gain, second_shift, gate_weight, down_weight, cotangent):
    floats = [tensor.astype(jnp.float32) for tensor in (inputs, first_gain, first_shift, project_in, project_bias, project_out, second_gain, second_shift, gate_weight, down_weight)]

    def forward(stream, *params):
        groups = stream.reshape(N_DP, SEQS * LENGTH, D)

        def run_group(group):
            return replica_layers(group, params)
        checked = jax.checkpoint(run_group)

        def step(carry, group):
            return (carry, checked(group))
        unused, stacked = lax.scan(step, jnp.zeros((), jnp.float32), groups)
        every_layer = jnp.transpose(stacked, (1, 0, 2, 3)).reshape(LAYERS, N_DP * SEQS * LENGTH, D)
        return (every_layer[LAYERS - 1], every_layer)
    final, pullback, every_layer = jax.vjp(forward, *floats, has_aux=True)
    grads = pullback(cotangent.astype(jnp.float32))
    return (every_layer.astype(jnp.bfloat16), grads[0], grads[1], grads[2], grads[3], grads[4], grads[5], grads[6], grads[7], grads[8], grads[9])
```

```python
import functools
import math

import jax
import jax.numpy as jnp
from jax import lax
from jax.experimental import pallas as pl
from jax.experimental.pallas import tpu as pltpu
from jax.sharding import Mesh
from jax.sharding import PartitionSpec as P

HEAD_DIM = 64
ROT = 16
LENGTH = 1024
EPSILON = 1e-05
F32 = jnp.float32
BF16 = jnp.bfloat16
LANES = 128
MIB = 1 << 20


def swap(x, axis):
    return lax.ppermute(x, axis, [(0, 1), (1, 0)])


PAIR = [(0, 1), (1, 0), (2, 3), (3, 2)]
MID = [(1, 2), (2, 1)]
OUT = [(1, 0), (2, 3)]
IN = [(0, 1), (3, 2)]
ORDER4 = ((0, 1, 2, 3), (1, 0, 2, 3), (2, 3, 1, 0), (3, 2, 1, 0))


def slot_order(place, count):
    if count == 4:
        return jnp.array(ORDER4, jnp.int32)[place]
    return jnp.arange(count, dtype=jnp.int32)


def gather_slots(own, count):
    if count != 4:
        return lax.all_gather(own, "col", axis=0, tiled=True)
    one = lax.ppermute(own, "col", PAIR)
    mid = lax.ppermute(own, "col", MID)
    far = lax.ppermute(one, "col", MID)
    two = mid + lax.ppermute(mid, "col", OUT)
    three = far + lax.ppermute(far, "col", OUT)
    return jnp.concatenate([own, one, two, three], axis=0)


def scatter_slots(parts, count):
    rows = parts.shape[0] // count
    if count != 4:
        mine = lax.psum_scatter(parts, "col", scatter_dimension=0, tiled=True)
        return (mine, jnp.zeros_like(mine), jnp.zeros_like(mine))
    part = [parts[i * rows : (i + 1) * rows] for i in range(4)]
    three = part[3] + lax.ppermute(part[3], "col", IN)
    two = part[2] + lax.ppermute(part[2], "col", IN)
    one = part[1] + lax.ppermute(three, "col", MID)
    from_mid = lax.ppermute(two, "col", MID)
    from_pair = lax.ppermute(one, "col", PAIR)
    return (part[0], from_mid, from_pair)


def params(mib, axes=1):
    return pltpu.CompilerParams(
        vmem_limit_bytes=mib * MIB, dimension_semantics=("arbitrary",) * axes
    )


def cost(flops, moved, trans=0):
    return pl.CostEstimate(flops=int(flops), bytes_accessed=int(moved), transcendentals=int(trans))


def stats_of(value):
    width = value.shape[1]
    average = jnp.sum(value, axis=1, keepdims=True) / width
    centred = value - average
    variance = jnp.sum(centred * centred, axis=1, keepdims=True) / width
    inv_root = lax.rsqrt(variance + EPSILON)
    return centred * inv_root, inv_root


def norm_first(stream, gain, shift):
    rows, width = stream.shape
    block = rows // 4

    def body(x_ref, gain_ref, shift_ref, low_ref):
        xhat, unused = stats_of(x_ref[...].astype(F32))
        low_ref[...] = (xhat * gain_ref[...] + shift_ref[...]).astype(BF16)

    row = pl.BlockSpec((block, width), lambda i: (i, 0))
    flat = pl.BlockSpec((1, width), lambda i: (0, 0))
    return pl.pallas_call(
        body,
        grid=(4,),
        in_specs=[row, flat, flat],
        out_specs=row,
        out_shape=jax.ShapeDtypeStruct((rows, width), BF16),
        compiler_params=params(16),
        cost_estimate=cost(rows * width * 10, rows * width * 4),
        name="norm_first",
    )(stream, gain, shift)


def norm_second(stream, terms, gain, shift):
    rows, width = stream.shape
    block = rows // 4

    def body(x_ref, a_ref, b_ref, c_ref, gain_ref, shift_ref, res_ref, low_ref):
        residual = (
            x_ref[...].astype(F32)
            + a_ref[...].astype(F32)
            + b_ref[...].astype(F32)
            + c_ref[...].astype(F32)
        )
        res_ref[...] = residual
        xhat, unused = stats_of(residual)
        low_ref[...] = (xhat * gain_ref[...] + shift_ref[...]).astype(BF16)

    row = pl.BlockSpec((block, width), lambda i: (i, 0))
    flat = pl.BlockSpec((1, width), lambda i: (0, 0))
    return pl.pallas_call(
        body,
        grid=(4,),
        in_specs=[row] * 4 + [flat, flat],
        out_specs=[row, row],
        out_shape=[
            jax.ShapeDtypeStruct((rows, width), F32),
            jax.ShapeDtypeStruct((rows, width), BF16),
        ],
        compiler_params=params(16),
        cost_estimate=cost(rows * width * 12, rows * width * 14),
        name="norm_second",
    )(stream, *terms, gain, shift)


def norm_back(stream, terms, upper, gain, both):
    rows, width = stream.shape
    block = rows // 4

    def body(x_ref, a_ref, b_ref, c_ref, up_ref, gain_ref, low_ref, sums_ref, *full_ref):
        xhat, inv_root = stats_of(x_ref[...].astype(F32))
        grad = a_ref[...].astype(F32) + b_ref[...].astype(F32) + c_ref[...].astype(F32)
        scaled = grad * gain_ref[...]
        mean_scaled = jnp.sum(scaled, axis=1, keepdims=True) / width
        mean_cross = jnp.sum(scaled * xhat, axis=1, keepdims=True) / width
        result = up_ref[...].astype(F32) + inv_root * (scaled - mean_scaled - xhat * mean_cross)
        low_ref[...] = result.astype(BF16)
        if full_ref:
            full_ref[0][...] = result

        @pl.when(pl.program_id(0) == 0)
        def _():
            sums_ref[...] = jnp.zeros_like(sums_ref)

        sums_ref[...] += jnp.concatenate(
            [
                jnp.sum(grad * xhat, axis=0, keepdims=True),
                jnp.sum(grad, axis=0, keepdims=True),
            ],
            axis=0,
        )

    row = pl.BlockSpec((block, width), lambda i: (i, 0))
    flat = pl.BlockSpec((1, width), lambda i: (0, 0))
    sums = pl.BlockSpec((2, width), lambda i: (0, 0))
    return pl.pallas_call(
        body,
        grid=(4,),
        in_specs=[row] * 5 + [flat],
        out_specs=[row, sums] + [row] * both,
        out_shape=[
            jax.ShapeDtypeStruct((rows, width), BF16),
            jax.ShapeDtypeStruct((2, width), F32),
        ]
        + [jax.ShapeDtypeStruct((rows, width), F32)] * both,
        compiler_params=params(24),
        cost_estimate=cost(rows * width * 20, rows * width * 18),
        name="norm_back",
    )(stream, *terms, upper, gain)


def roll_lanes(value, shift):
    return pltpu.roll(value, shift % value.shape[1], 1)


def turn(value, table, sign):
    times = value.shape[1] // LANES
    wide = [jnp.concatenate([table[i]] * times, axis=1) for i in range(3)]
    ahead = roll_lanes(value, -(ROT // 2))
    behind = roll_lanes(value, ROT // 2)
    moved = ahead * wide[1] + behind * wide[2]
    return value * wide[0] + (moved if sign > 0 else -moved)


def qkv_columns(tokens, weight, bias, table, half):
    rows, width = tokens.shape
    columns = weight.shape[2] // 2

    def body(half_ref, x_ref, w_ref, bias_ref, table_ref, out_ref):
        which = pl.program_id(0)
        acc = jnp.dot(x_ref[...], w_ref[0], preferred_element_type=F32) + bias_ref[0]

        @pl.when(which < 2)
        def _():
            out_ref[0] = turn(acc, table_ref, 1).astype(BF16)

        @pl.when(which == 2)
        def _():
            out_ref[0] = acc.astype(BF16)

    return pl.pallas_call(
        body,
        grid_spec=pltpu.PrefetchScalarGridSpec(
            num_scalar_prefetch=1,
            grid=(3,),
            in_specs=[
                pl.BlockSpec((rows, width), lambda j, h: (0, 0)),
                pl.BlockSpec((1, width, columns), lambda j, h: (j, 0, h[0])),
                pl.BlockSpec((1, 1, columns), lambda j, h: (j, 0, h[0])),
                pl.BlockSpec((3, rows, LANES), lambda j, h: (0, 0, 0)),
            ],
            out_specs=pl.BlockSpec((1, rows, columns), lambda j, h: (j, 0, 0)),
        ),
        out_shape=jax.ShapeDtypeStruct((3, rows, columns), BF16),
        compiler_params=params(40),
        cost_estimate=cost(6 * rows * width * columns, 2 * (rows * width + 3 * columns * width)),
        name="qkv_columns",
    )(half, tokens, weight, bias, table)


def place_of(order_ref, slot, core, rows):
    return pl.multiple_of((order_ref[1 + slot] * 2 + core) * rows, rows)


CHUNK = 256


def score_chunk(query, key, first, factor):
    scores = (
        lax.dot_general(query, key, (((1,), (1,)), ((), ())), preferred_element_type=F32) * factor
    )
    at_query = first + lax.broadcasted_iota(jnp.int32, scores.shape, 0)
    at_key = lax.broadcasted_iota(jnp.int32, scores.shape, 1)
    return jnp.where(at_query >= at_key, scores, -jnp.inf)


def attend(mine, other, order, factor):
    unused, rows, columns = mine.shape
    slots = order.shape[0] - 1
    piece = rows // slots
    length = 2 * rows

    def body(order_ref, mine_ref, other_ref, out_mine, out_other, lse_ref, whole, result):
        core = order_ref[0]
        for slot in range(slots):
            here = slice(slot * piece, (slot + 1) * piece)
            whole[:, pl.ds(place_of(order_ref, slot, core, piece), piece), :] = mine_ref[:, here, :]
            whole[:, pl.ds(place_of(order_ref, slot, 1 - core, piece), piece), :] = other_ref[
                :, here, :
            ]
        for head in range(LANES // HEAD_DIM):
            lanes = slice(head * HEAD_DIM, (head + 1) * HEAD_DIM)
            for first in range(0, length, CHUNK):
                upto = first + CHUNK
                scores = score_chunk(
                    whole[0, first:upto, lanes], whole[1, :upto, lanes], first, factor
                )
                highest = jnp.max(scores, axis=1, keepdims=True)
                exponent = jnp.exp(scores - highest)
                summed = jnp.sum(exponent, axis=1, keepdims=True)
                probs = (exponent * (1.0 / summed)).astype(BF16)
                result[first:upto, lanes] = jnp.dot(
                    probs, whole[2, :upto, lanes], preferred_element_type=F32
                ).astype(BF16)
                lse_ref[0, first:upto, head : head + 1] = highest + jnp.log(summed)
        for slot in range(slots):
            here = slice(slot * piece, (slot + 1) * piece)
            out_mine[here, :] = result[pl.ds(place_of(order_ref, slot, core, piece), piece), :]
            out_other[here, :] = result[pl.ds(place_of(order_ref, slot, 1 - core, piece), piece), :]

    groups = columns // LANES
    three = pl.BlockSpec((3, rows, LANES), lambda g, o: (0, 0, g))
    one = pl.BlockSpec((rows, LANES), lambda g, o: (0, g))
    return pl.pallas_call(
        body,
        grid_spec=pltpu.PrefetchScalarGridSpec(
            num_scalar_prefetch=1,
            grid=(groups,),
            in_specs=[three, three],
            out_specs=[one, one, pl.BlockSpec((1, length, 2), lambda g, o: (g, 0, 0))],
            scratch_shapes=[
                pltpu.VMEM((3, length, LANES), BF16),
                pltpu.VMEM((length, LANES), BF16),
            ],
        ),
        out_shape=[
            jax.ShapeDtypeStruct((rows, columns), BF16),
            jax.ShapeDtypeStruct((rows, columns), BF16),
            jax.ShapeDtypeStruct((groups, length, 2), F32),
        ],
        compiler_params=params(48),
        cost_estimate=cost(
            4 * length * length * columns, 16 * rows * columns, columns * length * length / 128
        ),
        name="attend",
    )(order, mine, other)


def attend_back(mine, other, grad_mine, grad_other, lse, table_mine, table_other, order, factor):
    unused, rows, columns = mine.shape
    slots = order.shape[0] - 1
    piece = rows // slots
    length = 2 * rows
    across = (((1,), (1,)), ((), ()))
    down = (((0,), (0,)), ((), ()))

    def body(
        order_ref,
        mine_ref,
        other_ref,
        gm_ref,
        go_ref,
        lse_ref,
        tm_ref,
        to_ref,
        out_mine,
        out_other,
        bias_ref,
        whole,
        grads,
        dq_ref,
        dkv_ref,
    ):
        core = order_ref[0]
        for slot in range(slots):
            here = slice(slot * piece, (slot + 1) * piece)
            one = pl.ds(place_of(order_ref, slot, core, piece), piece)
            two = pl.ds(place_of(order_ref, slot, 1 - core, piece), piece)
            whole[:, one, :] = mine_ref[:, here, :]
            whole[:, two, :] = other_ref[:, here, :]
            grads[one, :] = gm_ref[here, :]
            grads[two, :] = go_ref[here, :]
        heads = LANES // HEAD_DIM
        for head in range(heads):
            lanes = slice(head * HEAD_DIM, (head + 1) * HEAD_DIM)
            for first in reversed(range(0, length, CHUNK)):
                upto = first + CHUNK
                query = whole[0, first:upto, lanes]
                key = whole[1, :upto, lanes]
                value = whole[2, :upto, lanes]
                grad = grads[first:upto, lanes]
                scores = score_chunk(query, key, first, factor)
                probs = jnp.exp(scores - lse_ref[0, first:upto, head : head + 1])
                probs_grad = lax.dot_general(grad, value, across, preferred_element_type=F32)
                shift = jnp.sum(probs * probs_grad, axis=1, keepdims=True)
                scores_grad = (probs * (probs_grad - shift)).astype(BF16)
                dq_ref[first:upto, lanes] = (
                    jnp.dot(scores_grad, key, preferred_element_type=F32) * factor
                )
                dk = lax.dot_general(scores_grad, query, down, preferred_element_type=F32) * factor
                dv = lax.dot_general(
                    probs.astype(BF16), grad, down, preferred_element_type=F32
                )
                if upto == length:
                    dkv_ref[0, :, lanes] = dk
                    dkv_ref[1, :, lanes] = dv
                else:
                    dkv_ref[0, :upto, lanes] += dk
                    dkv_ref[1, :upto, lanes] += dv
        total = [jnp.zeros((1, LANES), F32) for _ in range(3)]
        for slot in range(slots):
            here = slice(slot * piece, (slot + 1) * piece)
            for at, table, out in (
                (core, tm_ref, out_mine),
                (1 - core, to_ref, out_other),
            ):
                rows_at = pl.ds(place_of(order_ref, slot, at, piece), piece)
                angles = table[:, here, :]
                parts = (
                    turn(dq_ref[rows_at, :], angles, -1).astype(BF16),
                    turn(dkv_ref[0, rows_at, :], angles, -1).astype(BF16),
                    dkv_ref[1, rows_at, :].astype(BF16),
                )
                for i in range(3):
                    out[i, here, :] = parts[i]
                    total[i] += jnp.sum(parts[i].astype(F32), axis=0, keepdims=True)
        for i in range(3):
            bias_ref[i] = total[i]

    groups = columns // LANES
    three = pl.BlockSpec((3, rows, LANES), lambda g, o: (0, 0, g))
    one = pl.BlockSpec((rows, LANES), lambda g, o: (0, g))
    full = pl.BlockSpec((3, rows, LANES), lambda g, o: (0, 0, 0))
    return pl.pallas_call(
        body,
        grid_spec=pltpu.PrefetchScalarGridSpec(
            num_scalar_prefetch=1,
            grid=(groups,),
            in_specs=[
                three,
                three,
                one,
                one,
                pl.BlockSpec((1, length, 2), lambda g, o: (g, 0, 0)),
                full,
                full,
            ],
            out_specs=[three, three, pl.BlockSpec((3, 1, LANES), lambda g, o: (0, 0, g))],
            scratch_shapes=[
                pltpu.VMEM((3, length, LANES), BF16),
                pltpu.VMEM((length, LANES), BF16),
                pltpu.VMEM((length, LANES), F32),
                pltpu.VMEM((2, length, LANES), F32),
            ],
        ),
        out_shape=[
            jax.ShapeDtypeStruct((3, rows, columns), BF16),
            jax.ShapeDtypeStruct((3, rows, columns), BF16),
            jax.ShapeDtypeStruct((3, 1, columns), F32),
        ],
        compiler_params=params(52),
        cost_estimate=cost(
            10 * length * length * columns, 40 * rows * columns, columns * length * length / 128
        ),
        name="attend_back",
    )(order, mine, other, grad_mine, grad_other, lse, table_mine, table_other)


def mlp(tokens, weight, hidden_grad):
    rows, width = tokens.shape
    units = weight.shape[2]
    block = LANES if units % LANES == 0 else units
    steps = units // block
    across = (((1,), (1,)), ((), ()))

    def body(x_ref, w_ref, hg_ref, hidden_ref, grad_ref, out_ref, acc):
        both = jnp.concatenate([w_ref[0], w_ref[1]], axis=1)
        gate_up = jnp.dot(x_ref[...], both, preferred_element_type=F32)
        gate, up = gate_up[:, :block], gate_up[:, block:]
        sigma = jax.nn.sigmoid(gate)
        silu = gate * sigma
        hidden_ref[...] = (silu * up).astype(BF16)
        grad = hg_ref[...].astype(F32)
        gate_grad = (grad * up * sigma * (1.0 + gate * (1.0 - sigma))).astype(BF16)
        up_grad = (grad * silu).astype(BF16)
        grad_ref[0] = gate_grad
        grad_ref[1] = up_grad
        part = lax.dot_general(
            jnp.concatenate([gate_grad, up_grad], axis=1), both, across, preferred_element_type=F32
        )
        step = pl.program_id(0)

        @pl.when(step == 0)
        def _():
            acc[...] = part

        @pl.when(step > 0)
        def _():
            acc[...] += part

        @pl.when(step == steps - 1)
        def _():
            out_ref[...] = acc[...].astype(BF16)

    return pl.pallas_call(
        body,
        grid=(steps,),
        in_specs=[
            pl.BlockSpec((rows, width), lambda j: (0, 0)),
            pl.BlockSpec((2, width, block), lambda j: (0, 0, j)),
            pl.BlockSpec((rows, block), lambda j: (0, j)),
        ],
        out_specs=[
            pl.BlockSpec((rows, block), lambda j: (0, j)),
            pl.BlockSpec((2, rows, block), lambda j: (0, 0, j)),
            pl.BlockSpec((rows, width), lambda j: (0, 0)),
        ],
        out_shape=[
            jax.ShapeDtypeStruct((rows, units), BF16),
            jax.ShapeDtypeStruct((2, rows, units), BF16),
            jax.ShapeDtypeStruct((rows, width), BF16),
        ],
        scratch_shapes=[pltpu.VMEM((rows, width), F32)],
        compiler_params=params(52),
        cost_estimate=cost(
            8 * rows * width * units, 4 * width * units + 4 * rows * width, rows * units
        ),
        name="mlp",
    )(tokens, weight, hidden_grad)


def rotary_table(position):
    half = ROT // 2
    frequency = 10000.0 ** (-(jnp.arange(half).astype(F32) * 2.0 / ROT))
    angles = position.astype(F32)[:, None] * frequency[None, :]
    cosine, sine = jnp.cos(angles), jnp.sin(angles)
    rest = HEAD_DIM - ROT
    count = position.shape[0]
    zero = jnp.zeros((count, half), F32)
    tail = jnp.zeros((count, rest), F32)
    keep = jnp.concatenate([cosine, cosine, tail + 1.0], axis=1)
    front = jnp.concatenate([-sine, zero, tail], axis=1)
    back = jnp.concatenate([zero, sine, tail], axis=1)
    return jnp.stack([jnp.concatenate([t, t], axis=1) for t in (keep, front, back)])


def local(
    inputs,
    first_gain,
    first_shift,
    project_in,
    project_bias,
    project_out,
    second_gain,
    second_shift,
    gate_weight,
    down_weight,
    cotangent,
):
    y_count = lax.axis_size("y")
    slots = lax.axis_size("col")
    y = lax.axis_index("y")
    core = lax.axis_index("core")
    row = lax.axis_index("row")
    place = lax.axis_index("col")
    factor = 1.0 / math.sqrt(HEAD_DIM)
    half_rows = inputs.shape[0] // 2
    wide = inputs.shape[1]
    width = 2 * wide

    def take(x, start, size, axis):
        return lax.dynamic_slice_in_dim(x, start, size, axis)

    straight = [(0, 0), (1, 2), (2, 1), (3, 3)]
    crossed = [(0, 2), (1, 0), (2, 3), (3, 1)]
    aligned = core == row

    def to_sequence(x):
        a = lax.ppermute(take(x, row * half_rows, half_rows, 0), ("core", "row"), straight)
        b = lax.ppermute(take(x, (1 - row) * half_rows, half_rows, 0), ("core", "row"), crossed)
        return jnp.concatenate([jnp.where(aligned, a, b), jnp.where(aligned, b, a)], axis=1)

    def from_sequence(x):
        own, oth = x[:, :wide], x[:, wide:]
        a = jnp.where(aligned, own, oth)
        b = jnp.where(aligned, oth, own)
        a = lax.ppermute(a, ("core", "row"), [(j, i) for i, j in straight])
        b = lax.ppermute(b, ("core", "row"), [(j, i) for i, j in crossed])
        top = jnp.where(row == 0, a, b)
        bottom = jnp.where(row == 0, b, a)
        return jnp.concatenate([top, bottom], axis=0)

    stream = to_sequence(inputs)

    vectors = jnp.concatenate([first_gain, first_shift, second_gain, second_shift], axis=0)
    vectors = jnp.concatenate([vectors, swap(vectors, "row")], axis=1)
    gain_a, shift_a, gain_b, shift_b = (vectors[i : i + 1] for i in range(4))

    def fetch(w, axis):
        size = w.shape[axis]
        pieces = []
        if y_count == 2:
            part = size // 4
            at = lambda c, yy: c * (size // 2) + yy * part
            first = swap(take(w, at(core, y), part, axis), "row")
            second = swap(first, "y")
            pieces = [
                (first, at(core, y)),
                (second, at(core, 1 - y)),
                (swap(first, "core"), at(1 - core, y)),
                (swap(second, "core"), at(1 - core, 1 - y)),
            ]
        else:
            part = size // 2
            first = swap(take(w, core * part, part, axis), "row")
            pieces = [(first, core * part), (swap(first, "core"), (1 - core) * part)]
        return pieces

    def assemble(w, pieces, cut, join):
        pads = [(0, w.shape[i] if i == join else 0, 0) for i in range(w.ndim)]
        full = lax.pad(w, jnp.zeros((), w.dtype), pads)
        for piece, start in pieces:
            at = [jnp.int32(0)] * w.ndim
            at[join] = jnp.int32(w.shape[join])
            at[cut] = at[cut] + start
            full = lax.dynamic_update_slice(full, piece, at)
        return full

    w_in = jnp.transpose(project_in[0], (1, 0, 2))
    w_in_full = assemble(w_in, fetch(w_in, 1), 1, 1)
    w_out = project_out[0]
    w_out_full = assemble(w_out, fetch(w_out, 0), 0, 1)
    w_down = down_weight[0]
    w_down_full = assemble(w_down, fetch(w_down, 0), 0, 1)
    w_gate = jnp.transpose(gate_weight[0], (1, 0, 2))
    w_gate_full = assemble(w_gate, fetch(w_gate, 1), 1, 1)

    order = slot_order(place, slots)
    table_of = jnp.concatenate([core[None], order]).astype(jnp.int32)
    inside = jnp.arange(half_rows)
    position = lambda c: ((order[:, None] * 2 + c) * half_rows + inside[None, :]).reshape(-1)
    rotary_mine = rotary_table(position(core))
    rotary_other = rotary_table(position(1 - core))

    tokens_a = gather_slots(norm_first(stream, gain_a, shift_a), slots)
    bias = project_bias[0][:, None, :]
    qkv_other = qkv_columns(tokens_a, w_in_full, bias, rotary_mine, (1 - core)[None])
    qkv_from = swap(qkv_other, "core")
    qkv_mine = qkv_columns(tokens_a, w_in_full, bias, rotary_mine, core[None])
    out_mine, out_other, lse = attend(qkv_mine, qkv_from, table_of, factor)
    out_from = swap(out_other, "core")
    attended = jnp.concatenate(
        [jnp.where(core == 0, out_mine, out_from), jnp.where(core == 0, out_from, out_mine)], axis=1
    )
    part_out = jnp.dot(attended, w_out_full, preferred_element_type=F32).astype(BF16)
    terms = scatter_slots(part_out, slots)
    residual, low_b = norm_second(stream, terms, gain_b, shift_b)

    cot = to_sequence(cotangent)
    grad_rows = gather_slots(cot, slots)
    hidden_grad = lax.dot_general(
        grad_rows, w_down_full, (((1,), (1,)), ((), ())), preferred_element_type=F32
    ).astype(BF16)

    tokens_b = gather_slots(low_b, slots)
    hidden, gate_up_grad, part_b = mlp(tokens_b, w_gate_full, hidden_grad)
    terms = scatter_slots(part_b, slots)
    g2_low, sums_b, g2 = norm_back(residual, terms, cot, gain_b, 1)

    part_down = jnp.dot(hidden, w_down_full, preferred_element_type=F32).astype(BF16)
    terms = scatter_slots(part_down, slots)
    layer_low = (residual + sum(t.astype(F32) for t in terms)).astype(BF16)
    layer_out = from_sequence(layer_low)

    g2_rows = gather_slots(g2_low, slots)
    attended_grad = lax.dot_general(
        g2_rows, w_out_full, (((1,), (1,)), ((), ())), preferred_element_type=F32
    ).astype(BF16)
    columns = attended_grad.shape[1] // 2
    grad_mine = take(attended_grad, core * columns, columns, 1)
    grad_from = swap(take(attended_grad, (1 - core) * columns, columns, 1), "core")
    mixed_mine, mixed_other, bias_part = attend_back(
        qkv_mine, qkv_from, grad_mine, grad_from, lse, rotary_mine, rotary_other, table_of, factor
    )
    mixed_from = swap(mixed_other, "core")
    mixed = jnp.concatenate(
        [
            jnp.where(core == 0, mixed_mine, mixed_from),
            jnp.where(core == 0, mixed_from, mixed_mine),
        ],
        axis=2,
    )
    part_a = lax.dot_general(
        mixed[0], w_in_full[0], (((1,), (1,)), ((), ())), preferred_element_type=F32
    )
    for i in (1, 2):
        part_a += lax.dot_general(
            mixed[i], w_in_full[i], (((1,), (1,)), ((), ())), preferred_element_type=F32
        )
    terms = scatter_slots(part_a.astype(BF16), slots)
    input_low, sums_a = norm_back(stream, terms, g2, gain_a, 0)
    input_grad = from_sequence(input_low).astype(F32)

    def sum_y(x):
        if y_count == 2:
            return (x.astype(F32) + swap(x, "y").astype(F32)).astype(x.dtype)
        return lax.psum(x, "y")

    def reduce_weight(grad, cut, join):
        size = grad.shape[cut] if cut != join else grad.shape[cut] // 2
        part = size // 2
        if cut == join:
            shape = list(grad.shape)
            shape[cut : cut + 1] = [2, size]
            grad = grad.reshape(shape)
            cut_at, join_at = cut + 1, join
        else:
            shape = list(grad.shape)
            shape[join : join + 1] = [2, grad.shape[join] // 2]
            cut_at, join_at = cut, join
            halves = jnp.split(grad, 2, axis=join)
            grad = None
        if grad is not None:
            pieces = [lax.index_in_dim(grad, i, join_at, keepdims=False) for i in range(2)]
        else:
            pieces = halves
        sent = [swap(take(p, (1 - core) * part, part, cut), "core") for p in pieces]
        kept = [
            (take(p, core * part, part, cut).astype(F32) + s.astype(F32))
            for p, s in zip(pieces, sent)
        ]
        arrived = swap(kept[1].astype(BF16), "row")
        total = sum_y((kept[0] + arrived.astype(F32)).astype(BF16))
        rest = swap(total, "core")
        first = jnp.where(core == 0, total, rest)
        second = jnp.where(core == 0, rest, total)
        return jnp.concatenate([first, second], axis=cut).astype(F32)

    down = (((0,), (0,)), ((), ()))
    down_grad = lax.dot_general(hidden, grad_rows, down, preferred_element_type=F32).astype(BF16)
    down_grad = reduce_weight(down_grad, 0, 1)
    gate_grad = jnp.stack(
        [
            lax.dot_general(tokens_b, gate_up_grad[i], down, preferred_element_type=F32).astype(BF16)
            for i in range(2)
        ]
    )
    gate_grad = reduce_weight(gate_grad, 1, 1)
    out_grad = lax.dot_general(attended, g2_rows, down, preferred_element_type=F32).astype(BF16)
    out_grad = reduce_weight(out_grad, 0, 1)
    in_grad = jnp.stack(
        [
            lax.dot_general(tokens_a, mixed[i], down, preferred_element_type=F32).astype(BF16)
            for i in range(3)
        ]
    )
    in_grad = reduce_weight(in_grad, 1, 1)

    bias_sum = bias_part[:, 0, :]
    bias_sum = bias_sum + swap(bias_sum, "row")
    bias_sum = lax.psum(bias_sum, "y") if y_count != 2 else bias_sum + swap(bias_sum, "y")
    bias_other = swap(bias_sum, "core")
    bias_grad = jnp.concatenate(
        [jnp.where(core == 0, bias_sum, bias_other), jnp.where(core == 0, bias_other, bias_sum)],
        axis=1,
    )

    def reduce_vector(sums):
        total = sums[:, :wide] + swap(sums[:, wide:], "row")
        total = total + swap(total, "core")
        total = lax.psum(total, "y") if y_count != 2 else total + swap(total, "y")
        if slots != 4:
            return lax.psum(total, "col")
        pair = total + lax.ppermute(total, "col", PAIR)
        inner = pair + lax.ppermute(pair, "col", MID)
        outer = lax.ppermute(inner, "col", OUT)
        return jnp.where((place == 0) | (place == 3), outer, inner)

    vec_b = reduce_vector(sums_b)
    vec_a = reduce_vector(sums_a)
    return (
        layer_out[None],
        input_grad,
        vec_a[0:1],
        vec_a[1:2],
        jnp.transpose(in_grad, (1, 0, 2))[None],
        bias_grad[None],
        out_grad[None],
        vec_b[0:1],
        vec_b[1:2],
        jnp.transpose(gate_grad, (1, 0, 2))[None],
        down_grad[None],
    )


def solution(mesh):
    dp, rows, cols = (mesh.shape[a] for a in ("dp", "row", "col"))
    split = Mesh(mesh.devices.reshape(dp // 2, 2, rows, cols), ("y", "core", "row", "col"))
    tokens = ("y", "core", "col")
    return jax.shard_map(
        local,
        mesh=split,
        in_specs=(
            P(tokens, "row"),
            P(None, "row"),
            P(None, "row"),
            P(None, "row", None, "col"),
            P(None, None, "col"),
            P(None, "col", "row"),
            P(None, "row"),
            P(None, "row"),
            P(None, "row", None, "col"),
            P(None, "col", "row"),
            P(tokens, "row"),
        ),
        out_specs=(
            P(None, tokens, "row"),
            P(tokens, "row"),
            P(None, "row"),
            P(None, "row"),
            P(None, "row", None, "col"),
            P(None, None, "col"),
            P(None, "col", "row"),
            P(None, "row"),
            P(None, "row"),
            P(None, "row", None, "col"),
            P(None, "col", "row"),
        ),
        check_vma=False,
    )
```

```python
import functools
import math

import jax
import jax.numpy as jnp
from jax import lax
from jax.experimental import pallas as pl
from jax.experimental.pallas import tpu as pltpu
from jax.sharding import Mesh
from jax.sharding import PartitionSpec as P

HEAD_DIM = 64
ROT = 16
LENGTH = 1024
EPSILON = 1e-05
F32 = jnp.float32
BF16 = jnp.bfloat16
LANES = 128
MIB = 1 << 20


def swap(x, axis):
    return lax.ppermute(x, axis, [(0, 1), (1, 0)])


PAIR = [(0, 1), (1, 0), (2, 3), (3, 2)]
MID = [(1, 2), (2, 1)]
OUT = [(1, 0), (2, 3)]
IN = [(0, 1), (3, 2)]
ORDER4 = ((0, 1, 2, 3), (1, 0, 2, 3), (2, 3, 1, 0), (3, 2, 1, 0))


def slot_order(place, count):
    if count == 4:
        return jnp.array(ORDER4, jnp.int32)[place]
    return jnp.arange(count, dtype=jnp.int32)


def gather_slots(own, count):
    if count != 4:
        return lax.all_gather(own, "col", axis=0, tiled=True)
    one = lax.ppermute(own, "col", PAIR)
    mid = lax.ppermute(own, "col", MID)
    far = lax.ppermute(one, "col", MID)
    two = mid + lax.ppermute(mid, "col", OUT)
    three = far + lax.ppermute(far, "col", OUT)
    return jnp.concatenate([own, one, two, three], axis=0)


def scatter_slots(parts, count):
    rows = parts.shape[0] // count
    if count != 4:
        mine = lax.psum_scatter(parts, "col", scatter_dimension=0, tiled=True)
        return (mine, jnp.zeros_like(mine), jnp.zeros_like(mine))
    part = [parts[i * rows : (i + 1) * rows] for i in range(4)]
    three = part[3] + lax.ppermute(part[3], "col", IN)
    two = part[2] + lax.ppermute(part[2], "col", IN)
    one = part[1] + lax.ppermute(three, "col", MID)
    from_mid = lax.ppermute(two, "col", MID)
    from_pair = lax.ppermute(one, "col", PAIR)
    return (part[0], from_mid, from_pair)


def params(mib, axes=1):
    return pltpu.CompilerParams(
        vmem_limit_bytes=mib * MIB, dimension_semantics=("arbitrary",) * axes
    )


def cost(flops, moved, trans=0):
    return pl.CostEstimate(flops=int(flops), bytes_accessed=int(moved), transcendentals=int(trans))


def stats_of(value):
    width = value.shape[1]
    average = jnp.sum(value, axis=1, keepdims=True) / width
    centred = value - average
    variance = jnp.sum(centred * centred, axis=1, keepdims=True) / width
    inv_root = lax.rsqrt(variance + EPSILON)
    return centred * inv_root, inv_root


def norm_first(stream, gain, shift):
    rows, width = stream.shape
    block = rows // 4

    def body(x_ref, gain_ref, shift_ref, low_ref):
        xhat, unused = stats_of(x_ref[...].astype(F32))
        low_ref[...] = (xhat * gain_ref[...] + shift_ref[...]).astype(BF16)

    row = pl.BlockSpec((block, width), lambda i: (i, 0))
    flat = pl.BlockSpec((1, width), lambda i: (0, 0))
    return pl.pallas_call(
        body,
        grid=(4,),
        in_specs=[row, flat, flat],
        out_specs=row,
        out_shape=jax.ShapeDtypeStruct((rows, width), BF16),
        compiler_params=params(16),
        cost_estimate=cost(rows * width * 10, rows * width * 4),
        name="norm_first",
    )(stream, gain, shift)


def norm_second(stream, terms, gain, shift):
    rows, width = stream.shape
    block = rows // 4

    def body(x_ref, a_ref, b_ref, c_ref, gain_ref, shift_ref, res_ref, low_ref):
        residual = (
            x_ref[...].astype(F32)
            + a_ref[...].astype(F32)
            + b_ref[...].astype(F32)
            + c_ref[...].astype(F32)
        )
        res_ref[...] = residual
        xhat, unused = stats_of(residual)
        low_ref[...] = (xhat * gain_ref[...] + shift_ref[...]).astype(BF16)

    row = pl.BlockSpec((block, width), lambda i: (i, 0))
    flat = pl.BlockSpec((1, width), lambda i: (0, 0))
    return pl.pallas_call(
        body,
        grid=(4,),
        in_specs=[row] * 4 + [flat, flat],
        out_specs=[row, row],
        out_shape=[
            jax.ShapeDtypeStruct((rows, width), F32),
            jax.ShapeDtypeStruct((rows, width), BF16),
        ],
        compiler_params=params(16),
        cost_estimate=cost(rows * width * 12, rows * width * 14),
        name="norm_second",
    )(stream, *terms, gain, shift)


def norm_back(stream, terms, upper, gain, both):
    rows, width = stream.shape
    block = rows // 4

    def body(x_ref, a_ref, b_ref, c_ref, up_ref, gain_ref, low_ref, sums_ref, *full_ref):
        xhat, inv_root = stats_of(x_ref[...].astype(F32))
        grad = a_ref[...].astype(F32) + b_ref[...].astype(F32) + c_ref[...].astype(F32)
        scaled = grad * gain_ref[...]
        mean_scaled = jnp.sum(scaled, axis=1, keepdims=True) / width
        mean_cross = jnp.sum(scaled * xhat, axis=1, keepdims=True) / width
        result = up_ref[...].astype(F32) + inv_root * (scaled - mean_scaled - xhat * mean_cross)
        low_ref[...] = result.astype(BF16)
        if full_ref:
            full_ref[0][...] = result

        @pl.when(pl.program_id(0) == 0)
        def _():
            sums_ref[...] = jnp.zeros_like(sums_ref)

        sums_ref[...] += jnp.concatenate(
            [
                jnp.sum(grad * xhat, axis=0, keepdims=True),
                jnp.sum(grad, axis=0, keepdims=True),
            ],
            axis=0,
        )

    row = pl.BlockSpec((block, width), lambda i: (i, 0))
    flat = pl.BlockSpec((1, width), lambda i: (0, 0))
    sums = pl.BlockSpec((2, width), lambda i: (0, 0))
    return pl.pallas_call(
        body,
        grid=(4,),
        in_specs=[row] * 5 + [flat],
        out_specs=[row, sums] + [row] * both,
        out_shape=[
            jax.ShapeDtypeStruct((rows, width), BF16),
            jax.ShapeDtypeStruct((2, width), F32),
        ]
        + [jax.ShapeDtypeStruct((rows, width), F32)] * both,
        compiler_params=params(24),
        cost_estimate=cost(rows * width * 20, rows * width * 18),
        name="norm_back",
    )(stream, *terms, upper, gain)


def cuts_of(sizes):
    ends = [sum(sizes[: i + 1]) for i in range(len(sizes))]
    return [(end - size, end) for end, size in zip(ends, sizes)]


def roll_lanes(value, shift):
    return pltpu.roll(value, shift % value.shape[1], 1)


def turn(value, table, sign):
    times = value.shape[1] // LANES
    wide = [jnp.concatenate([table[i]] * times, axis=1) for i in range(3)]
    ahead = roll_lanes(value, -(ROT // 2))
    behind = roll_lanes(value, ROT // 2)
    moved = ahead * wide[1] + behind * wide[2]
    return value * wide[0] + (moved if sign > 0 else -moved)


def qkv_columns(tokens, pieces, bias, table, half):
    rows, width = tokens.shape
    columns = pieces[0].shape[2] // 2
    cuts = cuts_of([p.shape[1] for p in pieces])

    def body(half_ref, x_ref, *refs):
        bias_ref, table_ref, out_ref = refs[-3:]
        which = pl.program_id(0)
        acc = bias_ref[0]
        for w_ref, (low, high) in zip(refs, cuts):
            acc = acc + jnp.dot(x_ref[:, low:high], w_ref[0], preferred_element_type=F32)

        @pl.when(which < 2)
        def _():
            out_ref[0] = turn(acc, table_ref, 1).astype(BF16)

        @pl.when(which == 2)
        def _():
            out_ref[0] = acc.astype(BF16)

    return pl.pallas_call(
        body,
        grid_spec=pltpu.PrefetchScalarGridSpec(
            num_scalar_prefetch=1,
            grid=(3,),
            in_specs=[pl.BlockSpec((rows, width), lambda j, h: (0, 0))]
            + [pl.BlockSpec((1, p.shape[1], columns), lambda j, h: (j, 0, h[0])) for p in pieces]
            + [
                pl.BlockSpec((1, 1, columns), lambda j, h: (j, 0, h[0])),
                pl.BlockSpec((3, rows, LANES), lambda j, h: (0, 0, 0)),
            ],
            out_specs=pl.BlockSpec((1, rows, columns), lambda j, h: (j, 0, 0)),
        ),
        out_shape=jax.ShapeDtypeStruct((3, rows, columns), BF16),
        compiler_params=params(40),
        cost_estimate=cost(6 * rows * width * columns, 2 * (rows * width + 3 * columns * width)),
        name="qkv_columns",
    )(half, tokens, *pieces, bias, table)


def place_of(order_ref, slot, core, rows):
    return pl.multiple_of((order_ref[1 + slot] * 2 + core) * rows, rows)


CHUNK = 256


def score_chunk(query, key, first, factor):
    scores = (
        lax.dot_general(query, key, (((1,), (1,)), ((), ())), preferred_element_type=F32) * factor
    )
    at_query = first + lax.broadcasted_iota(jnp.int32, scores.shape, 0)
    at_key = lax.broadcasted_iota(jnp.int32, scores.shape, 1)
    return jnp.where(at_query >= at_key, scores, -jnp.inf)


def attend(mine, other, order, factor):
    unused, rows, columns = mine.shape
    slots = order.shape[0] - 1
    piece = rows // slots
    length = 2 * rows

    def body(order_ref, mine_ref, other_ref, out_mine, out_other, lse_ref, whole, result):
        core = order_ref[0]
        for slot in range(slots):
            here = slice(slot * piece, (slot + 1) * piece)
            whole[:, pl.ds(place_of(order_ref, slot, core, piece), piece), :] = mine_ref[:, here, :]
            whole[:, pl.ds(place_of(order_ref, slot, 1 - core, piece), piece), :] = other_ref[
                :, here, :
            ]
        for head in range(LANES // HEAD_DIM):
            lanes = slice(head * HEAD_DIM, (head + 1) * HEAD_DIM)
            for first in range(0, length, CHUNK):
                upto = first + CHUNK
                scores = score_chunk(
                    whole[0, first:upto, lanes], whole[1, :upto, lanes], first, factor
                )
                highest = jnp.max(scores, axis=1, keepdims=True)
                exponent = jnp.exp(scores - highest)
                summed = jnp.sum(exponent, axis=1, keepdims=True)
                probs = (exponent * (1.0 / summed)).astype(BF16)
                result[first:upto, lanes] = jnp.dot(
                    probs, whole[2, :upto, lanes], preferred_element_type=F32
                ).astype(BF16)
                lse_ref[0, first:upto, head : head + 1] = highest + jnp.log(summed)
        for slot in range(slots):
            here = slice(slot * piece, (slot + 1) * piece)
            out_mine[here, :] = result[pl.ds(place_of(order_ref, slot, core, piece), piece), :]
            out_other[here, :] = result[pl.ds(place_of(order_ref, slot, 1 - core, piece), piece), :]

    groups = columns // LANES
    three = pl.BlockSpec((3, rows, LANES), lambda g, o: (0, 0, g))
    one = pl.BlockSpec((rows, LANES), lambda g, o: (0, g))
    return pl.pallas_call(
        body,
        grid_spec=pltpu.PrefetchScalarGridSpec(
            num_scalar_prefetch=1,
            grid=(groups,),
            in_specs=[three, three],
            out_specs=[one, one, pl.BlockSpec((1, length, 2), lambda g, o: (g, 0, 0))],
            scratch_shapes=[
                pltpu.VMEM((3, length, LANES), BF16),
                pltpu.VMEM((length, LANES), BF16),
            ],
        ),
        out_shape=[
            jax.ShapeDtypeStruct((rows, columns), BF16),
            jax.ShapeDtypeStruct((rows, columns), BF16),
            jax.ShapeDtypeStruct((groups, length, 2), F32),
        ],
        compiler_params=params(48),
        cost_estimate=cost(
            4 * length * length * columns, 16 * rows * columns, columns * length * length / 128
        ),
        name="attend",
    )(order, mine, other)


def attend_back(mine, other, grad_mine, grad_other, lse, table_mine, table_other, order, factor):
    unused, rows, columns = mine.shape
    slots = order.shape[0] - 1
    piece = rows // slots
    length = 2 * rows
    across = (((1,), (1,)), ((), ()))
    down = (((0,), (0,)), ((), ()))

    def body(
        order_ref,
        mine_ref,
        other_ref,
        gm_ref,
        go_ref,
        lse_ref,
        tm_ref,
        to_ref,
        out_mine,
        out_other,
        bias_ref,
        whole,
        grads,
        dq_ref,
        dkv_ref,
    ):
        core = order_ref[0]
        for slot in range(slots):
            here = slice(slot * piece, (slot + 1) * piece)
            one = pl.ds(place_of(order_ref, slot, core, piece), piece)
            two = pl.ds(place_of(order_ref, slot, 1 - core, piece), piece)
            whole[:, one, :] = mine_ref[:, here, :]
            whole[:, two, :] = other_ref[:, here, :]
            grads[one, :] = gm_ref[here, :]
            grads[two, :] = go_ref[here, :]
        heads = LANES // HEAD_DIM
        for head in range(heads):
            lanes = slice(head * HEAD_DIM, (head + 1) * HEAD_DIM)
            for first in reversed(range(0, length, CHUNK)):
                upto = first + CHUNK
                query = whole[0, first:upto, lanes]
                key = whole[1, :upto, lanes]
                value = whole[2, :upto, lanes]
                grad = grads[first:upto, lanes]
                scores = score_chunk(query, key, first, factor)
                probs = jnp.exp(scores - lse_ref[0, first:upto, head : head + 1])
                probs_grad = lax.dot_general(grad, value, across, preferred_element_type=F32)
                shift = jnp.sum(probs * probs_grad, axis=1, keepdims=True)
                scores_grad = (probs * (probs_grad - shift)).astype(BF16)
                dq_ref[first:upto, lanes] = (
                    jnp.dot(scores_grad, key, preferred_element_type=F32) * factor
                )
                dk = lax.dot_general(scores_grad, query, down, preferred_element_type=F32) * factor
                dv = lax.dot_general(
                    probs.astype(BF16), grad, down, preferred_element_type=F32
                )
                if upto == length:
                    dkv_ref[0, :, lanes] = dk
                    dkv_ref[1, :, lanes] = dv
                else:
                    dkv_ref[0, :upto, lanes] += dk
                    dkv_ref[1, :upto, lanes] += dv
        total = [jnp.zeros((1, LANES), F32) for _ in range(3)]
        for slot in range(slots):
            here = slice(slot * piece, (slot + 1) * piece)
            for at, table, out in (
                (core, tm_ref, out_mine),
                (1 - core, to_ref, out_other),
            ):
                rows_at = pl.ds(place_of(order_ref, slot, at, piece), piece)
                angles = table[:, here, :]
                parts = (
                    turn(dq_ref[rows_at, :], angles, -1).astype(BF16),
                    turn(dkv_ref[0, rows_at, :], angles, -1).astype(BF16),
                    dkv_ref[1, rows_at, :].astype(BF16),
                )
                for i in range(3):
                    out[i, here, :] = parts[i]
                    total[i] += jnp.sum(parts[i].astype(F32), axis=0, keepdims=True)
        for i in range(3):
            bias_ref[i] = total[i]

    groups = columns // LANES
    three = pl.BlockSpec((3, rows, LANES), lambda g, o: (0, 0, g))
    one = pl.BlockSpec((rows, LANES), lambda g, o: (0, g))
    full = pl.BlockSpec((3, rows, LANES), lambda g, o: (0, 0, 0))
    return pl.pallas_call(
        body,
        grid_spec=pltpu.PrefetchScalarGridSpec(
            num_scalar_prefetch=1,
            grid=(groups,),
            in_specs=[
                three,
                three,
                one,
                one,
                pl.BlockSpec((1, length, 2), lambda g, o: (g, 0, 0)),
                full,
                full,
            ],
            out_specs=[three, three, pl.BlockSpec((3, 1, LANES), lambda g, o: (0, 0, g))],
            scratch_shapes=[
                pltpu.VMEM((3, length, LANES), BF16),
                pltpu.VMEM((length, LANES), BF16),
                pltpu.VMEM((length, LANES), F32),
                pltpu.VMEM((2, length, LANES), F32),
            ],
        ),
        out_shape=[
            jax.ShapeDtypeStruct((3, rows, columns), BF16),
            jax.ShapeDtypeStruct((3, rows, columns), BF16),
            jax.ShapeDtypeStruct((3, 1, columns), F32),
        ],
        compiler_params=params(52),
        cost_estimate=cost(
            10 * length * length * columns, 40 * rows * columns, columns * length * length / 128
        ),
        name="attend_back",
    )(order, mine, other, grad_mine, grad_other, lse, table_mine, table_other)


ACROSS = (((1,), (1,)), ((), ()))
DOWN = (((0,), (0,)), ((), ()))


def feed_forward(tokens, pieces, hidden_grad):
    rows, width = tokens.shape
    units = pieces[0].shape[2]
    block = LANES if units % LANES == 0 else units
    cuts = cuts_of([p.shape[1] for p in pieces])

    def body(x_ref, *refs):
        hg_ref, hidden_ref, grad_ref = refs[-3:]
        gate_up = 0.0
        for w_ref, (low, high) in zip(refs, cuts):
            both = jnp.concatenate([w_ref[0], w_ref[1]], axis=1)
            gate_up += jnp.dot(x_ref[:, low:high], both, preferred_element_type=F32)
        gate, up = gate_up[:, :block], gate_up[:, block:]
        sigma = jax.nn.sigmoid(gate)
        silu = gate * sigma
        hidden_ref[...] = (silu * up).astype(BF16)
        grad = hg_ref[...].astype(F32)
        grad_ref[0] = (grad * up * sigma * (1.0 + gate * (1.0 - sigma))).astype(BF16)
        grad_ref[1] = (grad * silu).astype(BF16)

    return pl.pallas_call(
        body,
        grid=(units // block,),
        in_specs=[pl.BlockSpec((rows, width), lambda j: (0, 0))]
        + [pl.BlockSpec((2, p.shape[1], block), lambda j: (0, 0, j)) for p in pieces]
        + [pl.BlockSpec((rows, block), lambda j: (0, j))],
        out_specs=[
            pl.BlockSpec((rows, block), lambda j: (0, j)),
            pl.BlockSpec((2, rows, block), lambda j: (0, 0, j)),
        ],
        out_shape=[
            jax.ShapeDtypeStruct((rows, units), BF16),
            jax.ShapeDtypeStruct((2, rows, units), BF16),
        ],
        compiler_params=params(48),
        cost_estimate=cost(
            4 * rows * width * units, 4 * width * units + 2 * rows * width, rows * units
        ),
        name="feed_forward",
    )(tokens, *pieces, hidden_grad)


def to_features(values, pieces, across):
    count, rows, units = values.shape
    axis = 1 if across else 2
    sizes = [p.shape[axis] for p in pieces]
    block = sizes[-1]
    width = sum(sizes)
    owner = [i for i, size in enumerate(sizes) for _ in range(size // block)]
    starts = [owner.index(i) for i in range(len(pieces))]
    dims = ACROSS if across else (((1,), (0,)), ((), ()))

    def body(v_ref, *refs):
        step = pl.program_id(0)
        for i, w_ref in enumerate(refs[:-1]):

            @pl.when((step >= starts[i]) & (step < starts[i] + sizes[i] // block))
            def _():
                total = 0.0
                for n in range(count):
                    total += lax.dot_general(v_ref[n], w_ref[n], dims, preferred_element_type=F32)
                refs[-1][...] = total.astype(BF16)

    def spec(i):
        last = sizes[i] // block - 1
        at = lambda j: jnp.clip(j - starts[i], 0, last)
        if across:
            return pl.BlockSpec((count, block, units), lambda j: (0, at(j), 0))
        return pl.BlockSpec((count, units, block), lambda j: (0, 0, at(j)))

    return pl.pallas_call(
        body,
        grid=(width // block,),
        in_specs=[pl.BlockSpec((count, rows, units), lambda j: (0, 0, 0))]
        + [spec(i) for i in range(len(pieces))],
        out_specs=pl.BlockSpec((rows, block), lambda j: (0, j)),
        out_shape=jax.ShapeDtypeStruct((rows, width), BF16),
        compiler_params=params(56),
        cost_estimate=cost(
            2 * count * rows * width * units, 2 * count * (width + rows) * units + 2 * rows * width
        ),
        name="to_features",
    )(values, *pieces)


def from_features(index, tokens, pieces, block):
    rows, width = tokens.shape
    cuts = cuts_of([p.shape[1] for p in pieces])
    count = index.shape[0]

    def body(index_ref, x_ref, *refs):
        total = 0.0
        for w_ref, (low, high) in zip(refs, cuts):
            total += lax.dot_general(
                x_ref[:, low:high], w_ref[...], ACROSS, preferred_element_type=F32
            )
        refs[-1][0] = total.astype(BF16)

    out = pl.pallas_call(
        body,
        grid_spec=pltpu.PrefetchScalarGridSpec(
            num_scalar_prefetch=1,
            grid=(count,),
            in_specs=[pl.BlockSpec((rows, width), lambda j, q: (0, 0))]
            + [pl.BlockSpec((block, p.shape[1]), lambda j, q: (q[j], 0)) for p in pieces],
            out_specs=pl.BlockSpec((1, rows, block), lambda j, q: (j, 0, 0)),
        ),
        out_shape=jax.ShapeDtypeStruct((count, rows, block), BF16),
        compiler_params=params(40),
        cost_estimate=cost(
            2 * rows * width * block * count, 2 * width * (rows + block * count)
        ),
        name="from_features",
    )(index, tokens, *pieces)
    return out


def grad_quarters(quarters, tokens, others, adds, rows_first):
    rows, width = tokens.shape
    count, unused, units = others.shape
    quarter = width // 4
    k = quarters.shape[0]
    form = (quarter, units) if rows_first else (units, quarter)

    def body(q_ref, x_ref, y_ref, *refs):
        x, y = x_ref[...], y_ref[0]
        left, right = (x, y) if rows_first else (y, x)
        total = lax.dot_general(left, right, DOWN, preferred_element_type=F32)
        for ref in refs[:-1]:
            total += ref[0, 0].astype(F32)
        refs[-1][0, 0] = total.astype(BF16)

    def shifted(start):
        return pl.BlockSpec((1, 1, *form), lambda i, j, q: (i + start, j, 0, 0))

    return pl.pallas_call(
        body,
        grid_spec=pltpu.PrefetchScalarGridSpec(
            num_scalar_prefetch=1,
            grid=(k, count),
            in_specs=[
                pl.BlockSpec((rows, quarter), lambda i, j, q: (0, q[i])),
                pl.BlockSpec((1, rows, units), lambda i, j, q: (j, 0, 0)),
            ]
            + [shifted(start) for unused, start in adds],
            out_specs=shifted(0),
        ),
        out_shape=jax.ShapeDtypeStruct((k, count, *form), BF16),
        compiler_params=params(48, 2),
        cost_estimate=cost(
            2 * k * count * rows * quarter * units,
            2 * k * count * quarter * units * (1 + len(adds)) + 2 * rows * (width + count * units),
        ),
        name="grad_quarters",
    )(quarters, tokens, others, *[array for array, unused in adds])


def rotary_table(position):
    half = ROT // 2
    lane = jnp.arange(LANES) % HEAD_DIM
    frequency = 10000.0 ** (-((lane % half).astype(F32) * 2.0 / ROT))
    angles = position.astype(F32)[:, None] * frequency[None, :]
    lane = lane[None, :]
    cosine = jnp.where(lane < ROT, jnp.cos(angles), 1.0)
    sine = jnp.sin(angles)
    return jnp.stack(
        [
            cosine,
            jnp.where(lane < half, -sine, 0.0),
            jnp.where((lane >= half) & (lane < ROT), sine, 0.0),
        ]
    )


def local(
    inputs,
    first_gain,
    first_shift,
    project_in,
    project_bias,
    project_out,
    second_gain,
    second_shift,
    gate_weight,
    down_weight,
    cotangent,
):
    y_count = lax.axis_size("y")
    slots = lax.axis_size("col")
    y = lax.axis_index("y")
    core = lax.axis_index("core")
    row = lax.axis_index("row")
    place = lax.axis_index("col")
    factor = 1.0 / math.sqrt(HEAD_DIM)
    half_rows = inputs.shape[0] // 2
    wide = inputs.shape[1]
    width = 2 * wide

    def take(x, start, size, axis):
        return lax.dynamic_slice_in_dim(x, start, size, axis)

    straight = [(0, 0), (1, 2), (2, 1), (3, 3)]
    crossed = [(0, 2), (1, 0), (2, 3), (3, 1)]
    aligned = core == row

    def order_features(own, oth):
        low, high = oth[..., : wide // 2], oth[..., wide // 2 :]
        return jnp.concatenate(
            [own, jnp.where(core == 0, low, high), jnp.where(core == 0, high, low)], axis=-1
        )

    def natural(oth):
        low, high = oth[..., : wide // 2], oth[..., wide // 2 :]
        return jnp.concatenate(
            [jnp.where(core == 0, low, high), jnp.where(core == 0, high, low)], axis=-1
        )

    def to_sequence(x):
        a = lax.ppermute(take(x, row * half_rows, half_rows, 0), ("core", "row"), straight)
        b = lax.ppermute(take(x, (1 - row) * half_rows, half_rows, 0), ("core", "row"), crossed)
        return order_features(jnp.where(aligned, a, b), jnp.where(aligned, b, a))

    def from_sequence(x):
        own, oth = x[:, :wide], natural(x[:, wide:])
        a = jnp.where(aligned, own, oth)
        b = jnp.where(aligned, oth, own)
        a = lax.ppermute(a, ("core", "row"), [(j, i) for i, j in straight])
        b = lax.ppermute(b, ("core", "row"), [(j, i) for i, j in crossed])
        top = jnp.where(row == 0, a, b)
        bottom = jnp.where(row == 0, b, a)
        return jnp.concatenate([top, bottom], axis=0)

    def after(x, *others):
        return lax.optimization_barrier((x, *others))[0]

    order = slot_order(place, slots)
    table_of = jnp.concatenate([core[None], order]).astype(jnp.int32)
    inside = jnp.arange(half_rows)
    position = lambda c: ((order[:, None] * 2 + c) * half_rows + inside[None, :]).reshape(-1)
    rotary_mine = rotary_table(position(core))
    rotary_other = rotary_table(position(1 - core))

    stream = to_sequence(inputs)
    vectors = jnp.concatenate([first_gain, first_shift, second_gain, second_shift], axis=0)
    vectors = order_features(vectors, swap(vectors, "row"))
    gain_a, shift_a, gain_b, shift_b = (vectors[i : i + 1] for i in range(4))
    cot = to_sequence(cotangent)

    def part_of(w, axis):
        part = w.shape[axis] // 2
        return take(w, core * part, part, axis)

    w_in = jnp.transpose(project_in[0], (1, 0, 2))
    w_out, w_down = project_out[0], down_weight[0]
    w_gate = jnp.transpose(gate_weight[0], (1, 0, 2))
    low_a = norm_first(stream, gain_a, shift_a)
    in_half = swap(after(part_of(w_in, 1), stream, cot), "row")

    tokens_a = gather_slots(low_a, slots)
    tokens_a, in_half, w_gate = lax.optimization_barrier((tokens_a, in_half, w_gate))
    pieces_in = (w_in, in_half, swap(in_half, "core"))
    out_half = swap(after(part_of(w_out, 1), in_half), "row")
    down_half = swap(after(part_of(w_down, 1), in_half), "row")
    cot_rows = gather_slots(after(cot, tokens_a), slots)
    bias = project_bias[0][:, None, :]
    qkv_other = qkv_columns(tokens_a, pieces_in, bias, rotary_mine, (1 - core)[None])
    qkv_from = swap(qkv_other, "core")
    qkv_mine = qkv_columns(tokens_a, pieces_in, bias, rotary_mine, core[None])
    gate_half = swap(after(part_of(w_gate, 1), qkv_mine), "row")
    out_half = after(out_half, qkv_mine)
    pieces_out = (w_out, out_half, swap(out_half, "core"))
    out_mine, out_other, lse = attend(qkv_mine, qkv_from, table_of, factor)
    out_from = swap(out_other, "core")
    attended = jnp.concatenate(
        [jnp.where(core == 0, out_mine, out_from), jnp.where(core == 0, out_from, out_mine)], axis=1
    )
    part_out = to_features(attended[None], [p[None] for p in pieces_out], False)
    terms = scatter_slots(part_out, slots)
    residual, low_b = norm_second(stream, terms, gain_b, shift_b)

    tokens_b = gather_slots(low_b, slots)
    down_half, grad_rows = lax.optimization_barrier((down_half, cot_rows, low_b))[:2]
    pieces_down = (w_down, down_half, swap(down_half, "core"))
    units = w_down.shape[0]
    ways = 2 if units % 32 == 0 else 1
    hidden_grad = from_features(
        jnp.arange(ways, dtype=jnp.int32), grad_rows, pieces_down, units // ways
    )
    hidden_grad = jnp.concatenate([hidden_grad[i] for i in range(ways)], axis=1)
    tokens_b, gate_half, hidden_grad = lax.optimization_barrier((tokens_b, gate_half, hidden_grad))
    pieces_gate = (w_gate, gate_half, swap(gate_half, "core"))
    hidden, gate_up_grad = feed_forward(tokens_b, pieces_gate, hidden_grad)
    part_b = to_features(gate_up_grad, pieces_gate, True)
    terms = scatter_slots(part_b, slots)
    g2_low, sums_b, g2 = norm_back(residual, terms, cot, gain_b, 1)

    def quarters(*q):
        return jnp.stack(q).astype(jnp.int32)

    def to_core(tokens, others, rows_first):
        sent = grad_quarters(quarters(1 - core, 3 + 0 * core), tokens, others, (), rows_first)
        return swap(sent, "core")

    def to_row(tokens, others, rows_first, got):
        oth = grad_quarters(quarters(2 + 0 * core), tokens, others, ((got, 1),), rows_first)
        return oth

    def to_y(tokens, others, rows_first, got, arrived):
        own = grad_quarters(
            quarters(core), tokens, others, ((got, 0), (arrived, 0)), rows_first
        )[0]
        return own

    def finish(own, behind, rows_first):
        if y_count == 2:
            other = after(swap(own, "y"), behind)
            total = (own.astype(F32) + other.astype(F32)).astype(BF16)
        else:
            total = lax.psum(own, "y")
        rest = swap(total, "core")
        return jnp.concatenate(
            [jnp.where(core == 0, total, rest), jnp.where(core == 0, rest, total)],
            axis=1 if rows_first else 2,
        ).astype(F32)

    gate_got = to_core(tokens_b, gate_up_grad, True)
    down_got = to_core(grad_rows, hidden[None], False)
    down_oth = to_row(grad_rows, hidden[None], False, down_got)
    gate_oth = to_row(tokens_b, gate_up_grad, True, gate_got)
    down_arrived = swap(down_oth, "row")
    gate_arrived = swap(after(gate_oth, down_oth), "row")

    g2_low = after(g2_low, gate_oth, down_oth)
    g2_rows = gather_slots(g2_low, slots)
    down_own = to_y(grad_rows, hidden[None], False, down_got, after(down_arrived, g2_rows))
    columns = w_out.shape[0] // 2
    grad_other = from_features((1 - core)[None], g2_rows, pieces_out, columns)[0]
    grad_from = swap(grad_other, "core")
    grad_mine = from_features(core[None], g2_rows, pieces_out, columns)[0]
    part_down = to_features(after(hidden, g2_rows)[None], [p[None] for p in pieces_down], False)
    terms_down = scatter_slots(part_down, slots)
    out_got = to_core(g2_rows, attended[None], False)
    mixed_mine, mixed_other, bias_part = attend_back(
        qkv_mine, qkv_from, grad_mine, grad_from, lse, rotary_mine, rotary_other, table_of, factor
    )
    mixed_from = swap(mixed_other, "core")
    mixed = jnp.concatenate(
        [
            jnp.where(core == 0, mixed_mine, mixed_from),
            jnp.where(core == 0, mixed_from, mixed_mine),
        ],
        axis=2,
    )
    part_a = to_features(mixed, pieces_in, True)
    terms = scatter_slots(part_a, slots)
    in_got = to_core(tokens_a, mixed, True)
    gate_own = to_y(tokens_b, gate_up_grad, True, gate_got, after(gate_arrived, part_a))
    out_oth = to_row(g2_rows, attended[None], False, after(out_got, part_a))
    out_arrived = swap(out_oth, "row")
    in_oth = to_row(tokens_a, mixed, True, in_got)
    in_arrived = swap(after(in_oth, out_oth), "row")
    out_own = to_y(g2_rows, attended[None], False, out_got, out_arrived)
    in_own = to_y(tokens_a, mixed, True, in_got, in_arrived)
    input_low, sums_a = norm_back(stream, terms, g2, gain_a, 0)
    layer_low = (residual + sum(t.astype(F32) for t in terms_down)).astype(BF16)
    layer_out = from_sequence(after(layer_low, part_a))
    input_grad = from_sequence(input_low).astype(F32)
    down_grad = finish(down_own, part_a, False)[0]
    gate_grad = finish(gate_own, part_a, True)
    out_grad = finish(out_own, part_a, False)[0]
    in_grad = finish(in_own, part_a, True)

    def reduce_vector(own, oth, same):
        total = jnp.concatenate([own, same, oth], axis=0)
        if slots == 4:
            pair = total + lax.ppermute(total, "col", PAIR)
            inner = pair + lax.ppermute(pair, "col", MID)
            outer = lax.ppermute(inner, "col", OUT)
            total = jnp.where((place == 0) | (place == 3), outer, inner)
        else:
            total = lax.psum(total, "col")
        total = total + swap(total, "core")
        count = own.shape[0] + same.shape[0]
        sent = jnp.concatenate([total[count:], total[own.shape[0] : count]], axis=0)
        total = total[:count] + swap(sent, "row")
        return lax.psum(total, "y") if y_count != 2 else total + swap(total, "y")

    bias_all = jnp.zeros((3, 2 * slots * columns), F32)
    bias_all = lax.dynamic_update_slice(
        bias_all, bias_part[:, 0, :], (jnp.int32(0), (place * 2 + core) * columns)
    ).reshape(-1, wide)
    sums = jnp.concatenate([sums_a, sums_b], axis=0)
    vectors = reduce_vector(sums[:, :wide], natural(sums[:, wide:]), bias_all)
    bias_grad = take(vectors[4:].reshape(3, -1), place * 2 * columns, 2 * columns, 1)
    return (
        layer_out[None],
        input_grad,
        vectors[0:1],
        vectors[1:2],
        jnp.transpose(in_grad, (1, 0, 2))[None],
        bias_grad[None],
        out_grad[None],
        vectors[2:3],
        vectors[3:4],
        jnp.transpose(gate_grad, (1, 0, 2))[None],
        down_grad[None],
    )


def solution(mesh):
    dp, rows, cols = (mesh.shape[a] for a in ("dp", "row", "col"))
    split = Mesh(mesh.devices.reshape(dp // 2, 2, rows, cols), ("y", "core", "row", "col"))
    tokens = ("y", "core", "col")
    return jax.shard_map(
        local,
        mesh=split,
        in_specs=(
            P(tokens, "row"),
            P(None, "row"),
            P(None, "row"),
            P(None, "row", None, "col"),
            P(None, None, "col"),
            P(None, "col", "row"),
            P(None, "row"),
            P(None, "row"),
            P(None, "row", None, "col"),
            P(None, "col", "row"),
            P(tokens, "row"),
        ),
        out_specs=(
            P(None, tokens, "row"),
            P(tokens, "row"),
            P(None, "row"),
            P(None, "row"),
            P(None, "row", None, "col"),
            P(None, None, "col"),
            P(None, "col", "row"),
            P(None, "row"),
            P(None, "row"),
            P(None, "row", None, "col"),
            P(None, "col", "row"),
        ),
        check_vma=False,
    )
```

```python
import functools
import math

import jax
import jax.numpy as jnp
from jax import lax
from jax.experimental import pallas as pl
from jax.experimental.pallas import tpu as pltpu
from jax.sharding import Mesh
from jax.sharding import PartitionSpec as P

HEAD_DIM = 64
ROT = 16
LENGTH = 1024
EPSILON = 1e-05
F32 = jnp.float32
BF16 = jnp.bfloat16
LANES = 128
MIB = 1 << 20


def swap(x, axis):
    return lax.ppermute(x, axis, [(0, 1), (1, 0)])


PAIR = [(0, 1), (1, 0), (2, 3), (3, 2)]
MID = [(1, 2), (2, 1)]
OUT = [(1, 0), (2, 3)]
IN = [(0, 1), (3, 2)]
ORDER4 = ((0, 1, 2, 3), (1, 0, 2, 3), (2, 3, 1, 0), (3, 2, 1, 0))


def slot_order(place, count):
    if count == 4:
        return jnp.array(ORDER4, jnp.int32)[place]
    return jnp.arange(count, dtype=jnp.int32)


def tie(values, *behind):
    return lax.optimization_barrier((tuple(values), behind))[0]


def after(x, *behind):
    return tie((x,), *behind)[0] if behind else x


class Gather:
    def __init__(self, own, count):
        self.own, self.count, self.got = own, count, []
        self.flying = []
        if count == 4:
            self.flying = [lax.ppermute(own, "col", PAIR), lax.ppermute(own, "col", MID)]

    def hop(self):
        if self.count != 4:
            return
        if not self.got:
            one, mid = self.flying
            self.got = [one, mid]
            self.flying = [lax.ppermute(one, "col", MID), lax.ppermute(mid, "col", OUT)]
        else:
            far, mid_out = self.flying
            self.got += [far, mid_out]
            self.flying = [lax.ppermute(far, "col", OUT)]

    def rows(self):
        if self.count != 4:
            return lax.all_gather(self.own, "col", axis=0, tiled=True)
        one, mid, far, mid_out = self.got
        return jnp.concatenate([self.own, one, mid + mid_out, far + self.flying[0]], axis=0)


class Scatter:
    def __init__(self, parts, count):
        self.count, self.step, self.parts = count, 0, parts
        self.flying, self.two = [], None
        if count == 4:
            rows = parts.shape[0] // count
            self.part = [parts[i * rows : (i + 1) * rows] for i in range(4)]
            self.flying = [lax.ppermute(self.part[3], "col", IN)]
            self.two = lax.ppermute(self.part[2], "col", IN)

    def hop(self):
        if self.count != 4:
            return
        if self.step == 0:
            three = self.part[3] + self.flying[0]
            self.flying = [lax.ppermute(three, "col", MID), self.two]
        else:
            one, two = self.part[1] + self.flying[0], self.part[2] + self.flying[1]
            self.flying = [lax.ppermute(one, "col", PAIR), lax.ppermute(two, "col", MID)]
        self.step += 1

    def terms(self):
        if self.count != 4:
            mine = lax.psum_scatter(self.parts, "col", scatter_dimension=0, tiled=True)
            return (mine, jnp.zeros_like(mine), jnp.zeros_like(mine))
        return (self.part[0], *self.flying)


def sync(moving, *values):
    flat = [x for m in moving for x in m.flying] + list(values)
    flat = list(lax.optimization_barrier(tuple(flat)))
    for m in moving:
        count = len(m.flying)
        m.flying, flat = flat[:count], flat[count:]
    return flat[0] if len(flat) == 1 else flat


def params(mib, axes=1):
    return pltpu.CompilerParams(
        vmem_limit_bytes=mib * MIB, dimension_semantics=("arbitrary",) * axes
    )


SHARE = 8


def cost(flops, moved, trans=0):
    return pl.CostEstimate(
        flops=int(flops / SHARE),
        bytes_accessed=int(moved / SHARE),
        transcendentals=int(trans / SHARE),
    )


def stats_of(value):
    width = value.shape[1]
    average = jnp.sum(value, axis=1, keepdims=True) / width
    centred = value - average
    variance = jnp.sum(centred * centred, axis=1, keepdims=True) / width
    inv_root = lax.rsqrt(variance + EPSILON)
    return centred * inv_root, inv_root


def norm_first(stream, gain, shift):
    rows, width = stream.shape
    block = rows // 4

    def body(x_ref, gain_ref, shift_ref, low_ref):
        xhat, unused = stats_of(x_ref[...].astype(F32))
        low_ref[...] = (xhat * gain_ref[...] + shift_ref[...]).astype(BF16)

    row = pl.BlockSpec((block, width), lambda i: (i, 0))
    flat = pl.BlockSpec((1, width), lambda i: (0, 0))
    return pl.pallas_call(
        body,
        grid=(4,),
        in_specs=[row, flat, flat],
        out_specs=row,
        out_shape=jax.ShapeDtypeStruct((rows, width), BF16),
        compiler_params=params(16),
        cost_estimate=cost(rows * width * 10, rows * width * 4),
        name="norm_first",
    )(stream, gain, shift)


def norm_second(stream, terms, gain, shift):
    rows, width = stream.shape
    block = rows // 4

    def body(x_ref, a_ref, b_ref, c_ref, gain_ref, shift_ref, res_ref, low_ref):
        residual = (
            x_ref[...].astype(F32)
            + a_ref[...].astype(F32)
            + b_ref[...].astype(F32)
            + c_ref[...].astype(F32)
        )
        res_ref[...] = residual
        xhat, unused = stats_of(residual)
        low_ref[...] = (xhat * gain_ref[...] + shift_ref[...]).astype(BF16)

    row = pl.BlockSpec((block, width), lambda i: (i, 0))
    flat = pl.BlockSpec((1, width), lambda i: (0, 0))
    return pl.pallas_call(
        body,
        grid=(4,),
        in_specs=[row] * 4 + [flat, flat],
        out_specs=[row, row],
        out_shape=[
            jax.ShapeDtypeStruct((rows, width), F32),
            jax.ShapeDtypeStruct((rows, width), BF16),
        ],
        compiler_params=params(16),
        cost_estimate=cost(rows * width * 12, rows * width * 14),
        name="norm_second",
    )(stream, *terms, gain, shift)


def norm_back(stream, terms, upper, gain, both):
    rows, width = stream.shape
    block = rows // 4

    def body(x_ref, a_ref, b_ref, c_ref, up_ref, gain_ref, low_ref, sums_ref, *full_ref):
        xhat, inv_root = stats_of(x_ref[...].astype(F32))
        grad = a_ref[...].astype(F32) + b_ref[...].astype(F32) + c_ref[...].astype(F32)
        scaled = grad * gain_ref[...]
        mean_scaled = jnp.sum(scaled, axis=1, keepdims=True) / width
        mean_cross = jnp.sum(scaled * xhat, axis=1, keepdims=True) / width
        result = up_ref[...].astype(F32) + inv_root * (scaled - mean_scaled - xhat * mean_cross)
        low_ref[...] = result.astype(BF16)
        if full_ref:
            full_ref[0][...] = result

        @pl.when(pl.program_id(0) == 0)
        def _():
            sums_ref[...] = jnp.zeros_like(sums_ref)

        sums_ref[...] += jnp.concatenate(
            [
                jnp.sum(grad * xhat, axis=0, keepdims=True),
                jnp.sum(grad, axis=0, keepdims=True),
            ],
            axis=0,
        )

    row = pl.BlockSpec((block, width), lambda i: (i, 0))
    flat = pl.BlockSpec((1, width), lambda i: (0, 0))
    sums = pl.BlockSpec((2, width), lambda i: (0, 0))
    return pl.pallas_call(
        body,
        grid=(4,),
        in_specs=[row] * 5 + [flat],
        out_specs=[row, sums] + [row] * both,
        out_shape=[
            jax.ShapeDtypeStruct((rows, width), BF16),
            jax.ShapeDtypeStruct((2, width), F32),
        ]
        + [jax.ShapeDtypeStruct((rows, width), F32)] * both,
        compiler_params=params(24),
        cost_estimate=cost(rows * width * 20, rows * width * 18),
        name="norm_back",
    )(stream, *terms, upper, gain)


def cuts_of(sizes):
    ends = [sum(sizes[: i + 1]) for i in range(len(sizes))]
    return [(end - size, end) for end, size in zip(ends, sizes)]


def roll_lanes(value, shift):
    return pltpu.roll(value, shift % value.shape[1], 1)


def turn(value, table, sign):
    times = value.shape[1] // LANES
    wide = [jnp.concatenate([table[i]] * times, axis=1) for i in range(3)]
    ahead = roll_lanes(value, -(ROT // 2))
    behind = roll_lanes(value, ROT // 2)
    moved = ahead * wide[1] + behind * wide[2]
    return value * wide[0] + (moved if sign > 0 else -moved)


def qkv_columns(tokens, pieces, bias, table, half):
    rows, width = tokens.shape
    columns = pieces[0].shape[2] // 2
    cuts = cuts_of([p.shape[1] for p in pieces])

    def body(half_ref, x_ref, *refs):
        bias_ref, table_ref, out_ref = refs[-3:]
        which = pl.program_id(0)
        acc = bias_ref[0]
        for w_ref, (low, high) in zip(refs, cuts):
            acc = acc + jnp.dot(x_ref[:, low:high], w_ref[0], preferred_element_type=F32)

        @pl.when(which < 2)
        def _():
            out_ref[0] = turn(acc, table_ref, 1).astype(BF16)

        @pl.when(which == 2)
        def _():
            out_ref[0] = acc.astype(BF16)

    return pl.pallas_call(
        body,
        grid_spec=pltpu.PrefetchScalarGridSpec(
            num_scalar_prefetch=1,
            grid=(3,),
            in_specs=[pl.BlockSpec((rows, width), lambda j, h: (0, 0))]
            + [pl.BlockSpec((1, p.shape[1], columns), lambda j, h: (j, 0, h[0])) for p in pieces]
            + [
                pl.BlockSpec((1, 1, columns), lambda j, h: (j, 0, h[0])),
                pl.BlockSpec((3, rows, LANES), lambda j, h: (0, 0, 0)),
            ],
            out_specs=pl.BlockSpec((1, rows, columns), lambda j, h: (j, 0, 0)),
        ),
        out_shape=jax.ShapeDtypeStruct((3, rows, columns), BF16),
        compiler_params=params(40),
        cost_estimate=cost(6 * rows * width * columns, 2 * (rows * width + 3 * columns * width)),
        name="qkv_columns",
    )(half, tokens, *pieces, bias, table)


def place_of(order_ref, slot, core, rows):
    return pl.multiple_of((order_ref[1 + slot] * 2 + core) * rows, rows)


CHUNK = 256


def score_chunk(query, key, first, factor):
    scores = (
        lax.dot_general(query, key, (((1,), (1,)), ((), ())), preferred_element_type=F32) * factor
    )
    at_query = first + lax.broadcasted_iota(jnp.int32, scores.shape, 0)
    at_key = lax.broadcasted_iota(jnp.int32, scores.shape, 1)
    return jnp.where(at_query >= at_key, scores, -jnp.inf)


def attend(mine, other, order, factor):
    unused, rows, columns = mine.shape
    slots = order.shape[0] - 1
    piece = rows // slots
    length = 2 * rows

    def body(order_ref, mine_ref, other_ref, out_mine, out_other, lse_ref, whole, result):
        core = order_ref[0]
        for slot in range(slots):
            here = slice(slot * piece, (slot + 1) * piece)
            whole[:, pl.ds(place_of(order_ref, slot, core, piece), piece), :] = mine_ref[:, here, :]
            whole[:, pl.ds(place_of(order_ref, slot, 1 - core, piece), piece), :] = other_ref[
                :, here, :
            ]
        for head in range(LANES // HEAD_DIM):
            lanes = slice(head * HEAD_DIM, (head + 1) * HEAD_DIM)
            for first in range(0, length, CHUNK):
                upto = first + CHUNK
                scores = score_chunk(
                    whole[0, first:upto, lanes], whole[1, :upto, lanes], first, factor
                )
                highest = jnp.max(scores, axis=1, keepdims=True)
                exponent = jnp.exp(scores - highest)
                summed = jnp.sum(exponent, axis=1, keepdims=True)
                probs = (exponent * (1.0 / summed)).astype(BF16)
                result[first:upto, lanes] = jnp.dot(
                    probs, whole[2, :upto, lanes], preferred_element_type=F32
                ).astype(BF16)
                lse_ref[0, first:upto, head : head + 1] = highest + jnp.log(summed)
        for slot in range(slots):
            here = slice(slot * piece, (slot + 1) * piece)
            out_mine[here, :] = result[pl.ds(place_of(order_ref, slot, core, piece), piece), :]
            out_other[here, :] = result[pl.ds(place_of(order_ref, slot, 1 - core, piece), piece), :]

    groups = columns // LANES
    three = pl.BlockSpec((3, rows, LANES), lambda g, o: (0, 0, g))
    one = pl.BlockSpec((rows, LANES), lambda g, o: (0, g))
    return pl.pallas_call(
        body,
        grid_spec=pltpu.PrefetchScalarGridSpec(
            num_scalar_prefetch=1,
            grid=(groups,),
            in_specs=[three, three],
            out_specs=[one, one, pl.BlockSpec((1, length, 2), lambda g, o: (g, 0, 0))],
            scratch_shapes=[
                pltpu.VMEM((3, length, LANES), BF16),
                pltpu.VMEM((length, LANES), BF16),
            ],
        ),
        out_shape=[
            jax.ShapeDtypeStruct((rows, columns), BF16),
            jax.ShapeDtypeStruct((rows, columns), BF16),
            jax.ShapeDtypeStruct((groups, length, 2), F32),
        ],
        compiler_params=params(48),
        cost_estimate=cost(
            4 * length * length * columns, 16 * rows * columns, columns * length * length / 128
        ),
        name="attend",
    )(order, mine, other)


def attend_back(mine, other, grad_mine, grad_other, lse, table_mine, table_other, order, factor):
    unused, rows, columns = mine.shape
    slots = order.shape[0] - 1
    piece = rows // slots
    length = 2 * rows
    across = (((1,), (1,)), ((), ()))
    down = (((0,), (0,)), ((), ()))

    def body(
        order_ref,
        mine_ref,
        other_ref,
        gm_ref,
        go_ref,
        lse_ref,
        tm_ref,
        to_ref,
        out_mine,
        out_other,
        bias_ref,
        whole,
        grads,
        dq_ref,
        dkv_ref,
    ):
        core = order_ref[0]
        for slot in range(slots):
            here = slice(slot * piece, (slot + 1) * piece)
            one = pl.ds(place_of(order_ref, slot, core, piece), piece)
            two = pl.ds(place_of(order_ref, slot, 1 - core, piece), piece)
            whole[:, one, :] = mine_ref[:, here, :]
            whole[:, two, :] = other_ref[:, here, :]
            grads[one, :] = gm_ref[here, :]
            grads[two, :] = go_ref[here, :]
        heads = LANES // HEAD_DIM
        for head in range(heads):
            lanes = slice(head * HEAD_DIM, (head + 1) * HEAD_DIM)
            for first in reversed(range(0, length, CHUNK)):
                upto = first + CHUNK
                query = whole[0, first:upto, lanes]
                key = whole[1, :upto, lanes]
                value = whole[2, :upto, lanes]
                grad = grads[first:upto, lanes]
                scores = score_chunk(query, key, first, factor)
                probs = jnp.exp(scores - lse_ref[0, first:upto, head : head + 1])
                probs_grad = lax.dot_general(grad, value, across, preferred_element_type=F32)
                shift = jnp.sum(probs * probs_grad, axis=1, keepdims=True)
                scores_grad = (probs * (probs_grad - shift)).astype(BF16)
                dq_ref[first:upto, lanes] = (
                    jnp.dot(scores_grad, key, preferred_element_type=F32) * factor
                )
                dk = lax.dot_general(scores_grad, query, down, preferred_element_type=F32) * factor
                dv = lax.dot_general(
                    probs.astype(BF16), grad, down, preferred_element_type=F32
                )
                if upto == length:
                    dkv_ref[0, :, lanes] = dk
                    dkv_ref[1, :, lanes] = dv
                else:
                    dkv_ref[0, :upto, lanes] += dk
                    dkv_ref[1, :upto, lanes] += dv
        total = [jnp.zeros((1, LANES), F32) for _ in range(3)]
        for slot in range(slots):
            here = slice(slot * piece, (slot + 1) * piece)
            for at, table, out in (
                (core, tm_ref, out_mine),
                (1 - core, to_ref, out_other),
            ):
                rows_at = pl.ds(place_of(order_ref, slot, at, piece), piece)
                angles = table[:, here, :]
                parts = (
                    turn(dq_ref[rows_at, :], angles, -1).astype(BF16),
                    turn(dkv_ref[0, rows_at, :], angles, -1).astype(BF16),
                    dkv_ref[1, rows_at, :].astype(BF16),
                )
                for i in range(3):
                    out[i, here, :] = parts[i]
                    total[i] += jnp.sum(parts[i].astype(F32), axis=0, keepdims=True)
        for i in range(3):
            bias_ref[i] = total[i]

    groups = columns // LANES
    three = pl.BlockSpec((3, rows, LANES), lambda g, o: (0, 0, g))
    one = pl.BlockSpec((rows, LANES), lambda g, o: (0, g))
    full = pl.BlockSpec((3, rows, LANES), lambda g, o: (0, 0, 0))
    return pl.pallas_call(
        body,
        grid_spec=pltpu.PrefetchScalarGridSpec(
            num_scalar_prefetch=1,
            grid=(groups,),
            in_specs=[
                three,
                three,
                one,
                one,
                pl.BlockSpec((1, length, 2), lambda g, o: (g, 0, 0)),
                full,
                full,
            ],
            out_specs=[three, three, pl.BlockSpec((3, 1, LANES), lambda g, o: (0, 0, g))],
            scratch_shapes=[
                pltpu.VMEM((3, length, LANES), BF16),
                pltpu.VMEM((length, LANES), BF16),
                pltpu.VMEM((length, LANES), F32),
                pltpu.VMEM((2, length, LANES), F32),
            ],
        ),
        out_shape=[
            jax.ShapeDtypeStruct((3, rows, columns), BF16),
            jax.ShapeDtypeStruct((3, rows, columns), BF16),
            jax.ShapeDtypeStruct((3, 1, columns), F32),
        ],
        compiler_params=params(52),
        cost_estimate=cost(
            10 * length * length * columns, 40 * rows * columns, columns * length * length / 128
        ),
        name="attend_back",
    )(order, mine, other, grad_mine, grad_other, lse, table_mine, table_other)


ACROSS = (((1,), (1,)), ((), ()))
DOWN = (((0,), (0,)), ((), ()))


def feed_forward(tokens, pieces, hidden_grad):
    rows, width = tokens.shape
    units = pieces[0].shape[2]
    block = LANES if units % LANES == 0 else units
    cuts = cuts_of([p.shape[1] for p in pieces])

    def body(x_ref, *refs):
        hg_ref, hidden_ref, grad_ref = refs[-3:]
        gate_up = 0.0
        for w_ref, (low, high) in zip(refs, cuts):
            both = jnp.concatenate([w_ref[0], w_ref[1]], axis=1)
            gate_up += jnp.dot(x_ref[:, low:high], both, preferred_element_type=F32)
        gate, up = gate_up[:, :block], gate_up[:, block:]
        sigma = jax.nn.sigmoid(gate)
        silu = gate * sigma
        hidden_ref[...] = (silu * up).astype(BF16)
        grad = hg_ref[...].astype(F32)
        grad_ref[0] = (grad * up * sigma * (1.0 + gate * (1.0 - sigma))).astype(BF16)
        grad_ref[1] = (grad * silu).astype(BF16)

    return pl.pallas_call(
        body,
        grid=(units // block,),
        in_specs=[pl.BlockSpec((rows, width), lambda j: (0, 0))]
        + [pl.BlockSpec((2, p.shape[1], block), lambda j: (0, 0, j)) for p in pieces]
        + [pl.BlockSpec((rows, block), lambda j: (0, j))],
        out_specs=[
            pl.BlockSpec((rows, block), lambda j: (0, j)),
            pl.BlockSpec((2, rows, block), lambda j: (0, 0, j)),
        ],
        out_shape=[
            jax.ShapeDtypeStruct((rows, units), BF16),
            jax.ShapeDtypeStruct((2, rows, units), BF16),
        ],
        compiler_params=params(48),
        cost_estimate=cost(
            4 * rows * width * units, 4 * width * units + 2 * rows * width, rows * units
        ),
        name="feed_forward",
    )(tokens, *pieces, hidden_grad)


def to_features(values, pieces, across):
    count, rows, units = values.shape
    axis = 1 if across else 2
    sizes = [p.shape[axis] for p in pieces]
    block = sizes[-1]
    width = sum(sizes)
    owner = [i for i, size in enumerate(sizes) for _ in range(size // block)]
    starts = [owner.index(i) for i in range(len(pieces))]
    dims = ACROSS if across else (((1,), (0,)), ((), ()))

    def body(v_ref, *refs):
        step = pl.program_id(0)
        for i, w_ref in enumerate(refs[:-1]):

            @pl.when((step >= starts[i]) & (step < starts[i] + sizes[i] // block))
            def _():
                total = 0.0
                for n in range(count):
                    total += lax.dot_general(v_ref[n], w_ref[n], dims, preferred_element_type=F32)
                refs[-1][...] = total.astype(BF16)

    def spec(i):
        last = sizes[i] // block - 1
        at = lambda j: jnp.clip(j - starts[i], 0, last)
        if across:
            return pl.BlockSpec((count, block, units), lambda j: (0, at(j), 0))
        return pl.BlockSpec((count, units, block), lambda j: (0, 0, at(j)))

    return pl.pallas_call(
        body,
        grid=(width // block,),
        in_specs=[pl.BlockSpec((count, rows, units), lambda j: (0, 0, 0))]
        + [spec(i) for i in range(len(pieces))],
        out_specs=pl.BlockSpec((rows, block), lambda j: (0, j)),
        out_shape=jax.ShapeDtypeStruct((rows, width), BF16),
        compiler_params=params(56),
        cost_estimate=cost(
            2 * count * rows * width * units, 2 * count * (width + rows) * units + 2 * rows * width
        ),
        name="to_features",
    )(values, *pieces)


def from_features(index, tokens, pieces, block):
    rows, width = tokens.shape
    cuts = cuts_of([p.shape[1] for p in pieces])
    count = index.shape[0]

    def body(index_ref, x_ref, *refs):
        total = 0.0
        for w_ref, (low, high) in zip(refs, cuts):
            total += lax.dot_general(
                x_ref[:, low:high], w_ref[...], ACROSS, preferred_element_type=F32
            )
        refs[-1][0] = total.astype(BF16)

    out = pl.pallas_call(
        body,
        grid_spec=pltpu.PrefetchScalarGridSpec(
            num_scalar_prefetch=1,
            grid=(count,),
            in_specs=[pl.BlockSpec((rows, width), lambda j, q: (0, 0))]
            + [pl.BlockSpec((block, p.shape[1]), lambda j, q: (q[j], 0)) for p in pieces],
            out_specs=pl.BlockSpec((1, rows, block), lambda j, q: (j, 0, 0)),
        ),
        out_shape=jax.ShapeDtypeStruct((count, rows, block), BF16),
        compiler_params=params(40),
        cost_estimate=cost(
            2 * rows * width * block * count, 2 * width * (rows + block * count)
        ),
        name="from_features",
    )(index, tokens, *pieces)
    return out


def grad_quarters(quarters, tokens, others, adds, rows_first, first=0, count=None):
    rows, width = tokens.shape
    units = others.shape[2]
    count = others.shape[0] if count is None else count
    quarter = width // 4
    k = quarters.shape[0]
    form = (quarter, units) if rows_first else (units, quarter)

    def body(q_ref, x_ref, y_ref, *refs):
        x, y = x_ref[...], y_ref[0]
        left, right = (x, y) if rows_first else (y, x)
        total = lax.dot_general(left, right, DOWN, preferred_element_type=F32)
        for ref in refs[:-1]:
            total += ref[0, 0].astype(F32)
        refs[-1][0, 0] = total.astype(BF16)

    def shifted(at_k, at_n):
        return pl.BlockSpec((1, 1, *form), lambda i, j, q: (i + at_k, j + at_n, 0, 0))

    return pl.pallas_call(
        body,
        grid_spec=pltpu.PrefetchScalarGridSpec(
            num_scalar_prefetch=1,
            grid=(k, count),
            in_specs=[
                pl.BlockSpec((rows, quarter), lambda i, j, q: (0, q[i])),
                pl.BlockSpec((1, rows, units), lambda i, j, q: (j + first, 0, 0)),
            ]
            + [shifted(at_k, at_n) for unused, at_k, at_n in adds],
            out_specs=shifted(0, 0),
        ),
        out_shape=jax.ShapeDtypeStruct((k, count, *form), BF16),
        compiler_params=params(48, 2),
        cost_estimate=cost(
            2 * k * count * rows * quarter * units,
            2 * k * count * quarter * units * (1 + len(adds)) + 2 * rows * (width + count * units),
        ),
        name="grad_quarters",
    )(quarters, tokens, others, *[add[0] for add in adds])


def join_pairs(core, parts, rests):
    rows, units = parts[0].shape[1:]
    block = 128 if rows % 128 == 0 else rows
    steps = rows // block

    def body(core_ref, *refs):
        half = pl.program_id(0)
        out_ref = refs[-1]
        for i in range(2):

            @pl.when(half == core_ref[0])
            def _():
                out_ref[:, i, :] = refs[i][0].astype(F32)

            @pl.when(half != core_ref[0])
            def _():
                out_ref[:, i, :] = refs[2 + i][0].astype(F32)

    def spec(same):
        def at(h, j, c):
            wanted = (h == c[0]) if same else (h != c[0])
            return (0, jnp.where(wanted, j, 0), 0)

        return pl.BlockSpec((1, block, units), at)

    return pl.pallas_call(
        body,
        grid_spec=pltpu.PrefetchScalarGridSpec(
            num_scalar_prefetch=1,
            grid=(2, steps),
            in_specs=[spec(True), spec(True), spec(False), spec(False)],
            out_specs=pl.BlockSpec((block, 2, units), lambda h, j, c: (h * steps + j, 0, 0)),
        ),
        out_shape=jax.ShapeDtypeStruct((2 * rows, 2, units), F32),
        compiler_params=params(40, 2),
        cost_estimate=cost(rows * units, 24 * rows * units),
        name="join_pairs",
    )(core, *parts, *rests)


def rotary_table(position):
    half = ROT // 2
    lane = jnp.arange(LANES) % HEAD_DIM
    frequency = 10000.0 ** (-((lane % half).astype(F32) * 2.0 / ROT))
    angles = position.astype(F32)[:, None] * frequency[None, :]
    lane = lane[None, :]
    cosine = jnp.where(lane < ROT, jnp.cos(angles), 1.0)
    sine = jnp.sin(angles)
    return jnp.stack(
        [
            cosine,
            jnp.where(lane < half, -sine, 0.0),
            jnp.where((lane >= half) & (lane < ROT), sine, 0.0),
        ]
    )


def local(
    inputs,
    first_gain,
    first_shift,
    project_in,
    project_bias,
    project_out,
    second_gain,
    second_shift,
    gate_weight,
    down_weight,
    cotangent,
):
    y_count = lax.axis_size("y")
    slots = lax.axis_size("col")
    y = lax.axis_index("y")
    core = lax.axis_index("core")
    row = lax.axis_index("row")
    place = lax.axis_index("col")
    factor = 1.0 / math.sqrt(HEAD_DIM)
    half_rows = inputs.shape[0] // 2
    wide = inputs.shape[1]
    width = 2 * wide

    def take(x, start, size, axis):
        return lax.dynamic_slice_in_dim(x, start, size, axis)

    straight = [(0, 0), (1, 2), (2, 1), (3, 3)]
    crossed = [(0, 2), (1, 0), (2, 3), (3, 1)]
    aligned = core == row

    def order_features(own, oth):
        low, high = oth[..., : wide // 2], oth[..., wide // 2 :]
        return jnp.concatenate(
            [own, jnp.where(core == 0, low, high), jnp.where(core == 0, high, low)], axis=-1
        )

    def natural(oth):
        low, high = oth[..., : wide // 2], oth[..., wide // 2 :]
        return jnp.concatenate(
            [jnp.where(core == 0, low, high), jnp.where(core == 0, high, low)], axis=-1
        )

    def to_sequence(x):
        a = lax.ppermute(take(x, row * half_rows, half_rows, 0), ("core", "row"), straight)
        b = lax.ppermute(take(x, (1 - row) * half_rows, half_rows, 0), ("core", "row"), crossed)
        return order_features(jnp.where(aligned, a, b), jnp.where(aligned, b, a))

    def from_sequence(x):
        own, oth = x[:, :wide], natural(x[:, wide:])
        a = jnp.where(aligned, own, oth)
        b = jnp.where(aligned, oth, own)
        a = lax.ppermute(a, ("core", "row"), [(j, i) for i, j in straight])
        b = lax.ppermute(b, ("core", "row"), [(j, i) for i, j in crossed])
        top = jnp.where(row == 0, a, b)
        bottom = jnp.where(row == 0, b, a)
        return jnp.concatenate([top, bottom], axis=0)

    order = slot_order(place, slots)
    table_of = jnp.concatenate([core[None], order]).astype(jnp.int32)
    inside = jnp.arange(half_rows)
    position = lambda c: ((order[:, None] * 2 + c) * half_rows + inside[None, :]).reshape(-1)
    rotary_mine = rotary_table(position(core))
    rotary_other = rotary_table(position(1 - core))

    stream = to_sequence(inputs)
    vectors = jnp.concatenate([first_gain, first_shift, second_gain, second_shift], axis=0)
    vectors = order_features(vectors, swap(vectors, "row"))
    gain_a, shift_a, gain_b, shift_b = (vectors[i : i + 1] for i in range(4))

    def part_of(w, axis):
        part = w.shape[axis] // 2
        return take(w, core * part, part, axis)

    w_in = jnp.transpose(project_in[0], (1, 0, 2))
    w_out, w_down = project_out[0], down_weight[0]
    w_gate = jnp.transpose(gate_weight[0], (1, 0, 2))
    fixed = 0 * core

    def quarters(*q):
        return jnp.stack(q).astype(jnp.int32)

    def for_core(tokens, others, rows_first, **span):
        return grad_quarters(quarters(1 - core, 3 + fixed), tokens, others, (), rows_first, **span)

    def for_row(tokens, others, rows_first, got, at=0, **span):
        return grad_quarters(
            quarters(2 + fixed), tokens, others, ((got, 1, at),), rows_first, **span
        )

    def for_y(tokens, others, rows_first, got, arrived, at=0, **span):
        adds = ((got, 0, at), (arrived, 0, 0))
        return grad_quarters(quarters(core), tokens, others, adds, rows_first, **span)[0]

    def y_swap(own):
        return swap(own, "y") if y_count == 2 else lax.psum(own, "y")

    def y_total(own, other):
        return (own.astype(F32) + other.astype(F32)).astype(BF16) if y_count == 2 else other

    def join(total, rest, axis):
        return jnp.concatenate(
            [jnp.where(core == 0, total, rest), jnp.where(core == 0, rest, total)], axis=axis
        ).astype(F32)

    low_a = norm_first(stream, gain_a, shift_a)
    in_half = swap(after(part_of(w_in, 1), stream), "row")
    cot = to_sequence(after(cotangent, low_a))
    hops = Gather(low_a, slots)
    rotary_mine = sync([hops], rotary_mine)
    hops.hop()
    rotary_other = sync([hops], rotary_other)
    hops.hop()
    out_half = swap(after(part_of(w_out, 1), rotary_other), "row")
    w_gate, gate_part, in_half, cot = sync([hops], w_gate, part_of(w_gate, 1), in_half, cot)
    tokens_a = hops.rows()
    pieces_in = (w_in, in_half, swap(in_half, "core"))
    cot_hops = Gather(cot, slots)
    down_half = swap(after(part_of(w_down, 1), cot), "row")
    bias = project_bias[0][:, None, :]
    qkv_other = qkv_columns(tokens_a, pieces_in, bias, rotary_mine, (1 - core)[None])
    qkv_from = swap(qkv_other, "core")
    qkv_mine = qkv_columns(tokens_a, pieces_in, bias, rotary_mine, core[None])
    out_mine, out_other, lse = attend(qkv_mine, qkv_from, table_of, factor)
    out_mine, out_other, out_half = sync([cot_hops], out_mine, out_other, out_half)
    cot_hops.hop()
    pieces_out = (w_out, out_half, swap(out_half, "core"))
    out_from = swap(out_other, "core")
    attended = jnp.concatenate(
        [jnp.where(core == 0, out_mine, out_from), jnp.where(core == 0, out_from, out_mine)], axis=1
    )
    part_out = to_features(attended[None], [p[None] for p in pieces_out], False)
    part_out, gate_part = sync([cot_hops], part_out, gate_part)
    hops = Scatter(part_out, slots)
    cot_hops.hop()
    gate_half = swap(gate_part, "row")
    down_half = sync([hops, cot_hops], down_half)
    hops.hop()
    down_rest = sync([hops], swap(down_half, "core"))
    hops.hop()
    pieces_down = (w_down, down_half, down_rest)
    units = w_down.shape[0]
    ways = 2 if units % 32 == 0 else 1
    grad_rows = cot_hops.rows()
    hidden_grad = from_features(
        jnp.arange(ways, dtype=jnp.int32), grad_rows, pieces_down, units // ways
    )
    hidden_grad = jnp.concatenate([hidden_grad[i] for i in range(ways)], axis=1)
    grad_rows, hidden_grad = sync([hops], grad_rows, hidden_grad)
    residual, low_b = norm_second(stream, hops.terms(), gain_b, shift_b)

    hops = Gather(low_b, slots)
    sync([hops], low_b)
    hops.hop()
    gate_half = sync([hops], gate_half)
    hops.hop()
    gate_half, gate_rest = sync([hops], gate_half, swap(gate_half, "core"))
    tokens_b = hops.rows()
    pieces_gate = (w_gate, gate_half, gate_rest)
    hidden, pair = feed_forward(tokens_b, pieces_gate, hidden_grad)
    part_b = to_features(pair, pieces_gate, True)
    part_b, hidden, pair = sync([], part_b, hidden, pair)

    hops = Scatter(part_b, slots)
    down_got = swap(for_core(grad_rows, hidden[None], False), "core")
    gate_sent = for_core(tokens_b, pair, True)
    down_got, gate_sent = sync([hops], down_got, gate_sent)
    hops.hop()
    gate_got = swap(gate_sent, "core")
    down_oth = for_row(grad_rows, hidden[None], False, down_got)
    down_oth, gate_got = sync([hops], down_oth, gate_got)
    hops.hop()
    down_arrived = swap(down_oth, "row")
    gate_oth = [
        for_row(tokens_b, pair, True, gate_got, at=i, first=i, count=1) for i in range(2)
    ]
    gate_oth = list(sync([hops], *gate_oth))
    g2_low, sums_b, g2 = norm_back(residual, hops.terms(), cot, gain_b, 1)

    hops = Gather(g2_low, slots)
    gate_arrived = [swap(gate_oth[0], "row"), None]
    part_down = to_features(hidden[None], [p[None] for p in pieces_down], False)
    part_down, down_arrived = sync([hops], part_down, down_arrived)
    hops.hop()
    down_own = for_y(grad_rows, hidden[None], False, down_got, down_arrived)
    down_own, part_down = sync([hops], down_own, part_down)
    hops.hop()
    down_other = y_swap(down_own)
    gate_arrived[0], gate_oth[1] = sync([hops], gate_arrived[0], gate_oth[1])
    gate_arrived[1] = swap(gate_oth[1], "row")
    g2_rows = hops.rows()
    columns = w_out.shape[0] // 2
    grad_other = from_features((1 - core)[None], g2_rows, pieces_out, columns)[0]
    grad_from = swap(grad_other, "core")
    grad_mine = from_features(core[None], g2_rows, pieces_out, columns)[0]
    gate_own = [
        for_y(tokens_b, pair, True, gate_got, gate_arrived[0], at=0, first=0, count=1),
        None,
    ]
    out_sent = for_core(g2_rows, attended[None], False)
    grad_from, grad_mine, out_sent, gate_own[0], part_down, down_other = sync(
        [], grad_from, grad_mine, out_sent, gate_own[0], part_down, down_other
    )
    down_hops = Scatter(part_down, slots)
    gate_other = [y_swap(gate_own[0]), None]
    out_got = swap(out_sent, "core")
    mixed_mine, mixed_other, bias_part = attend_back(
        qkv_mine, qkv_from, grad_mine, grad_from, lse, rotary_mine, rotary_other, table_of, factor
    )
    mixed_mine, mixed_other, out_got, gate_arrived[1] = sync(
        [down_hops], mixed_mine, mixed_other, out_got, gate_arrived[1]
    )
    down_hops.hop()
    mixed_from = swap(mixed_other, "core")
    out_oth = for_row(g2_rows, attended[None], False, out_got)
    gate_own[1] = for_y(tokens_b, pair, True, gate_got, gate_arrived[1], at=1, first=1, count=1)
    mixed = jnp.concatenate(
        [
            jnp.where(core == 0, mixed_mine, mixed_from),
            jnp.where(core == 0, mixed_from, mixed_mine),
        ],
        axis=2,
    )
    in_sent = for_core(tokens_a, mixed, True)
    in_sent, mixed, gate_own[1], gate_other[0], out_oth = sync(
        [], in_sent, mixed, gate_own[1], gate_other[0], out_oth
    )
    in_got = swap(in_sent, "core")
    out_arrived = swap(out_oth, "row")
    gate_other[1] = y_swap(gate_own[1])
    part_a = to_features(mixed, pieces_in, True)
    part_a, in_got, out_arrived = sync([down_hops], part_a, in_got, out_arrived)
    hops = Scatter(part_a, slots)
    spans = (dict(at=0, first=0, count=2), dict(at=2, first=2, count=1))
    in_oth = [for_row(tokens_a, mixed, True, in_got, **span) for span in spans]
    in_arrived = [swap(x, "row") for x in in_oth]
    out_own = for_y(g2_rows, attended[None], False, out_got, out_arrived)
    *in_oth, out_own = sync([hops], *in_oth, out_own)
    hops.hop()
    down_total = y_total(down_own, down_other)
    gate_total = [y_total(gate_own[0], gate_other[0]), None]
    in_arrived[0], gate_other[1], down_total, gate_total[0] = sync(
        [hops], in_arrived[0], gate_other[1], down_total, gate_total[0]
    )
    hops.hop()
    out_other_y = y_swap(out_own)
    in_own = [for_y(tokens_a, mixed, True, in_got, in_arrived[0], **spans[0])]
    gate_total[1] = y_total(gate_own[1], gate_other[1])
    in_own[0], gate_total[1], in_arrived[1], out_other_y = sync(
        [hops], in_own[0], gate_total[1], in_arrived[1], out_other_y
    )
    in_other = [y_swap(in_own[0])]
    input_low, sums_a = norm_back(stream, hops.terms(), g2, gain_a, 0)
    down_rest = swap(down_total, "core")
    gate_rest = [swap(x, "core") for x in gate_total]
    in_own.append(for_y(tokens_a, mixed, True, in_got, in_arrived[1], **spans[1]))
    input_low, sums_a, in_own[1], down_rest, *gate_rest = sync(
        [], input_low, sums_a, in_own[1], down_rest, *gate_rest
    )
    input_grad = from_sequence(input_low)
    in_other.append(y_swap(in_own[1]))
    out_total = y_total(out_own, out_other_y)
    out_rest = swap(out_total, "core")
    gate_grad = join_pairs(core[None], gate_total, gate_rest)
    gate_grad, out_rest, input_grad = sync([], gate_grad, out_rest, input_grad)

    input_grad = input_grad.astype(F32)
    down_grad = join(down_total, down_rest, 2)[0]
    out_grad = join(out_total, out_rest, 2)[0]
    down_hops.flying = list(tie(down_hops.flying, input_grad)) if slots == 4 else []
    down_hops.hop()
    layer_low = (residual + sum(t.astype(F32) for t in down_hops.terms())).astype(BF16)
    layer_out = from_sequence(layer_low)
    in_total = [y_total(x, o) for x, o in zip(in_own, in_other)]
    in_grad = jnp.concatenate([join(x, swap(x, "core"), 1) for x in in_total], axis=0)

    def reduce_vector(own, oth, same):
        total = jnp.concatenate([own, same, oth], axis=0)
        if slots == 4:
            pair = total + lax.ppermute(total, "col", PAIR)
            inner = pair + lax.ppermute(pair, "col", MID)
            outer = lax.ppermute(inner, "col", OUT)
            total = jnp.where((place == 0) | (place == 3), outer, inner)
        else:
            total = lax.psum(total, "col")
        total = total + swap(total, "core")
        count = own.shape[0] + same.shape[0]
        sent = jnp.concatenate([total[count:], total[own.shape[0] : count]], axis=0)
        total = total[:count] + swap(sent, "row")
        return lax.psum(total, "y") if y_count != 2 else total + swap(total, "y")

    bias_all = jnp.zeros((3, 2 * slots * columns), F32)
    bias_all = lax.dynamic_update_slice(
        bias_all, bias_part[:, 0, :], (jnp.int32(0), (place * 2 + core) * columns)
    ).reshape(-1, wide)
    sums = after(jnp.concatenate([sums_a, sums_b], axis=0), in_own[1])
    vectors = reduce_vector(sums[:, :wide], natural(sums[:, wide:]), bias_all)
    bias_grad = take(vectors[4:].reshape(3, -1), place * 2 * columns, 2 * columns, 1)
    return (
        layer_out[None],
        input_grad,
        vectors[0:1],
        vectors[1:2],
        jnp.transpose(in_grad, (1, 0, 2))[None],
        bias_grad[None],
        out_grad[None],
        vectors[2:3],
        vectors[3:4],
        gate_grad[None],
        down_grad[None],
    )


def solution(mesh):
    dp, rows, cols = (mesh.shape[a] for a in ("dp", "row", "col"))
    split = Mesh(mesh.devices.reshape(dp // 2, 2, rows, cols), ("y", "core", "row", "col"))
    tokens = ("y", "core", "col")
    return jax.shard_map(
        local,
        mesh=split,
        in_specs=(
            P(tokens, "row"),
            P(None, "row"),
            P(None, "row"),
            P(None, "row", None, "col"),
            P(None, None, "col"),
            P(None, "col", "row"),
            P(None, "row"),
            P(None, "row"),
            P(None, "row", None, "col"),
            P(None, "col", "row"),
            P(tokens, "row"),
        ),
        out_specs=(
            P(None, tokens, "row"),
            P(tokens, "row"),
            P(None, "row"),
            P(None, "row"),
            P(None, "row", None, "col"),
            P(None, None, "col"),
            P(None, "col", "row"),
            P(None, "row"),
            P(None, "row"),
            P(None, "row", None, "col"),
            P(None, "col", "row"),
        ),
        check_vma=False,
    )
```

```python
import functools
import math

import jax
import jax.numpy as jnp
from jax import lax
from jax.experimental import pallas as pl
from jax.experimental.pallas import tpu as pltpu
from jax.sharding import Mesh
from jax.sharding import PartitionSpec as P

HEAD_DIM = 64
ROT = 16
LENGTH = 1024
EPSILON = 1e-05
F32 = jnp.float32
BF16 = jnp.bfloat16
LANES = 128
MIB = 1 << 20


def swap(x, axis):
    return lax.ppermute(x, axis, [(0, 1), (1, 0)])


PAIR = [(0, 1), (1, 0), (2, 3), (3, 2)]
MID = [(1, 2), (2, 1)]
OUT = [(1, 0), (2, 3)]
IN = [(0, 1), (3, 2)]
ORDER4 = ((0, 1, 2, 3), (1, 0, 2, 3), (2, 3, 1, 0), (3, 2, 1, 0))


def slot_order(place, count):
    if count == 4:
        return jnp.array(ORDER4, jnp.int32)[place]
    return jnp.arange(count, dtype=jnp.int32)


def tie(values, *behind):
    return lax.optimization_barrier((tuple(values), behind))[0]


def after(x, *behind):
    return tie((x,), *behind)[0] if behind else x


class Gather:
    def __init__(self, own, count):
        self.own, self.count, self.got = own, count, []
        self.flying = []
        if count == 4:
            self.flying = [lax.ppermute(own, "col", PAIR), lax.ppermute(own, "col", MID)]

    def hop(self):
        if self.count != 4:
            return
        if not self.got:
            one, mid = self.flying
            self.got = [one, mid]
            self.flying = [lax.ppermute(one, "col", MID), lax.ppermute(mid, "col", OUT)]
        else:
            far, mid_out = self.flying
            self.got += [far, mid_out]
            self.flying = [lax.ppermute(far, "col", OUT)]

    def rows(self):
        if self.count != 4:
            return lax.all_gather(self.own, "col", axis=0, tiled=True)
        one, mid, far, mid_out = self.got
        return jnp.concatenate([self.own, one, mid + mid_out, far + self.flying[0]], axis=0)


class Scatter:
    def __init__(self, parts, count):
        self.count, self.step, self.parts = count, 0, parts
        self.flying, self.two = [], None
        if count == 4:
            rows = parts.shape[0] // count
            self.part = [parts[i * rows : (i + 1) * rows] for i in range(4)]
            self.flying = [lax.ppermute(self.part[3], "col", IN)]
            self.two = lax.ppermute(self.part[2], "col", IN)

    def hop(self):
        if self.count != 4:
            return
        if self.step == 0:
            three = self.part[3] + self.flying[0]
            self.flying = [lax.ppermute(three, "col", MID), self.two]
        else:
            one, two = self.part[1] + self.flying[0], self.part[2] + self.flying[1]
            self.flying = [lax.ppermute(one, "col", PAIR), lax.ppermute(two, "col", MID)]
        self.step += 1

    def terms(self):
        if self.count != 4:
            mine = lax.psum_scatter(self.parts, "col", scatter_dimension=0, tiled=True)
            return (mine, jnp.zeros_like(mine), jnp.zeros_like(mine))
        return (self.part[0], *self.flying)


def sync(moving, *values):
    flat = [x for m in moving for x in m.flying] + list(values)
    flat = list(lax.optimization_barrier(tuple(flat)))
    for m in moving:
        count = len(m.flying)
        m.flying, flat = flat[:count], flat[count:]
    return flat[0] if len(flat) == 1 else flat


def params(mib, axes=1):
    return pltpu.CompilerParams(
        vmem_limit_bytes=mib * MIB, dimension_semantics=("arbitrary",) * axes
    )


SHARE = 8


def cost(flops, moved, trans=0):
    return pl.CostEstimate(
        flops=int(flops / SHARE),
        bytes_accessed=int(moved / SHARE),
        transcendentals=int(trans / SHARE),
    )


def stats_of(value):
    width = value.shape[1]
    average = jnp.sum(value, axis=1, keepdims=True) / width
    centred = value - average
    variance = jnp.sum(centred * centred, axis=1, keepdims=True) / width
    inv_root = lax.rsqrt(variance + EPSILON)
    return centred * inv_root, inv_root


def norm_first(stream, gain, shift):
    rows, width = stream.shape
    block = rows // 4

    def body(x_ref, gain_ref, shift_ref, low_ref):
        xhat, unused = stats_of(x_ref[...].astype(F32))
        low_ref[...] = (xhat * gain_ref[...] + shift_ref[...]).astype(BF16)

    row = pl.BlockSpec((block, width), lambda i: (i, 0))
    flat = pl.BlockSpec((1, width), lambda i: (0, 0))
    return pl.pallas_call(
        body,
        grid=(4,),
        in_specs=[row, flat, flat],
        out_specs=row,
        out_shape=jax.ShapeDtypeStruct((rows, width), BF16),
        compiler_params=params(16),
        cost_estimate=cost(rows * width * 10, rows * width * 4),
        name="norm_first",
    )(stream, gain, shift)


def norm_second(stream, terms, gain, shift):
    rows, width = stream.shape
    block = rows // 4

    def body(x_ref, a_ref, b_ref, c_ref, gain_ref, shift_ref, res_ref, low_ref):
        residual = (
            x_ref[...].astype(F32)
            + a_ref[...].astype(F32)
            + b_ref[...].astype(F32)
            + c_ref[...].astype(F32)
        )
        res_ref[...] = residual
        xhat, unused = stats_of(residual)
        low_ref[...] = (xhat * gain_ref[...] + shift_ref[...]).astype(BF16)

    row = pl.BlockSpec((block, width), lambda i: (i, 0))
    flat = pl.BlockSpec((1, width), lambda i: (0, 0))
    return pl.pallas_call(
        body,
        grid=(4,),
        in_specs=[row] * 4 + [flat, flat],
        out_specs=[row, row],
        out_shape=[
            jax.ShapeDtypeStruct((rows, width), F32),
            jax.ShapeDtypeStruct((rows, width), BF16),
        ],
        compiler_params=params(16),
        cost_estimate=cost(rows * width * 12, rows * width * 14),
        name="norm_second",
    )(stream, *terms, gain, shift)


def norm_back(stream, terms, upper, gain, both):
    rows, width = stream.shape
    block = rows // 4

    def body(x_ref, a_ref, b_ref, c_ref, up_ref, gain_ref, low_ref, sums_ref, *full_ref):
        xhat, inv_root = stats_of(x_ref[...].astype(F32))
        grad = a_ref[...].astype(F32) + b_ref[...].astype(F32) + c_ref[...].astype(F32)
        scaled = grad * gain_ref[...]
        mean_scaled = jnp.sum(scaled, axis=1, keepdims=True) / width
        mean_cross = jnp.sum(scaled * xhat, axis=1, keepdims=True) / width
        result = up_ref[...].astype(F32) + inv_root * (scaled - mean_scaled - xhat * mean_cross)
        low_ref[...] = result.astype(BF16)
        if full_ref:
            full_ref[0][...] = result

        @pl.when(pl.program_id(0) == 0)
        def _():
            sums_ref[...] = jnp.zeros_like(sums_ref)

        sums_ref[...] += jnp.concatenate(
            [
                jnp.sum(grad * xhat, axis=0, keepdims=True),
                jnp.sum(grad, axis=0, keepdims=True),
            ],
            axis=0,
        )

    row = pl.BlockSpec((block, width), lambda i: (i, 0))
    flat = pl.BlockSpec((1, width), lambda i: (0, 0))
    sums = pl.BlockSpec((2, width), lambda i: (0, 0))
    return pl.pallas_call(
        body,
        grid=(4,),
        in_specs=[row] * 5 + [flat],
        out_specs=[row, sums] + [row] * both,
        out_shape=[
            jax.ShapeDtypeStruct((rows, width), BF16),
            jax.ShapeDtypeStruct((2, width), F32),
        ]
        + [jax.ShapeDtypeStruct((rows, width), F32)] * both,
        compiler_params=params(24),
        cost_estimate=cost(rows * width * 20, rows * width * 18),
        name="norm_back",
    )(stream, *terms, upper, gain)


def cuts_of(sizes):
    ends = [sum(sizes[: i + 1]) for i in range(len(sizes))]
    return [(end - size, end) for end, size in zip(ends, sizes)]


def roll_lanes(value, shift):
    return pltpu.roll(value, shift % value.shape[1], 1)


def turn(value, table, sign):
    times = value.shape[1] // LANES
    wide = [jnp.concatenate([table[i]] * times, axis=1) for i in range(3)]
    ahead = roll_lanes(value, -(ROT // 2))
    behind = roll_lanes(value, ROT // 2)
    moved = ahead * wide[1] + behind * wide[2]
    return value * wide[0] + (moved if sign > 0 else -moved)


def qkv_columns(tokens, pieces, bias, table, half):
    rows, width = tokens.shape
    columns = pieces[0].shape[2] // 2
    cuts = cuts_of([p.shape[1] for p in pieces])

    def body(half_ref, x_ref, *refs):
        bias_ref, table_ref, out_ref = refs[-3:]
        which = pl.program_id(0)
        acc = bias_ref[0]
        for w_ref, (low, high) in zip(refs, cuts):
            acc = acc + jnp.dot(x_ref[:, low:high], w_ref[0], preferred_element_type=F32)

        @pl.when(which < 2)
        def _():
            out_ref[0] = turn(acc, table_ref, 1).astype(BF16)

        @pl.when(which == 2)
        def _():
            out_ref[0] = acc.astype(BF16)

    return pl.pallas_call(
        body,
        grid_spec=pltpu.PrefetchScalarGridSpec(
            num_scalar_prefetch=1,
            grid=(3,),
            in_specs=[pl.BlockSpec((rows, width), lambda j, h: (0, 0))]
            + [pl.BlockSpec((1, p.shape[1], columns), lambda j, h: (j, 0, h[0])) for p in pieces]
            + [
                pl.BlockSpec((1, 1, columns), lambda j, h: (j, 0, h[0])),
                pl.BlockSpec((3, rows, LANES), lambda j, h: (0, 0, 0)),
            ],
            out_specs=pl.BlockSpec((1, rows, columns), lambda j, h: (j, 0, 0)),
        ),
        out_shape=jax.ShapeDtypeStruct((3, rows, columns), BF16),
        compiler_params=params(40),
        cost_estimate=cost(6 * rows * width * columns, 2 * (rows * width + 3 * columns * width)),
        name="qkv_columns",
    )(half, tokens, *pieces, bias, table)


def place_of(order_ref, slot, core, rows):
    return pl.multiple_of((order_ref[1 + slot] * 2 + core) * rows, rows)


CHUNK = 256


def score_chunk(query, key, first):
    scores = lax.dot_general(query, key, (((1,), (1,)), ((), ())), preferred_element_type=F32)
    last = scores[:, first:]
    at_query = lax.broadcasted_iota(jnp.int32, last.shape, 0)
    at_key = lax.broadcasted_iota(jnp.int32, last.shape, 1)
    last = jnp.where(at_query >= at_key, last, -jnp.inf)
    return last if first == 0 else jnp.concatenate([scores[:, :first], last], axis=1)


def attend(mine, other, order, factor):
    unused, rows, columns = mine.shape
    slots = order.shape[0] - 1
    piece = rows // slots
    length = 2 * rows

    def body(order_ref, mine_ref, other_ref, out_mine, out_other, lse_ref, whole, result):
        core = order_ref[0]
        for slot in range(slots):
            here = slice(slot * piece, (slot + 1) * piece)
            whole[:, pl.ds(place_of(order_ref, slot, core, piece), piece), :] = mine_ref[:, here, :]
            whole[:, pl.ds(place_of(order_ref, slot, 1 - core, piece), piece), :] = other_ref[
                :, here, :
            ]
        for head in range(LANES // HEAD_DIM):
            lanes = slice(head * HEAD_DIM, (head + 1) * HEAD_DIM)
            for first in range(0, length, CHUNK):
                upto = first + CHUNK
                query = whole[0, first:upto, lanes] * jnp.bfloat16(factor)
                scores = score_chunk(query, whole[1, :upto, lanes], first)
                highest = jnp.max(scores, axis=1, keepdims=True)
                exponent = jnp.exp(scores - highest)
                summed = jnp.sum(exponent, axis=1, keepdims=True)
                mixed = jnp.dot(
                    exponent.astype(BF16), whole[2, :upto, lanes], preferred_element_type=F32
                )
                result[first:upto, lanes] = (mixed * (1.0 / summed)).astype(BF16)
                lse_ref[0, first:upto, head : head + 1] = highest + jnp.log(summed)
        for slot in range(slots):
            here = slice(slot * piece, (slot + 1) * piece)
            out_mine[here, :] = result[pl.ds(place_of(order_ref, slot, core, piece), piece), :]
            out_other[here, :] = result[pl.ds(place_of(order_ref, slot, 1 - core, piece), piece), :]

    groups = columns // LANES
    three = pl.BlockSpec((3, rows, LANES), lambda g, o: (0, 0, g))
    one = pl.BlockSpec((rows, LANES), lambda g, o: (0, g))
    return pl.pallas_call(
        body,
        grid_spec=pltpu.PrefetchScalarGridSpec(
            num_scalar_prefetch=1,
            grid=(groups,),
            in_specs=[three, three],
            out_specs=[one, one, pl.BlockSpec((1, length, 2), lambda g, o: (g, 0, 0))],
            scratch_shapes=[
                pltpu.VMEM((3, length, LANES), BF16),
                pltpu.VMEM((length, LANES), BF16),
            ],
        ),
        out_shape=[
            jax.ShapeDtypeStruct((rows, columns), BF16),
            jax.ShapeDtypeStruct((rows, columns), BF16),
            jax.ShapeDtypeStruct((groups, length, 2), F32),
        ],
        compiler_params=params(48),
        cost_estimate=cost(
            4 * length * length * columns, 16 * rows * columns, columns * length * length / 128
        ),
        name="attend",
    )(order, mine, other)


def attend_back(mine, other, grad_mine, grad_other, lse, table_mine, table_other, order, factor):
    unused, rows, columns = mine.shape
    slots = order.shape[0] - 1
    piece = rows // slots
    length = 2 * rows
    across = (((1,), (1,)), ((), ()))
    down = (((0,), (0,)), ((), ()))

    def body(
        order_ref,
        mine_ref,
        other_ref,
        gm_ref,
        go_ref,
        lse_ref,
        tm_ref,
        to_ref,
        out_mine,
        out_other,
        bias_ref,
        whole,
        grads,
        dq_ref,
        dkv_ref,
    ):
        core = order_ref[0]
        for slot in range(slots):
            here = slice(slot * piece, (slot + 1) * piece)
            one = pl.ds(place_of(order_ref, slot, core, piece), piece)
            two = pl.ds(place_of(order_ref, slot, 1 - core, piece), piece)
            whole[:, one, :] = mine_ref[:, here, :]
            whole[:, two, :] = other_ref[:, here, :]
            grads[one, :] = gm_ref[here, :]
            grads[two, :] = go_ref[here, :]
        heads = LANES // HEAD_DIM
        for head in range(heads):
            lanes = slice(head * HEAD_DIM, (head + 1) * HEAD_DIM)
            for first in reversed(range(0, length, CHUNK)):
                upto = first + CHUNK
                query = whole[0, first:upto, lanes] * jnp.bfloat16(factor)
                key = whole[1, :upto, lanes]
                value = whole[2, :upto, lanes]
                grad = grads[first:upto, lanes]
                scores = score_chunk(query, key, first)
                probs = jnp.exp(scores - lse_ref[0, first:upto, head : head + 1])
                probs_grad = lax.dot_general(grad, value, across, preferred_element_type=F32)
                shift = jnp.sum(probs * probs_grad, axis=1, keepdims=True)
                scores_grad = (probs * (probs_grad - shift)).astype(BF16)
                dq_ref[first:upto, lanes] = (
                    jnp.dot(scores_grad, key, preferred_element_type=F32) * factor
                )
                dk = lax.dot_general(scores_grad, query, down, preferred_element_type=F32)
                dv = lax.dot_general(
                    probs.astype(BF16), grad, down, preferred_element_type=F32
                )
                if upto == length:
                    dkv_ref[0, :, lanes] = dk
                    dkv_ref[1, :, lanes] = dv
                else:
                    dkv_ref[0, :upto, lanes] += dk
                    dkv_ref[1, :upto, lanes] += dv
        total = [jnp.zeros((1, LANES), F32) for _ in range(3)]
        for slot in range(slots):
            here = slice(slot * piece, (slot + 1) * piece)
            for at, table, out in (
                (core, tm_ref, out_mine),
                (1 - core, to_ref, out_other),
            ):
                rows_at = pl.ds(place_of(order_ref, slot, at, piece), piece)
                angles = table[:, here, :]
                parts = (
                    turn(dq_ref[rows_at, :], angles, -1).astype(BF16),
                    turn(dkv_ref[0, rows_at, :], angles, -1).astype(BF16),
                    dkv_ref[1, rows_at, :].astype(BF16),
                )
                for i in range(3):
                    out[i, here, :] = parts[i]
                    total[i] += jnp.sum(parts[i].astype(F32), axis=0, keepdims=True)
        for i in range(3):
            bias_ref[i] = total[i]

    groups = columns // LANES
    three = pl.BlockSpec((3, rows, LANES), lambda g, o: (0, 0, g))
    one = pl.BlockSpec((rows, LANES), lambda g, o: (0, g))
    full = pl.BlockSpec((3, rows, LANES), lambda g, o: (0, 0, 0))
    return pl.pallas_call(
        body,
        grid_spec=pltpu.PrefetchScalarGridSpec(
            num_scalar_prefetch=1,
            grid=(groups,),
            in_specs=[
                three,
                three,
                one,
                one,
                pl.BlockSpec((1, length, 2), lambda g, o: (g, 0, 0)),
                full,
                full,
            ],
            out_specs=[three, three, pl.BlockSpec((3, 1, LANES), lambda g, o: (0, 0, g))],
            scratch_shapes=[
                pltpu.VMEM((3, length, LANES), BF16),
                pltpu.VMEM((length, LANES), BF16),
                pltpu.VMEM((length, LANES), F32),
                pltpu.VMEM((2, length, LANES), F32),
            ],
        ),
        out_shape=[
            jax.ShapeDtypeStruct((3, rows, columns), BF16),
            jax.ShapeDtypeStruct((3, rows, columns), BF16),
            jax.ShapeDtypeStruct((3, 1, columns), F32),
        ],
        compiler_params=params(52),
        cost_estimate=cost(
            10 * length * length * columns, 40 * rows * columns, columns * length * length / 128
        ),
        name="attend_back",
    )(order, mine, other, grad_mine, grad_other, lse, table_mine, table_other)


ACROSS = (((1,), (1,)), ((), ()))
DOWN = (((0,), (0,)), ((), ()))


def feed_forward(tokens, pieces, hidden_grad):
    rows, width = tokens.shape
    units = pieces[0].shape[2]
    block = 256 if units > 256 else units
    cuts = cuts_of([p.shape[1] for p in pieces])

    def body(x_ref, *refs):
        hg_ref, hidden_ref, grad_ref = refs[-3:]
        gate_up = 0.0
        for w_ref, (low, high) in zip(refs, cuts):
            both = jnp.concatenate([w_ref[0], w_ref[1]], axis=1)
            gate_up += jnp.dot(x_ref[:, low:high], both, preferred_element_type=F32)
        gate, up = gate_up[:, :block], gate_up[:, block:]
        sigma = jax.nn.sigmoid(gate)
        silu = gate * sigma
        hidden_ref[...] = (silu * up).astype(BF16)
        grad = hg_ref[...].astype(F32)
        grad_ref[0] = (grad * up * (sigma + silu * (1.0 - sigma))).astype(BF16)
        grad_ref[1] = (grad * silu).astype(BF16)

    return pl.pallas_call(
        body,
        grid=(pl.cdiv(units, block),),
        in_specs=[pl.BlockSpec((rows, width), lambda j: (0, 0))]
        + [pl.BlockSpec((2, p.shape[1], block), lambda j: (0, 0, j)) for p in pieces]
        + [pl.BlockSpec((rows, block), lambda j: (0, j))],
        out_specs=[
            pl.BlockSpec((rows, block), lambda j: (0, j)),
            pl.BlockSpec((2, rows, block), lambda j: (0, 0, j)),
        ],
        out_shape=[
            jax.ShapeDtypeStruct((rows, units), BF16),
            jax.ShapeDtypeStruct((2, rows, units), BF16),
        ],
        compiler_params=params(48),
        cost_estimate=cost(
            4 * rows * width * units, 4 * width * units + 2 * rows * width, rows * units
        ),
        name="feed_forward",
    )(tokens, *pieces, hidden_grad)


def to_features(values, pieces, across):
    count, rows, units = values.shape
    axis = 1 if across else 2
    sizes = [p.shape[axis] for p in pieces]
    block = sizes[-1]
    width = sum(sizes)
    owner = [i for i, size in enumerate(sizes) for _ in range(size // block)]
    starts = [owner.index(i) for i in range(len(pieces))]
    dims = ACROSS if across else (((1,), (0,)), ((), ()))

    def body(v_ref, *refs):
        step = pl.program_id(0)
        for i, w_ref in enumerate(refs[:-1]):

            @pl.when((step >= starts[i]) & (step < starts[i] + sizes[i] // block))
            def _():
                total = 0.0
                for n in range(count):
                    total += lax.dot_general(v_ref[n], w_ref[n], dims, preferred_element_type=F32)
                refs[-1][...] = total.astype(BF16)

    def spec(i):
        last = sizes[i] // block - 1
        at = lambda j: jnp.clip(j - starts[i], 0, last)
        if across:
            return pl.BlockSpec((count, block, units), lambda j: (0, at(j), 0))
        return pl.BlockSpec((count, units, block), lambda j: (0, 0, at(j)))

    return pl.pallas_call(
        body,
        grid=(width // block,),
        in_specs=[pl.BlockSpec((count, rows, units), lambda j: (0, 0, 0))]
        + [spec(i) for i in range(len(pieces))],
        out_specs=pl.BlockSpec((rows, block), lambda j: (0, j)),
        out_shape=jax.ShapeDtypeStruct((rows, width), BF16),
        compiler_params=params(56),
        cost_estimate=cost(
            2 * count * rows * width * units, 2 * count * (width + rows) * units + 2 * rows * width
        ),
        name="to_features",
    )(values, *pieces)


def from_features(index, tokens, pieces, block):
    rows, width = tokens.shape
    cuts = cuts_of([p.shape[1] for p in pieces])
    count = index.shape[0]

    def body(index_ref, x_ref, *refs):
        total = 0.0
        for w_ref, (low, high) in zip(refs, cuts):
            total += lax.dot_general(
                x_ref[:, low:high], w_ref[...], ACROSS, preferred_element_type=F32
            )
        refs[-1][0] = total.astype(BF16)

    out = pl.pallas_call(
        body,
        grid_spec=pltpu.PrefetchScalarGridSpec(
            num_scalar_prefetch=1,
            grid=(count,),
            in_specs=[pl.BlockSpec((rows, width), lambda j, q: (0, 0))]
            + [pl.BlockSpec((block, p.shape[1]), lambda j, q: (q[j], 0)) for p in pieces],
            out_specs=pl.BlockSpec((1, rows, block), lambda j, q: (j, 0, 0)),
        ),
        out_shape=jax.ShapeDtypeStruct((count, rows, block), BF16),
        compiler_params=params(40),
        cost_estimate=cost(
            2 * rows * width * block * count, 2 * width * (rows + block * count)
        ),
        name="from_features",
    )(index, tokens, *pieces)
    return out


def grad_quarters(quarters, tokens, others, adds, rows_first, first=0, count=None):
    rows, width = tokens.shape
    units = others.shape[2]
    count = others.shape[0] if count is None else count
    quarter = width // 4
    k = quarters.shape[0]
    form = (quarter, units) if rows_first else (units, quarter)

    def body(q_ref, x_ref, y_ref, *refs):
        x, y = x_ref[...], y_ref[0]
        left, right = (x, y) if rows_first else (y, x)
        total = lax.dot_general(left, right, DOWN, preferred_element_type=F32)
        for ref in refs[:-1]:
            total += ref[0, 0].astype(F32)
        refs[-1][0, 0] = total.astype(BF16)

    def shifted(at_k, at_n):
        return pl.BlockSpec((1, 1, *form), lambda i, j, q: (i + at_k, j + at_n, 0, 0))

    return pl.pallas_call(
        body,
        grid_spec=pltpu.PrefetchScalarGridSpec(
            num_scalar_prefetch=1,
            grid=(k, count),
            in_specs=[
                pl.BlockSpec((rows, quarter), lambda i, j, q: (0, q[i])),
                pl.BlockSpec((1, rows, units), lambda i, j, q: (j + first, 0, 0)),
            ]
            + [shifted(at_k, at_n) for unused, at_k, at_n in adds],
            out_specs=shifted(0, 0),
        ),
        out_shape=jax.ShapeDtypeStruct((k, count, *form), BF16),
        compiler_params=params(48, 2),
        cost_estimate=cost(
            2 * k * count * rows * quarter * units,
            2 * k * count * quarter * units * (1 + len(adds)) + 2 * rows * (width + count * units),
        ),
        name="grad_quarters",
    )(quarters, tokens, others, *[add[0] for add in adds])


def join_pairs(core, parts, rests):
    rows, units = parts[0].shape[1:]
    block = 128 if rows % 128 == 0 else rows
    steps = rows // block

    def body(core_ref, *refs):
        half = pl.program_id(0)
        out_ref = refs[-1]
        for i in range(2):

            @pl.when(half == core_ref[0])
            def _():
                out_ref[:, i, :] = refs[i][0].astype(F32)

            @pl.when(half != core_ref[0])
            def _():
                out_ref[:, i, :] = refs[2 + i][0].astype(F32)

    def spec(same):
        def at(h, j, c):
            wanted = (h == c[0]) if same else (h != c[0])
            return (0, jnp.where(wanted, j, 0), 0)

        return pl.BlockSpec((1, block, units), at)

    return pl.pallas_call(
        body,
        grid_spec=pltpu.PrefetchScalarGridSpec(
            num_scalar_prefetch=1,
            grid=(2, steps),
            in_specs=[spec(True), spec(True), spec(False), spec(False)],
            out_specs=pl.BlockSpec((block, 2, units), lambda h, j, c: (h * steps + j, 0, 0)),
        ),
        out_shape=jax.ShapeDtypeStruct((2 * rows, 2, units), F32),
        compiler_params=params(40, 2),
        cost_estimate=cost(rows * units, 24 * rows * units),
        name="join_pairs",
    )(core, *parts, *rests)


def rotary_table(position):
    half = ROT // 2
    lane = jnp.arange(LANES) % HEAD_DIM
    frequency = 10000.0 ** (-((lane % half).astype(F32) * 2.0 / ROT))
    angles = position.astype(F32)[:, None] * frequency[None, :]
    lane = lane[None, :]
    cosine = jnp.where(lane < ROT, jnp.cos(angles), 1.0)
    sine = jnp.sin(angles)
    return jnp.stack(
        [
            cosine,
            jnp.where(lane < half, -sine, 0.0),
            jnp.where((lane >= half) & (lane < ROT), sine, 0.0),
        ]
    )


def local(
    inputs,
    first_gain,
    first_shift,
    project_in,
    project_bias,
    project_out,
    second_gain,
    second_shift,
    gate_weight,
    down_weight,
    cotangent,
):
    y_count = lax.axis_size("y")
    slots = lax.axis_size("col")
    y = lax.axis_index("y")
    core = lax.axis_index("core")
    row = lax.axis_index("row")
    place = lax.axis_index("col")
    factor = 1.0 / math.sqrt(HEAD_DIM)
    half_rows = inputs.shape[0] // 2
    wide = inputs.shape[1]
    width = 2 * wide

    def take(x, start, size, axis):
        return lax.dynamic_slice_in_dim(x, start, size, axis)

    straight = [(0, 0), (1, 2), (2, 1), (3, 3)]
    crossed = [(0, 2), (1, 0), (2, 3), (3, 1)]
    aligned = core == row

    def order_features(own, oth):
        low, high = oth[..., : wide // 2], oth[..., wide // 2 :]
        return jnp.concatenate(
            [own, jnp.where(core == 0, low, high), jnp.where(core == 0, high, low)], axis=-1
        )

    def natural(oth):
        low, high = oth[..., : wide // 2], oth[..., wide // 2 :]
        return jnp.concatenate(
            [jnp.where(core == 0, low, high), jnp.where(core == 0, high, low)], axis=-1
        )

    def to_sequence(x):
        a = lax.ppermute(take(x, row * half_rows, half_rows, 0), ("core", "row"), straight)
        b = lax.ppermute(take(x, (1 - row) * half_rows, half_rows, 0), ("core", "row"), crossed)
        return order_features(jnp.where(aligned, a, b), jnp.where(aligned, b, a))

    def from_sequence(x):
        own, oth = x[:, :wide], natural(x[:, wide:])
        a = jnp.where(aligned, own, oth)
        b = jnp.where(aligned, oth, own)
        a = lax.ppermute(a, ("core", "row"), [(j, i) for i, j in straight])
        b = lax.ppermute(b, ("core", "row"), [(j, i) for i, j in crossed])
        top = jnp.where(row == 0, a, b)
        bottom = jnp.where(row == 0, b, a)
        return jnp.concatenate([top, bottom], axis=0)

    order = slot_order(place, slots)
    table_of = jnp.concatenate([core[None], order]).astype(jnp.int32)
    inside = jnp.arange(half_rows)
    position = lambda c: ((order[:, None] * 2 + c) * half_rows + inside[None, :]).reshape(-1)
    rotary_mine = rotary_table(position(core))
    rotary_other = rotary_table(position(1 - core))

    stream = to_sequence(inputs)
    vectors = jnp.concatenate([first_gain, first_shift, second_gain, second_shift], axis=0)
    vectors = order_features(vectors, swap(vectors, "row"))
    gain_a, shift_a, gain_b, shift_b = (vectors[i : i + 1] for i in range(4))

    def part_of(w, axis):
        part = w.shape[axis] // 2
        return take(w, core * part, part, axis)

    w_in = jnp.transpose(project_in[0], (1, 0, 2))
    w_out, w_down = project_out[0], down_weight[0]
    w_gate = jnp.transpose(gate_weight[0], (1, 0, 2))
    fixed = 0 * core

    def quarters(*q):
        return jnp.stack(q).astype(jnp.int32)

    def for_core(tokens, others, rows_first, **span):
        return grad_quarters(quarters(1 - core, 3 + fixed), tokens, others, (), rows_first, **span)

    def for_row(tokens, others, rows_first, got, at=0, **span):
        return grad_quarters(
            quarters(2 + fixed), tokens, others, ((got, 1, at),), rows_first, **span
        )

    def for_y(tokens, others, rows_first, got, arrived, at=0, **span):
        adds = ((got, 0, at), (arrived, 0, 0))
        return grad_quarters(quarters(core), tokens, others, adds, rows_first, **span)[0]

    def y_swap(own):
        return swap(own, "y") if y_count == 2 else lax.psum(own, "y")

    def y_total(own, other):
        return (own.astype(F32) + other.astype(F32)).astype(BF16) if y_count == 2 else other

    def join(total, rest, axis):
        return jnp.concatenate(
            [jnp.where(core == 0, total, rest), jnp.where(core == 0, rest, total)], axis=axis
        ).astype(F32)

    low_a = norm_first(stream, gain_a, shift_a)
    in_half = swap(after(part_of(w_in, 1), stream), "row")
    cot = to_sequence(after(cotangent, low_a))
    hops = Gather(low_a, slots)
    rotary_mine = sync([hops], rotary_mine)
    hops.hop()
    rotary_other = sync([hops], rotary_other)
    hops.hop()
    out_half = swap(after(part_of(w_out, 1), rotary_other), "row")
    w_gate, gate_part, in_half, cot = sync([hops], w_gate, part_of(w_gate, 1), in_half, cot)
    tokens_a = hops.rows()
    pieces_in = (w_in, in_half, swap(in_half, "core"))
    cot_hops = Gather(cot, slots)
    down_half = swap(after(part_of(w_down, 1), cot), "row")
    bias = project_bias[0][:, None, :]
    qkv_other = qkv_columns(tokens_a, pieces_in, bias, rotary_mine, (1 - core)[None])
    qkv_from = swap(qkv_other, "core")
    qkv_mine = qkv_columns(tokens_a, pieces_in, bias, rotary_mine, core[None])
    out_mine, out_other, lse = attend(qkv_mine, qkv_from, table_of, factor)
    out_mine, out_other, out_half = sync([cot_hops], out_mine, out_other, out_half)
    cot_hops.hop()
    pieces_out = (w_out, out_half, swap(out_half, "core"))
    out_from = swap(out_other, "core")
    attended = jnp.concatenate(
        [jnp.where(core == 0, out_mine, out_from), jnp.where(core == 0, out_from, out_mine)], axis=1
    )
    part_out = to_features(attended[None], [p[None] for p in pieces_out], False)
    part_out, gate_part = sync([cot_hops], part_out, gate_part)
    hops = Scatter(part_out, slots)
    cot_hops.hop()
    gate_half = swap(gate_part, "row")
    down_half = sync([hops, cot_hops], down_half)
    hops.hop()
    down_rest = sync([hops], swap(down_half, "core"))
    hops.hop()
    pieces_down = (w_down, down_half, down_rest)
    units = w_down.shape[0]
    ways = 2 if units % 32 == 0 else 1
    grad_rows = cot_hops.rows()
    hidden_grad = from_features(
        jnp.arange(ways, dtype=jnp.int32), grad_rows, pieces_down, units // ways
    )
    hidden_grad = jnp.concatenate([hidden_grad[i] for i in range(ways)], axis=1)
    grad_rows, hidden_grad = sync([hops], grad_rows, hidden_grad)
    residual, low_b = norm_second(stream, hops.terms(), gain_b, shift_b)

    hops = Gather(low_b, slots)
    sync([hops], low_b)
    hops.hop()
    gate_half = sync([hops], gate_half)
    hops.hop()
    gate_half, gate_rest = sync([hops], gate_half, swap(gate_half, "core"))
    tokens_b = hops.rows()
    pieces_gate = (w_gate, gate_half, gate_rest)
    hidden, pair = feed_forward(tokens_b, pieces_gate, hidden_grad)
    part_b = to_features(pair, pieces_gate, True)
    part_b, hidden, pair = sync([], part_b, hidden, pair)

    hops = Scatter(part_b, slots)
    down_sent = for_core(grad_rows, hidden[None], False)
    gate_sent = for_core(tokens_b, pair, True)
    down_sent, gate_sent = sync([hops], down_sent, gate_sent)
    hops.hop()
    down_got = swap(down_sent, "core")
    gate_got = swap(gate_sent, "core")
    down_oth = for_row(grad_rows, hidden[None], False, down_got)
    down_oth, gate_got = sync([hops], down_oth, gate_got)
    hops.hop()
    down_arrived = swap(down_oth, "row")
    gate_oth = [
        for_row(tokens_b, pair, True, gate_got, at=i, first=i, count=1) for i in range(2)
    ]
    gate_oth = list(sync([hops], *gate_oth))
    g2_low, sums_b, g2 = norm_back(residual, hops.terms(), cot, gain_b, 1)

    hops = Gather(g2_low, slots)
    gate_arrived = [swap(gate_oth[0], "row"), None]
    part_down = to_features(hidden[None], [p[None] for p in pieces_down], False)
    part_down, down_arrived = sync([hops], part_down, down_arrived)
    hops.hop()
    down_own = for_y(grad_rows, hidden[None], False, down_got, down_arrived)
    down_own, part_down = sync([hops], down_own, part_down)
    hops.hop()
    down_other = y_swap(down_own)
    gate_arrived[0], gate_oth[1] = sync([hops], gate_arrived[0], gate_oth[1])
    gate_arrived[1] = swap(gate_oth[1], "row")
    g2_rows = hops.rows()
    columns = w_out.shape[0] // 2
    grad_other = from_features((1 - core)[None], g2_rows, pieces_out, columns)[0]
    grad_from = swap(grad_other, "core")
    grad_mine = from_features(core[None], g2_rows, pieces_out, columns)[0]
    gate_own = [
        for_y(tokens_b, pair, True, gate_got, gate_arrived[0], at=0, first=0, count=1),
        None,
    ]
    out_sent = for_core(g2_rows, attended[None], False)
    grad_from, grad_mine, out_sent, gate_own[0], part_down, down_other = sync(
        [], grad_from, grad_mine, out_sent, gate_own[0], part_down, down_other
    )
    down_hops = Scatter(part_down, slots)
    gate_other = [y_swap(gate_own[0]), None]
    out_got = swap(out_sent, "core")
    mixed_mine, mixed_other, bias_part = attend_back(
        qkv_mine, qkv_from, grad_mine, grad_from, lse, rotary_mine, rotary_other, table_of, factor
    )
    mixed_mine, mixed_other, out_got, gate_arrived[1] = sync(
        [down_hops], mixed_mine, mixed_other, out_got, gate_arrived[1]
    )
    down_hops.hop()
    mixed_from = swap(mixed_other, "core")
    out_oth = for_row(g2_rows, attended[None], False, out_got)
    gate_own[1] = for_y(tokens_b, pair, True, gate_got, gate_arrived[1], at=1, first=1, count=1)
    mixed = jnp.concatenate(
        [
            jnp.where(core == 0, mixed_mine, mixed_from),
            jnp.where(core == 0, mixed_from, mixed_mine),
        ],
        axis=2,
    )
    in_sent = for_core(tokens_a, mixed, True)
    in_sent, mixed, gate_own[1], gate_other[0], out_oth = sync(
        [], in_sent, mixed, gate_own[1], gate_other[0], out_oth
    )
    in_got = swap(in_sent, "core")
    out_arrived = swap(out_oth, "row")
    gate_other[1] = y_swap(gate_own[1])
    part_a = to_features(mixed, pieces_in, True)
    part_a, in_got, out_arrived = sync([down_hops], part_a, in_got, out_arrived)
    hops = Scatter(part_a, slots)
    spans = (dict(at=0, first=0, count=2), dict(at=2, first=2, count=1))
    in_oth = [for_row(tokens_a, mixed, True, in_got, **span) for span in spans]
    in_arrived = [swap(x, "row") for x in in_oth]
    out_own = for_y(g2_rows, attended[None], False, out_got, out_arrived)
    *in_oth, out_own = sync([hops], *in_oth, out_own)
    hops.hop()
    down_total = y_total(down_own, down_other)
    gate_total = [y_total(gate_own[0], gate_other[0]), None]
    in_arrived[0], gate_other[1], down_total, gate_total[0] = sync(
        [hops], in_arrived[0], gate_other[1], down_total, gate_total[0]
    )
    hops.hop()
    out_other_y = y_swap(out_own)
    in_own = [for_y(tokens_a, mixed, True, in_got, in_arrived[0], **spans[0])]
    gate_total[1] = y_total(gate_own[1], gate_other[1])
    in_own[0], gate_total[1], in_arrived[1], out_other_y = sync(
        [hops], in_own[0], gate_total[1], in_arrived[1], out_other_y
    )
    in_other = [y_swap(in_own[0])]
    input_low, sums_a = norm_back(stream, hops.terms(), g2, gain_a, 0)
    down_rest = swap(down_total, "core")
    gate_rest = [swap(x, "core") for x in gate_total]
    out_total = y_total(out_own, out_other_y)
    out_rest = swap(out_total, "core")
    in_own.append(for_y(tokens_a, mixed, True, in_got, in_arrived[1], **spans[1]))
    input_low, sums_a, in_own[1], down_rest, out_rest, *gate_rest = sync(
        [], input_low, sums_a, in_own[1], down_rest, out_rest, *gate_rest
    )

    bias_all = jnp.zeros((3, 2 * slots * columns), F32)
    bias_all = lax.dynamic_update_slice(
        bias_all, bias_part[:, 0, :], (jnp.int32(0), (place * 2 + core) * columns)
    ).reshape(-1, wide)
    sums = jnp.concatenate([sums_a, sums_b], axis=0)
    own, oth = sums[:, :wide], natural(sums[:, wide:])
    total = jnp.concatenate([own, bias_all, oth], axis=0)

    in_other.append(y_swap(in_own[1]))
    input_grad = from_sequence(input_low)
    down_grad = join(down_total, down_rest, 2)[0]
    if slots == 4:
        arrived = lax.ppermute(total, "col", PAIR)
        arrived, input_grad, down_grad = sync([], arrived, input_grad, down_grad)
        total = total + arrived
        arrived = lax.ppermute(total, "col", MID)
        down_hops.flying = list(tie(down_hops.flying, input_grad))
        down_hops.hop()
        gate_grad = join_pairs(core[None], gate_total, gate_rest)
        arrived, gate_grad, in_other[0] = sync([down_hops], arrived, gate_grad, in_other[0])
        total = total + arrived
        outer = lax.ppermute(total, "col", OUT)
        layer_low = (residual + sum(t.astype(F32) for t in down_hops.terms())).astype(BF16)
        in_total = [y_total(in_own[0], in_other[0])]
        in_rest = [swap(in_total[0], "core")]
        outer, layer_low, in_rest[0] = sync([], outer, layer_low, in_rest[0])
        total = jnp.where((place == 0) | (place == 3), outer, total)
    else:
        gate_grad = join_pairs(core[None], gate_total, gate_rest)
        layer_low = (residual + sum(t.astype(F32) for t in down_hops.terms())).astype(BF16)
        in_total = [y_total(in_own[0], in_other[0])]
        in_rest = [swap(in_total[0], "core")]
        total = lax.psum(total, "col")
    layer_out = from_sequence(layer_low)
    out_grad = join(out_total, out_rest, 2)[0]
    arrived = swap(total, "core")
    arrived, layer_out, in_other[1], out_grad = sync([], arrived, layer_out, in_other[1], out_grad)
    total = total + arrived
    cut = own.shape[0] + bias_all.shape[0]
    sent = jnp.concatenate([total[cut:], total[own.shape[0] : cut]], axis=0)
    total = total[:cut] + swap(sent, "row")
    vectors = lax.psum(total, "y") if y_count != 2 else total + swap(total, "y")
    bias_grad = take(vectors[4:].reshape(3, -1), place * 2 * columns, 2 * columns, 1)
    input_grad = input_grad.astype(F32)
    in_total.append(y_total(in_own[1], in_other[1]))
    in_rest.append(swap(in_total[1], "core"))
    in_grad = jnp.concatenate([join(x, r, 1) for x, r in zip(in_total, in_rest)], axis=0)
    return (
        layer_out[None],
        input_grad,
        vectors[0:1],
        vectors[1:2],
        jnp.transpose(in_grad, (1, 0, 2))[None],
        bias_grad[None],
        out_grad[None],
        vectors[2:3],
        vectors[3:4],
        gate_grad[None],
        down_grad[None],
    )


def solution(mesh):
    dp, rows, cols = (mesh.shape[a] for a in ("dp", "row", "col"))
    split = Mesh(mesh.devices.reshape(dp // 2, 2, rows, cols), ("y", "core", "row", "col"))
    tokens = ("y", "core", "col")
    return jax.shard_map(
        local,
        mesh=split,
        in_specs=(
            P(tokens, "row"),
            P(None, "row"),
            P(None, "row"),
            P(None, "row", None, "col"),
            P(None, None, "col"),
            P(None, "col", "row"),
            P(None, "row"),
            P(None, "row"),
            P(None, "row", None, "col"),
            P(None, "col", "row"),
            P(tokens, "row"),
        ),
        out_specs=(
            P(None, tokens, "row"),
            P(tokens, "row"),
            P(None, "row"),
            P(None, "row"),
            P(None, "row", None, "col"),
            P(None, None, "col"),
            P(None, "col", "row"),
            P(None, "row"),
            P(None, "row"),
            P(None, "row", None, "col"),
            P(None, "col", "row"),
        ),
        check_vma=False,
    )
```

```python
import functools
import math

import jax
import jax.numpy as jnp
from jax import lax
from jax.experimental import pallas as pl
from jax.experimental.pallas import tpu as pltpu
from jax.sharding import Mesh
from jax.sharding import PartitionSpec as P

HEAD_DIM = 64
ROT = 16
LENGTH = 1024
EPSILON = 1e-05
F32 = jnp.float32
BF16 = jnp.bfloat16
LANES = 128
MIB = 1 << 20


def swap(x, axis):
    return lax.ppermute(x, axis, [(0, 1), (1, 0)])


PAIR = [(0, 1), (1, 0), (2, 3), (3, 2)]
MID = [(1, 2), (2, 1)]
OUT = [(1, 0), (2, 3)]
IN = [(0, 1), (3, 2)]
ORDER4 = ((0, 1, 2, 3), (1, 0, 2, 3), (2, 3, 1, 0), (3, 2, 1, 0))


def slot_order(place, count):
    if count == 4:
        return jnp.array(ORDER4, jnp.int32)[place]
    return jnp.arange(count, dtype=jnp.int32)


def tie(values, *behind):
    return lax.optimization_barrier((tuple(values), behind))[0]


def after(x, *behind):
    return tie((x,), *behind)[0] if behind else x


class Gather:
    def __init__(self, own, count):
        self.own, self.count, self.got = own, count, []
        self.flying = []
        if count == 4:
            self.flying = [lax.ppermute(own, "col", PAIR), lax.ppermute(own, "col", MID)]

    def hop(self):
        if self.count != 4:
            return
        if not self.got:
            one, mid = self.flying
            self.got = [one, mid]
            self.flying = [lax.ppermute(one, "col", MID), lax.ppermute(mid, "col", OUT)]
        else:
            far, mid_out = self.flying
            self.got += [far, mid_out]
            self.flying = [lax.ppermute(far, "col", OUT)]

    def rows(self):
        if self.count != 4:
            return lax.all_gather(self.own, "col", axis=0, tiled=True)
        one, mid, far, mid_out = self.got
        return jnp.concatenate([self.own, one, mid + mid_out, far + self.flying[0]], axis=0)


class Scatter:
    def __init__(self, parts, count):
        self.count, self.step, self.parts = count, 0, parts
        self.flying, self.two = [], None
        if count == 4:
            rows = parts.shape[0] // count
            self.part = [parts[i * rows : (i + 1) * rows] for i in range(4)]
            self.flying = [lax.ppermute(self.part[3], "col", IN)]
            self.two = lax.ppermute(self.part[2], "col", IN)

    def hop(self):
        if self.count != 4:
            return
        if self.step == 0:
            three = self.part[3] + self.flying[0]
            self.flying = [lax.ppermute(three, "col", MID), self.two]
        else:
            one, two = self.part[1] + self.flying[0], self.part[2] + self.flying[1]
            self.flying = [lax.ppermute(one, "col", PAIR), lax.ppermute(two, "col", MID)]
        self.step += 1

    def terms(self):
        if self.count != 4:
            mine = lax.psum_scatter(self.parts, "col", scatter_dimension=0, tiled=True)
            return (mine, jnp.zeros_like(mine), jnp.zeros_like(mine))
        return (self.part[0], *self.flying)


def sync(moving, *values):
    flat = [x for m in moving for x in m.flying] + list(values)
    flat = list(lax.optimization_barrier(tuple(flat)))
    for m in moving:
        count = len(m.flying)
        m.flying, flat = flat[:count], flat[count:]
    return flat[0] if len(flat) == 1 else flat


def params(mib, axes=1):
    return pltpu.CompilerParams(
        vmem_limit_bytes=mib * MIB, dimension_semantics=("arbitrary",) * axes
    )


SHARE = 8


def cost(flops, moved, trans=0):
    return pl.CostEstimate(
        flops=int(flops / SHARE),
        bytes_accessed=int(moved / SHARE),
        transcendentals=int(trans / SHARE),
    )


def stats_of(value):
    width = value.shape[1]
    average = jnp.sum(value, axis=1, keepdims=True) / width
    centred = value - average
    variance = jnp.sum(centred * centred, axis=1, keepdims=True) / width
    inv_root = lax.rsqrt(variance + EPSILON)
    return centred * inv_root, inv_root


def norm_first(stream, gain, shift):
    rows, width = stream.shape
    block = rows // 4

    def body(x_ref, gain_ref, shift_ref, low_ref):
        xhat, unused = stats_of(x_ref[...].astype(F32))
        low_ref[...] = (xhat * gain_ref[...] + shift_ref[...]).astype(BF16)

    row = pl.BlockSpec((block, width), lambda i: (i, 0))
    flat = pl.BlockSpec((1, width), lambda i: (0, 0))
    return pl.pallas_call(
        body,
        grid=(4,),
        in_specs=[row, flat, flat],
        out_specs=row,
        out_shape=jax.ShapeDtypeStruct((rows, width), BF16),
        compiler_params=params(6),
        cost_estimate=cost(rows * width * 10, rows * width * 4),
        name="norm_first",
    )(stream, gain, shift)


def norm_second(stream, terms, gain, shift):
    rows, width = stream.shape
    block = rows // 4

    def body(x_ref, a_ref, b_ref, c_ref, gain_ref, shift_ref, res_ref, low_ref):
        residual = (
            x_ref[...].astype(F32)
            + a_ref[...].astype(F32)
            + b_ref[...].astype(F32)
            + c_ref[...].astype(F32)
        )
        res_ref[...] = residual
        xhat, unused = stats_of(residual)
        low_ref[...] = (xhat * gain_ref[...] + shift_ref[...]).astype(BF16)

    row = pl.BlockSpec((block, width), lambda i: (i, 0))
    flat = pl.BlockSpec((1, width), lambda i: (0, 0))
    return pl.pallas_call(
        body,
        grid=(4,),
        in_specs=[row] * 4 + [flat, flat],
        out_specs=[row, row],
        out_shape=[
            jax.ShapeDtypeStruct((rows, width), F32),
            jax.ShapeDtypeStruct((rows, width), BF16),
        ],
        compiler_params=params(6),
        cost_estimate=cost(rows * width * 12, rows * width * 14),
        name="norm_second",
    )(stream, *terms, gain, shift)


def norm_back(stream, terms, upper, gain, both):
    rows, width = stream.shape
    block = rows // 4

    def body(x_ref, a_ref, b_ref, c_ref, up_ref, gain_ref, low_ref, sums_ref, *full_ref):
        xhat, inv_root = stats_of(x_ref[...].astype(F32))
        grad = a_ref[...].astype(F32) + b_ref[...].astype(F32) + c_ref[...].astype(F32)
        scaled = grad * gain_ref[...]
        mean_scaled = jnp.sum(scaled, axis=1, keepdims=True) / width
        mean_cross = jnp.sum(scaled * xhat, axis=1, keepdims=True) / width
        result = up_ref[...].astype(F32) + inv_root * (scaled - mean_scaled - xhat * mean_cross)
        low_ref[...] = result.astype(BF16)
        if full_ref:
            full_ref[0][...] = result

        @pl.when(pl.program_id(0) == 0)
        def _():
            sums_ref[...] = jnp.zeros_like(sums_ref)

        sums_ref[...] += jnp.concatenate(
            [
                jnp.sum(grad * xhat, axis=0, keepdims=True),
                jnp.sum(grad, axis=0, keepdims=True),
            ],
            axis=0,
        )

    row = pl.BlockSpec((block, width), lambda i: (i, 0))
    flat = pl.BlockSpec((1, width), lambda i: (0, 0))
    sums = pl.BlockSpec((2, width), lambda i: (0, 0))
    return pl.pallas_call(
        body,
        grid=(4,),
        in_specs=[row] * 5 + [flat],
        out_specs=[row, sums] + [row] * both,
        out_shape=[
            jax.ShapeDtypeStruct((rows, width), BF16),
            jax.ShapeDtypeStruct((2, width), F32),
        ]
        + [jax.ShapeDtypeStruct((rows, width), F32)] * both,
        compiler_params=params(10),
        cost_estimate=cost(rows * width * 20, rows * width * 18),
        name="norm_back",
    )(stream, *terms, upper, gain)


def cuts_of(sizes):
    ends = [sum(sizes[: i + 1]) for i in range(len(sizes))]
    return [(end - size, end) for end, size in zip(ends, sizes)]


def roll_lanes(value, shift):
    return pltpu.roll(value, shift % value.shape[1], 1)


def turn(value, table, sign):
    times = value.shape[1] // LANES
    wide = [jnp.concatenate([table[i]] * times, axis=1) for i in range(3)]
    ahead = roll_lanes(value, -(ROT // 2))
    behind = roll_lanes(value, ROT // 2)
    moved = ahead * wide[1] + behind * wide[2]
    return value * wide[0] + (moved if sign > 0 else -moved)


def qkv_columns(tokens, pieces, bias, table, half):
    rows, width = tokens.shape
    columns = pieces[0].shape[2] // 2
    cuts = cuts_of([p.shape[1] for p in pieces])

    def body(half_ref, x_ref, *refs):
        bias_ref, table_ref, out_ref = refs[-3:]
        which = pl.program_id(0)
        acc = bias_ref[0]
        for w_ref, (low, high) in zip(refs, cuts):
            acc = acc + jnp.dot(x_ref[:, low:high], w_ref[0], preferred_element_type=F32)

        @pl.when(which < 2)
        def _():
            out_ref[0] = turn(acc, table_ref, 1).astype(BF16)

        @pl.when(which == 2)
        def _():
            out_ref[0] = acc.astype(BF16)

    return pl.pallas_call(
        body,
        grid_spec=pltpu.PrefetchScalarGridSpec(
            num_scalar_prefetch=1,
            grid=(3,),
            in_specs=[pl.BlockSpec((rows, width), lambda j, h: (0, 0))]
            + [pl.BlockSpec((1, p.shape[1], columns), lambda j, h: (j, 0, h[0])) for p in pieces]
            + [
                pl.BlockSpec((1, 1, columns), lambda j, h: (j, 0, h[0])),
                pl.BlockSpec((3, rows, LANES), lambda j, h: (0, 0, 0)),
            ],
            out_specs=pl.BlockSpec((1, rows, columns), lambda j, h: (j, 0, 0)),
        ),
        out_shape=jax.ShapeDtypeStruct((3, rows, columns), BF16),
        compiler_params=params(16),
        cost_estimate=cost(6 * rows * width * columns, 2 * (rows * width + 3 * columns * width)),
        name="qkv_columns",
    )(half, tokens, *pieces, bias, table)


def place_of(order_ref, slot, core, rows):
    return pl.multiple_of((order_ref[1 + slot] * 2 + core) * rows, rows)


CHUNK = 256


def score_chunk(query, key, first):
    scores = lax.dot_general(query, key, (((1,), (1,)), ((), ())), preferred_element_type=F32)
    last = scores[:, first:]
    at_query = lax.broadcasted_iota(jnp.int32, last.shape, 0)
    at_key = lax.broadcasted_iota(jnp.int32, last.shape, 1)
    last = jnp.where(at_query >= at_key, last, -jnp.inf)
    return last if first == 0 else jnp.concatenate([scores[:, :first], last], axis=1)


def attend(mine, other, order, factor):
    unused, rows, columns = mine.shape
    slots = order.shape[0] - 1
    piece = rows // slots
    length = 2 * rows

    def body(order_ref, mine_ref, other_ref, out_mine, out_other, lse_ref, whole, result):
        core = order_ref[0]
        for slot in range(slots):
            here = slice(slot * piece, (slot + 1) * piece)
            whole[:, pl.ds(place_of(order_ref, slot, core, piece), piece), :] = mine_ref[:, here, :]
            whole[:, pl.ds(place_of(order_ref, slot, 1 - core, piece), piece), :] = other_ref[
                :, here, :
            ]
        for head in range(LANES // HEAD_DIM):
            lanes = slice(head * HEAD_DIM, (head + 1) * HEAD_DIM)
            for first in range(0, length, CHUNK):
                upto = first + CHUNK
                query = whole[0, first:upto, lanes] * jnp.bfloat16(factor)
                scores = score_chunk(query, whole[1, :upto, lanes], first)
                highest = jnp.max(scores, axis=1, keepdims=True)
                exponent = jnp.exp(scores - highest)
                summed = jnp.sum(exponent, axis=1, keepdims=True)
                mixed = jnp.dot(
                    exponent.astype(BF16), whole[2, :upto, lanes], preferred_element_type=F32
                )
                result[first:upto, lanes] = (mixed * (1.0 / summed)).astype(BF16)
                lse_ref[0, first:upto, head : head + 1] = highest + jnp.log(summed)
        for slot in range(slots):
            here = slice(slot * piece, (slot + 1) * piece)
            out_mine[here, :] = result[pl.ds(place_of(order_ref, slot, core, piece), piece), :]
            out_other[here, :] = result[pl.ds(place_of(order_ref, slot, 1 - core, piece), piece), :]

    groups = columns // LANES
    three = pl.BlockSpec((3, rows, LANES), lambda g, o: (0, 0, g))
    one = pl.BlockSpec((rows, LANES), lambda g, o: (0, g))
    return pl.pallas_call(
        body,
        grid_spec=pltpu.PrefetchScalarGridSpec(
            num_scalar_prefetch=1,
            grid=(groups,),
            in_specs=[three, three],
            out_specs=[one, one, pl.BlockSpec((1, length, 2), lambda g, o: (g, 0, 0))],
            scratch_shapes=[
                pltpu.VMEM((3, length, LANES), BF16),
                pltpu.VMEM((length, LANES), BF16),
            ],
        ),
        out_shape=[
            jax.ShapeDtypeStruct((rows, columns), BF16),
            jax.ShapeDtypeStruct((rows, columns), BF16),
            jax.ShapeDtypeStruct((groups, length, 2), F32),
        ],
        compiler_params=params(20),
        cost_estimate=cost(
            4 * length * length * columns, 16 * rows * columns, columns * length * length / 128
        ),
        name="attend",
    )(order, mine, other)


def attend_back(mine, other, grad_mine, grad_other, lse, table_mine, table_other, order, factor):
    unused, rows, columns = mine.shape
    slots = order.shape[0] - 1
    piece = rows // slots
    length = 2 * rows
    across = (((1,), (1,)), ((), ()))
    down = (((0,), (0,)), ((), ()))

    def body(
        order_ref,
        mine_ref,
        other_ref,
        gm_ref,
        go_ref,
        lse_ref,
        tm_ref,
        to_ref,
        out_mine,
        out_other,
        bias_ref,
        whole,
        grads,
        dq_ref,
        dkv_ref,
    ):
        core = order_ref[0]
        for slot in range(slots):
            here = slice(slot * piece, (slot + 1) * piece)
            one = pl.ds(place_of(order_ref, slot, core, piece), piece)
            two = pl.ds(place_of(order_ref, slot, 1 - core, piece), piece)
            whole[:, one, :] = mine_ref[:, here, :]
            whole[:, two, :] = other_ref[:, here, :]
            grads[one, :] = gm_ref[here, :]
            grads[two, :] = go_ref[here, :]
        heads = LANES // HEAD_DIM
        for head in range(heads):
            lanes = slice(head * HEAD_DIM, (head + 1) * HEAD_DIM)
            for first in reversed(range(0, length, CHUNK)):
                upto = first + CHUNK
                query = whole[0, first:upto, lanes] * jnp.bfloat16(factor)
                key = whole[1, :upto, lanes]
                value = whole[2, :upto, lanes]
                grad = grads[first:upto, lanes]
                scores = score_chunk(query, key, first)
                probs = jnp.exp(scores - lse_ref[0, first:upto, head : head + 1])
                probs_grad = lax.dot_general(grad, value, across, preferred_element_type=F32)
                shift = jnp.sum(probs * probs_grad, axis=1, keepdims=True)
                scores_grad = (probs * (probs_grad - shift)).astype(BF16)
                dq_ref[first:upto, lanes] = (
                    jnp.dot(scores_grad, key, preferred_element_type=F32) * factor
                )
                dk = lax.dot_general(scores_grad, query, down, preferred_element_type=F32)
                dv = lax.dot_general(
                    probs.astype(BF16), grad, down, preferred_element_type=F32
                )
                if upto == length:
                    dkv_ref[0, :, lanes] = dk
                    dkv_ref[1, :, lanes] = dv
                else:
                    dkv_ref[0, :upto, lanes] += dk
                    dkv_ref[1, :upto, lanes] += dv
        total = [jnp.zeros((1, LANES), F32) for _ in range(3)]
        for slot in range(slots):
            here = slice(slot * piece, (slot + 1) * piece)
            for at, table, out in (
                (core, tm_ref, out_mine),
                (1 - core, to_ref, out_other),
            ):
                rows_at = pl.ds(place_of(order_ref, slot, at, piece), piece)
                angles = table[:, here, :]
                parts = (
                    turn(dq_ref[rows_at, :], angles, -1).astype(BF16),
                    turn(dkv_ref[0, rows_at, :], angles, -1).astype(BF16),
                    dkv_ref[1, rows_at, :].astype(BF16),
                )
                for i in range(3):
                    out[i, here, :] = parts[i]
                    total[i] += jnp.sum(parts[i].astype(F32), axis=0, keepdims=True)
        for i in range(3):
            bias_ref[i] = total[i]

    groups = columns // LANES
    three = pl.BlockSpec((3, rows, LANES), lambda g, o: (0, 0, g))
    one = pl.BlockSpec((rows, LANES), lambda g, o: (0, g))
    full = pl.BlockSpec((3, rows, LANES), lambda g, o: (0, 0, 0))
    return pl.pallas_call(
        body,
        grid_spec=pltpu.PrefetchScalarGridSpec(
            num_scalar_prefetch=1,
            grid=(groups,),
            in_specs=[
                three,
                three,
                one,
                one,
                pl.BlockSpec((1, length, 2), lambda g, o: (g, 0, 0)),
                full,
                full,
            ],
            out_specs=[three, three, pl.BlockSpec((3, 1, LANES), lambda g, o: (0, 0, g))],
            scratch_shapes=[
                pltpu.VMEM((3, length, LANES), BF16),
                pltpu.VMEM((length, LANES), BF16),
                pltpu.VMEM((length, LANES), F32),
                pltpu.VMEM((2, length, LANES), F32),
            ],
        ),
        out_shape=[
            jax.ShapeDtypeStruct((3, rows, columns), BF16),
            jax.ShapeDtypeStruct((3, rows, columns), BF16),
            jax.ShapeDtypeStruct((3, 1, columns), F32),
        ],
        compiler_params=params(20),
        cost_estimate=cost(
            10 * length * length * columns, 40 * rows * columns, columns * length * length / 128
        ),
        name="attend_back",
    )(order, mine, other, grad_mine, grad_other, lse, table_mine, table_other)


ACROSS = (((1,), (1,)), ((), ()))
DOWN = (((0,), (0,)), ((), ()))


def feed_forward(tokens, pieces, hidden_grad):
    rows, width = tokens.shape
    units = pieces[0].shape[2]
    block = 256 if units > 256 else units
    cuts = cuts_of([p.shape[1] for p in pieces])

    def body(x_ref, *refs):
        hg_ref, hidden_ref, grad_ref = refs[-3:]
        gate_up = 0.0
        for w_ref, (low, high) in zip(refs, cuts):
            both = jnp.concatenate([w_ref[0], w_ref[1]], axis=1)
            gate_up += jnp.dot(x_ref[:, low:high], both, preferred_element_type=F32)
        gate, up = gate_up[:, :block], gate_up[:, block:]
        sigma = jax.nn.sigmoid(gate)
        silu = gate * sigma
        hidden_ref[...] = (silu * up).astype(BF16)
        grad = hg_ref[...].astype(F32)
        grad_ref[0] = (grad * up * (sigma + silu * (1.0 - sigma))).astype(BF16)
        grad_ref[1] = (grad * silu).astype(BF16)

    return pl.pallas_call(
        body,
        grid=(pl.cdiv(units, block),),
        in_specs=[pl.BlockSpec((rows, width), lambda j: (0, 0))]
        + [pl.BlockSpec((2, p.shape[1], block), lambda j: (0, 0, j)) for p in pieces]
        + [pl.BlockSpec((rows, block), lambda j: (0, j))],
        out_specs=[
            pl.BlockSpec((rows, block), lambda j: (0, j)),
            pl.BlockSpec((2, rows, block), lambda j: (0, 0, j)),
        ],
        out_shape=[
            jax.ShapeDtypeStruct((rows, units), BF16),
            jax.ShapeDtypeStruct((2, rows, units), BF16),
        ],
        compiler_params=params(20),
        cost_estimate=cost(
            4 * rows * width * units, 4 * width * units + 2 * rows * width, rows * units
        ),
        name="feed_forward",
    )(tokens, *pieces, hidden_grad)


def to_features(values, pieces, across):
    count, rows, units = values.shape
    axis = 1 if across else 2
    sizes = [p.shape[axis] for p in pieces]
    block = sizes[-1]
    width = sum(sizes)
    owner = [i for i, size in enumerate(sizes) for _ in range(size // block)]
    starts = [owner.index(i) for i in range(len(pieces))]
    dims = ACROSS if across else (((1,), (0,)), ((), ()))

    def body(v_ref, *refs):
        step = pl.program_id(0)
        for i, w_ref in enumerate(refs[:-1]):

            @pl.when((step >= starts[i]) & (step < starts[i] + sizes[i] // block))
            def _():
                total = 0.0
                for n in range(count):
                    total += lax.dot_general(v_ref[n], w_ref[n], dims, preferred_element_type=F32)
                refs[-1][...] = total.astype(BF16)

    def spec(i):
        last = sizes[i] // block - 1
        at = lambda j: jnp.clip(j - starts[i], 0, last)
        if across:
            return pl.BlockSpec((count, block, units), lambda j: (0, at(j), 0))
        return pl.BlockSpec((count, units, block), lambda j: (0, 0, at(j)))

    return pl.pallas_call(
        body,
        grid=(width // block,),
        in_specs=[pl.BlockSpec((count, rows, units), lambda j: (0, 0, 0))]
        + [spec(i) for i in range(len(pieces))],
        out_specs=pl.BlockSpec((rows, block), lambda j: (0, j)),
        out_shape=jax.ShapeDtypeStruct((rows, width), BF16),
        compiler_params=params(32),
        cost_estimate=cost(
            2 * count * rows * width * units, 2 * count * (width + rows) * units + 2 * rows * width
        ),
        name="to_features",
    )(values, *pieces)


def from_features(index, tokens, pieces, block):
    rows, width = tokens.shape
    cuts = cuts_of([p.shape[1] for p in pieces])
    count = index.shape[0]

    def body(index_ref, x_ref, *refs):
        total = 0.0
        for w_ref, (low, high) in zip(refs, cuts):
            total += lax.dot_general(
                x_ref[:, low:high], w_ref[...], ACROSS, preferred_element_type=F32
            )
        refs[-1][0] = total.astype(BF16)

    out = pl.pallas_call(
        body,
        grid_spec=pltpu.PrefetchScalarGridSpec(
            num_scalar_prefetch=1,
            grid=(count,),
            in_specs=[pl.BlockSpec((rows, width), lambda j, q: (0, 0))]
            + [pl.BlockSpec((block, p.shape[1]), lambda j, q: (q[j], 0)) for p in pieces],
            out_specs=pl.BlockSpec((1, rows, block), lambda j, q: (j, 0, 0)),
        ),
        out_shape=jax.ShapeDtypeStruct((count, rows, block), BF16),
        compiler_params=params(16),
        cost_estimate=cost(
            2 * rows * width * block * count, 2 * width * (rows + block * count)
        ),
        name="from_features",
    )(index, tokens, *pieces)
    return out


def grad_quarters(quarters, tokens, others, adds, rows_first, first=0, count=None):
    rows, width = tokens.shape
    units = others.shape[2]
    count = others.shape[0] if count is None else count
    quarter = width // 4
    k = quarters.shape[0]
    form = (quarter, units) if rows_first else (units, quarter)

    def body(q_ref, x_ref, y_ref, *refs):
        x, y = x_ref[...], y_ref[0]
        left, right = (x, y) if rows_first else (y, x)
        total = lax.dot_general(left, right, DOWN, preferred_element_type=F32)
        for ref in refs[:-1]:
            total += ref[0, 0].astype(F32)
        refs[-1][0, 0] = total.astype(BF16)

    def shifted(at_k, at_n):
        return pl.BlockSpec((1, 1, *form), lambda i, j, q: (i + at_k, j + at_n, 0, 0))

    return pl.pallas_call(
        body,
        grid_spec=pltpu.PrefetchScalarGridSpec(
            num_scalar_prefetch=1,
            grid=(k, count),
            in_specs=[
                pl.BlockSpec((rows, quarter), lambda i, j, q: (0, q[i])),
                pl.BlockSpec((1, rows, units), lambda i, j, q: (j + first, 0, 0)),
            ]
            + [shifted(at_k, at_n) for unused, at_k, at_n in adds],
            out_specs=shifted(0, 0),
        ),
        out_shape=jax.ShapeDtypeStruct((k, count, *form), BF16),
        compiler_params=params(20, 2),
        cost_estimate=cost(
            2 * k * count * rows * quarter * units,
            2 * k * count * quarter * units * (1 + len(adds)) + 2 * rows * (width + count * units),
        ),
        name="grad_quarters",
    )(quarters, tokens, others, *[add[0] for add in adds])


def join_pairs(core, parts, rests):
    rows, units = parts[0].shape[1:]
    block = 128 if rows % 128 == 0 else rows
    steps = rows // block

    def body(core_ref, *refs):
        half = pl.program_id(0)
        out_ref = refs[-1]
        for i in range(2):

            @pl.when(half == core_ref[0])
            def _():
                out_ref[:, i, :] = refs[i][0].astype(F32)

            @pl.when(half != core_ref[0])
            def _():
                out_ref[:, i, :] = refs[2 + i][0].astype(F32)

    def spec(same):
        def at(h, j, c):
            wanted = (h == c[0]) if same else (h != c[0])
            return (0, jnp.where(wanted, j, 0), 0)

        return pl.BlockSpec((1, block, units), at)

    return pl.pallas_call(
        body,
        grid_spec=pltpu.PrefetchScalarGridSpec(
            num_scalar_prefetch=1,
            grid=(2, steps),
            in_specs=[spec(True), spec(True), spec(False), spec(False)],
            out_specs=pl.BlockSpec((block, 2, units), lambda h, j, c: (h * steps + j, 0, 0)),
        ),
        out_shape=jax.ShapeDtypeStruct((2 * rows, 2, units), F32),
        compiler_params=params(16, 2),
        cost_estimate=cost(rows * units, 24 * rows * units),
        name="join_pairs",
    )(core, *parts, *rests)


def rotary_table(position):
    half = ROT // 2
    lane = jnp.arange(LANES) % HEAD_DIM
    frequency = 10000.0 ** (-((lane % half).astype(F32) * 2.0 / ROT))
    angles = position.astype(F32)[:, None] * frequency[None, :]
    lane = lane[None, :]
    cosine = jnp.where(lane < ROT, jnp.cos(angles), 1.0)
    sine = jnp.sin(angles)
    return jnp.stack(
        [
            cosine,
            jnp.where(lane < half, -sine, 0.0),
            jnp.where((lane >= half) & (lane < ROT), sine, 0.0),
        ]
    )


def local(
    inputs,
    first_gain,
    first_shift,
    project_in,
    project_bias,
    project_out,
    second_gain,
    second_shift,
    gate_weight,
    down_weight,
    cotangent,
):
    y_count = lax.axis_size("y")
    slots = lax.axis_size("col")
    y = lax.axis_index("y")
    core = lax.axis_index("core")
    row = lax.axis_index("row")
    place = lax.axis_index("col")
    factor = 1.0 / math.sqrt(HEAD_DIM)
    half_rows = inputs.shape[0] // 2
    wide = inputs.shape[1]
    width = 2 * wide

    def take(x, start, size, axis):
        return lax.dynamic_slice_in_dim(x, start, size, axis)

    straight = [(0, 0), (1, 2), (2, 1), (3, 3)]
    crossed = [(0, 2), (1, 0), (2, 3), (3, 1)]
    aligned = core == row

    def order_features(own, oth):
        low, high = oth[..., : wide // 2], oth[..., wide // 2 :]
        return jnp.concatenate(
            [own, jnp.where(core == 0, low, high), jnp.where(core == 0, high, low)], axis=-1
        )

    def natural(oth):
        low, high = oth[..., : wide // 2], oth[..., wide // 2 :]
        return jnp.concatenate(
            [jnp.where(core == 0, low, high), jnp.where(core == 0, high, low)], axis=-1
        )

    def to_sequence(x):
        a = lax.ppermute(take(x, row * half_rows, half_rows, 0), ("core", "row"), straight)
        b = lax.ppermute(take(x, (1 - row) * half_rows, half_rows, 0), ("core", "row"), crossed)
        return order_features(jnp.where(aligned, a, b), jnp.where(aligned, b, a))

    def from_sequence(x):
        own, oth = x[:, :wide], natural(x[:, wide:])
        a = jnp.where(aligned, own, oth)
        b = jnp.where(aligned, oth, own)
        a = lax.ppermute(a, ("core", "row"), [(j, i) for i, j in straight])
        b = lax.ppermute(b, ("core", "row"), [(j, i) for i, j in crossed])
        top = jnp.where(row == 0, a, b)
        bottom = jnp.where(row == 0, b, a)
        return jnp.concatenate([top, bottom], axis=0)

    order = slot_order(place, slots)
    table_of = jnp.concatenate([core[None], order]).astype(jnp.int32)
    inside = jnp.arange(half_rows)
    position = lambda c: ((order[:, None] * 2 + c) * half_rows + inside[None, :]).reshape(-1)
    rotary_mine = rotary_table(position(core))
    rotary_other = rotary_table(position(1 - core))

    stream = to_sequence(inputs)
    vectors = jnp.concatenate([first_gain, first_shift, second_gain, second_shift], axis=0)
    vectors = order_features(vectors, swap(vectors, "row"))
    gain_a, shift_a, gain_b, shift_b = (vectors[i : i + 1] for i in range(4))

    def part_of(w, axis):
        part = w.shape[axis] // 2
        return take(w, core * part, part, axis)

    w_in = jnp.transpose(project_in[0], (1, 0, 2))
    w_out, w_down = project_out[0], down_weight[0]
    w_gate = jnp.transpose(gate_weight[0], (1, 0, 2))
    fixed = 0 * core

    def quarters(*q):
        return jnp.stack(q).astype(jnp.int32)

    def for_core(tokens, others, rows_first, **span):
        return grad_quarters(quarters(1 - core, 3 + fixed), tokens, others, (), rows_first, **span)

    def for_row(tokens, others, rows_first, got, at=0, **span):
        return grad_quarters(
            quarters(2 + fixed), tokens, others, ((got, 1, at),), rows_first, **span
        )

    def for_y(tokens, others, rows_first, got, arrived, at=0, **span):
        adds = ((got, 0, at), (arrived, 0, 0))
        return grad_quarters(quarters(core), tokens, others, adds, rows_first, **span)[0]

    def y_swap(own):
        return swap(own, "y") if y_count == 2 else lax.psum(own, "y")

    def y_total(own, other):
        return (own.astype(F32) + other.astype(F32)).astype(BF16) if y_count == 2 else other

    def join(total, rest, axis):
        return jnp.concatenate(
            [jnp.where(core == 0, total, rest), jnp.where(core == 0, rest, total)], axis=axis
        ).astype(F32)

    low_a = norm_first(stream, gain_a, shift_a)
    in_half = swap(after(part_of(w_in, 1), stream), "row")
    cot = to_sequence(after(cotangent, low_a))
    hops = Gather(low_a, slots)
    rotary_mine = sync([hops], rotary_mine)
    hops.hop()
    rotary_other, out_part, down_part = sync(
        [hops], rotary_other, part_of(w_out, 1), part_of(w_down, 1)
    )
    hops.hop()
    out_half = swap(out_part, "row")
    w_gate, gate_part, in_half, cot = sync([hops], w_gate, part_of(w_gate, 1), in_half, cot)
    tokens_a = hops.rows()
    pieces_in = (w_in, in_half, swap(in_half, "core"))
    cot_hops = Gather(cot, slots)
    down_half = swap(after(down_part, cot), "row")
    bias = project_bias[0][:, None, :]
    qkv_other = qkv_columns(tokens_a, pieces_in, bias, rotary_mine, (1 - core)[None])
    qkv_from = swap(qkv_other, "core")
    qkv_mine = qkv_columns(tokens_a, pieces_in, bias, rotary_mine, core[None])
    out_mine, out_other, lse = attend(qkv_mine, qkv_from, table_of, factor)
    out_mine, out_other, out_half = sync([cot_hops], out_mine, out_other, out_half)
    cot_hops.hop()
    pieces_out = (w_out, out_half, swap(out_half, "core"))
    out_from = swap(out_other, "core")
    attended = jnp.concatenate(
        [jnp.where(core == 0, out_mine, out_from), jnp.where(core == 0, out_from, out_mine)], axis=1
    )
    part_out = to_features(attended[None], [p[None] for p in pieces_out], False)
    part_out, gate_part = sync([], part_out, gate_part)
    hops = Scatter(part_out, slots)
    down_half = sync([hops, cot_hops], down_half)
    hops.hop()
    cot_hops.hop()
    gate_half = swap(after(gate_part, down_half), "row")
    down_rest = sync([hops, cot_hops], swap(down_half, "core"))
    hops.hop()
    pieces_down = (w_down, down_half, down_rest)
    units = w_down.shape[0]
    ways = 2 if units % 32 == 0 else 1
    grad_rows = cot_hops.rows()
    hidden_grad = from_features(
        jnp.arange(ways, dtype=jnp.int32), grad_rows, pieces_down, units // ways
    )
    hidden_grad = jnp.concatenate([hidden_grad[i] for i in range(ways)], axis=1)
    grad_rows, hidden_grad = sync([hops], grad_rows, hidden_grad)
    residual, low_b = norm_second(stream, hops.terms(), gain_b, shift_b)

    hops = Gather(low_b, slots)
    sync([hops], low_b)
    hops.hop()
    gate_half = sync([hops], gate_half)
    hops.hop()
    gate_half, gate_rest = sync([hops], gate_half, swap(gate_half, "core"))
    tokens_b = hops.rows()
    pieces_gate = (w_gate, gate_half, gate_rest)
    hidden, pair = feed_forward(tokens_b, pieces_gate, hidden_grad)
    part_b = to_features(pair, pieces_gate, True)
    part_b, hidden, pair = sync([], part_b, hidden, pair)

    hops = Scatter(part_b, slots)
    down_sent = for_core(grad_rows, hidden[None], False)
    gate_sent = for_core(tokens_b, pair, True)
    down_sent, gate_sent = sync([hops], down_sent, gate_sent)
    hops.hop()
    down_got = swap(down_sent, "core")
    gate_got = swap(gate_sent, "core")
    down_oth = for_row(grad_rows, hidden[None], False, down_got)
    down_oth, gate_got = sync([hops], down_oth, gate_got)
    hops.hop()
    down_arrived = swap(down_oth, "row")
    gate_oth = [
        for_row(tokens_b, pair, True, gate_got, at=i, first=i, count=1) for i in range(2)
    ]
    gate_oth = list(sync([hops], *gate_oth))
    g2_low, sums_b, g2 = norm_back(residual, hops.terms(), cot, gain_b, 1)

    hops = Gather(g2_low, slots)
    gate_arrived = [swap(gate_oth[0], "row"), None]
    part_down = to_features(hidden[None], [p[None] for p in pieces_down], False)
    part_down, down_arrived = sync([hops], part_down, down_arrived)
    hops.hop()
    down_own = for_y(grad_rows, hidden[None], False, down_got, down_arrived)
    down_own, part_down = sync([hops], down_own, part_down)
    hops.hop()
    down_other = y_swap(down_own)
    gate_arrived[0], gate_oth[1] = sync([hops], gate_arrived[0], gate_oth[1])
    gate_arrived[1] = swap(gate_oth[1], "row")
    g2_rows = hops.rows()
    columns = w_out.shape[0] // 2
    grad_other = from_features((1 - core)[None], g2_rows, pieces_out, columns)[0]
    grad_from = swap(grad_other, "core")
    grad_mine = from_features(core[None], g2_rows, pieces_out, columns)[0]
    gate_own = [
        for_y(tokens_b, pair, True, gate_got, gate_arrived[0], at=0, first=0, count=1),
        None,
    ]
    out_sent = for_core(g2_rows, attended[None], False)
    grad_from, grad_mine, out_sent, gate_own[0], part_down, down_other = sync(
        [], grad_from, grad_mine, out_sent, gate_own[0], part_down, down_other
    )
    down_hops = Scatter(part_down, slots)
    gate_other = [y_swap(gate_own[0]), None]
    out_got = swap(out_sent, "core")
    mixed_mine, mixed_other, bias_part = attend_back(
        qkv_mine, qkv_from, grad_mine, grad_from, lse, rotary_mine, rotary_other, table_of, factor
    )
    mixed_mine, mixed_other, out_got, gate_arrived[1] = sync(
        [down_hops], mixed_mine, mixed_other, out_got, gate_arrived[1]
    )
    down_hops.hop()
    mixed_from = swap(mixed_other, "core")
    out_oth = for_row(g2_rows, attended[None], False, out_got)
    gate_own[1] = for_y(tokens_b, pair, True, gate_got, gate_arrived[1], at=1, first=1, count=1)
    mixed = jnp.concatenate(
        [
            jnp.where(core == 0, mixed_mine, mixed_from),
            jnp.where(core == 0, mixed_from, mixed_mine),
        ],
        axis=2,
    )
    in_sent = for_core(tokens_a, mixed, True)
    in_sent, mixed, gate_own[1], gate_other[0], out_oth = sync(
        [], in_sent, mixed, gate_own[1], gate_other[0], out_oth
    )
    in_got = swap(in_sent, "core")
    out_arrived = swap(out_oth, "row")
    gate_other[1] = y_swap(gate_own[1])
    part_a = to_features(mixed, pieces_in, True)
    part_a, in_got, out_arrived = sync([down_hops], part_a, in_got, out_arrived)
    hops = Scatter(part_a, slots)
    spans = (dict(at=0, first=0, count=2), dict(at=2, first=2, count=1))
    in_oth = [for_row(tokens_a, mixed, True, in_got, **span) for span in spans]
    in_arrived = [swap(x, "row") for x in in_oth]
    out_own = for_y(g2_rows, attended[None], False, out_got, out_arrived)
    *in_oth, out_own = sync([hops], *in_oth, out_own)
    hops.hop()
    down_total = y_total(down_own, down_other)
    gate_total = [y_total(gate_own[0], gate_other[0]), None]
    in_arrived[0], gate_other[1], down_total, gate_total[0] = sync(
        [hops], in_arrived[0], gate_other[1], down_total, gate_total[0]
    )
    hops.hop()
    out_other_y = y_swap(out_own)
    in_own = [for_y(tokens_a, mixed, True, in_got, in_arrived[0], **spans[0])]
    gate_total[1] = y_total(gate_own[1], gate_other[1])
    in_own[0], gate_total[1], in_arrived[1], out_other_y = sync(
        [hops], in_own[0], gate_total[1], in_arrived[1], out_other_y
    )
    in_other = [y_swap(in_own[0])]
    input_low, sums_a = norm_back(stream, hops.terms(), g2, gain_a, 0)
    down_rest = swap(down_total, "core")
    gate_rest = [swap(x, "core") for x in gate_total]
    out_total = y_total(out_own, out_other_y)
    out_rest = swap(out_total, "core")
    in_own.append(for_y(tokens_a, mixed, True, in_got, in_arrived[1], **spans[1]))
    input_low, sums_a, in_own[1], down_rest, out_rest, *gate_rest = sync(
        [], input_low, sums_a, in_own[1], down_rest, out_rest, *gate_rest
    )

    bias_all = jnp.zeros((3, 2 * slots * columns), F32)
    bias_all = lax.dynamic_update_slice(
        bias_all, bias_part[:, 0, :], (jnp.int32(0), (place * 2 + core) * columns)
    ).reshape(-1, wide)
    sums = jnp.concatenate([sums_a, sums_b], axis=0)
    own, oth = sums[:, :wide], natural(sums[:, wide:])
    total = jnp.concatenate([own, bias_all, oth], axis=0)

    in_other.append(y_swap(in_own[1]))
    input_grad = from_sequence(input_low)
    down_grad = join(down_total, down_rest, 2)[0]
    if slots == 4:
        arrived = lax.ppermute(total, "col", PAIR)
        arrived, input_grad, down_grad = sync([], arrived, input_grad, down_grad)
        total = total + arrived
        arrived = lax.ppermute(total, "col", MID)
        down_hops.flying = list(tie(down_hops.flying, input_grad))
        down_hops.hop()
        gate_grad = join_pairs(core[None], gate_total, gate_rest)
        arrived, gate_grad, in_other[0] = sync([down_hops], arrived, gate_grad, in_other[0])
        total = total + arrived
        outer = lax.ppermute(total, "col", OUT)
        layer_low = (residual + sum(t.astype(F32) for t in down_hops.terms())).astype(BF16)
        in_total = [y_total(in_own[0], in_other[0])]
        in_rest = [swap(in_total[0], "core")]
        outer, layer_low, in_rest[0] = sync([], outer, layer_low, in_rest[0])
        total = jnp.where((place == 0) | (place == 3), outer, total)
    else:
        gate_grad = join_pairs(core[None], gate_total, gate_rest)
        layer_low = (residual + sum(t.astype(F32) for t in down_hops.terms())).astype(BF16)
        in_total = [y_total(in_own[0], in_other[0])]
        in_rest = [swap(in_total[0], "core")]
        total = lax.psum(total, "col")
    layer_out = from_sequence(layer_low)
    out_grad = join(out_total, out_rest, 2)[0]
    arrived = swap(total, "core")
    arrived, layer_out, in_other[1], out_grad = sync([], arrived, layer_out, in_other[1], out_grad)
    total = total + arrived
    cut = own.shape[0] + bias_all.shape[0]
    sent = jnp.concatenate([total[cut:], total[own.shape[0] : cut]], axis=0)
    total = total[:cut] + swap(sent, "row")
    vectors = lax.psum(total, "y") if y_count != 2 else total + swap(total, "y")
    bias_grad = take(vectors[4:].reshape(3, -1), place * 2 * columns, 2 * columns, 1)
    input_grad = input_grad.astype(F32)
    in_total.append(y_total(in_own[1], in_other[1]))
    in_rest.append(swap(in_total[1], "core"))
    in_grad = jnp.concatenate([join(x, r, 1) for x, r in zip(in_total, in_rest)], axis=0)
    return (
        layer_out[None],
        input_grad,
        vectors[0:1],
        vectors[1:2],
        jnp.transpose(in_grad, (1, 0, 2))[None],
        bias_grad[None],
        out_grad[None],
        vectors[2:3],
        vectors[3:4],
        gate_grad[None],
        down_grad[None],
    )


def solution(mesh):
    dp, rows, cols = (mesh.shape[a] for a in ("dp", "row", "col"))
    split = Mesh(mesh.devices.reshape(dp // 2, 2, rows, cols), ("y", "core", "row", "col"))
    tokens = ("y", "core", "col")
    return jax.shard_map(
        local,
        mesh=split,
        in_specs=(
            P(tokens, "row"),
            P(None, "row"),
            P(None, "row"),
            P(None, "row", None, "col"),
            P(None, None, "col"),
            P(None, "col", "row"),
            P(None, "row"),
            P(None, "row"),
            P(None, "row", None, "col"),
            P(None, "col", "row"),
            P(tokens, "row"),
        ),
        out_specs=(
            P(None, tokens, "row"),
            P(tokens, "row"),
            P(None, "row"),
            P(None, "row"),
            P(None, "row", None, "col"),
            P(None, None, "col"),
            P(None, "col", "row"),
            P(None, "row"),
            P(None, "row"),
            P(None, "row", None, "col"),
            P(None, "col", "row"),
        ),
        check_vma=False,
    )
```

```python
import functools
import math

import jax
import jax.numpy as jnp
from jax import lax
from jax.experimental import pallas as pl
from jax.experimental.pallas import tpu as pltpu
from jax.sharding import Mesh
from jax.sharding import PartitionSpec as P

HEAD_DIM = 64
ROT = 16
LENGTH = 1024
EPSILON = 1e-05
F32 = jnp.float32
BF16 = jnp.bfloat16
LANES = 128
MIB = 1 << 20


def swap(x, axis):
    return lax.ppermute(x, axis, [(0, 1), (1, 0)])


PAIR = [(0, 1), (1, 0), (2, 3), (3, 2)]
MID = [(1, 2), (2, 1)]
OUT = [(1, 0), (2, 3)]
IN = [(0, 1), (3, 2)]
ORDER4 = ((0, 1, 2, 3), (1, 0, 2, 3), (2, 3, 1, 0), (3, 2, 1, 0))


def slot_order(place, count):
    if count == 4:
        return jnp.array(ORDER4, jnp.int32)[place]
    return jnp.arange(count, dtype=jnp.int32)


def tie(values, *behind):
    return lax.optimization_barrier((tuple(values), behind))[0]


def after(x, *behind):
    return tie((x,), *behind)[0] if behind else x


class Gather:
    def __init__(self, own, count):
        self.own, self.count, self.got = own, count, []
        self.flying = []
        if count == 4:
            self.flying = [lax.ppermute(own, "col", PAIR), lax.ppermute(own, "col", MID)]

    def hop(self):
        if self.count != 4:
            return
        if not self.got:
            one, mid = self.flying
            self.got = [one, mid]
            self.flying = [lax.ppermute(one, "col", MID), lax.ppermute(mid, "col", OUT)]
        else:
            far, mid_out = self.flying
            self.got += [far, mid_out]
            self.flying = [lax.ppermute(far, "col", OUT)]

    def rows(self):
        if self.count != 4:
            return lax.all_gather(self.own, "col", axis=0, tiled=True)
        one, mid, far, mid_out = self.got
        return jnp.concatenate([self.own, one, mid + mid_out, far + self.flying[0]], axis=0)


class Scatter:
    def __init__(self, parts, count):
        self.count, self.step, self.parts = count, 0, parts
        self.flying, self.two = [], None
        if count == 4:
            rows = parts.shape[0] // count
            self.part = [parts[i * rows : (i + 1) * rows] for i in range(4)]
            self.flying = [lax.ppermute(self.part[3], "col", IN)]
            self.two = lax.ppermute(self.part[2], "col", IN)

    def hop(self):
        if self.count != 4:
            return
        if self.step == 0:
            three = self.part[3] + self.flying[0]
            self.flying = [lax.ppermute(three, "col", MID), self.two]
        else:
            one, two = self.part[1] + self.flying[0], self.part[2] + self.flying[1]
            self.flying = [lax.ppermute(one, "col", PAIR), lax.ppermute(two, "col", MID)]
        self.step += 1

    def terms(self):
        if self.count != 4:
            mine = lax.psum_scatter(self.parts, "col", scatter_dimension=0, tiled=True)
            return (mine, jnp.zeros_like(mine), jnp.zeros_like(mine))
        return (self.part[0], *self.flying)


def sync(moving, *values):
    flat = [x for m in moving for x in m.flying] + list(values)
    flat = list(lax.optimization_barrier(tuple(flat)))
    for m in moving:
        count = len(m.flying)
        m.flying, flat = flat[:count], flat[count:]
    return flat[0] if len(flat) == 1 else flat


def params(mib, axes=1):
    return pltpu.CompilerParams(
        vmem_limit_bytes=mib * MIB, dimension_semantics=("arbitrary",) * axes
    )


SHARE = 8


def cost(flops, moved, trans=0):
    return pl.CostEstimate(
        flops=int(flops / SHARE),
        bytes_accessed=int(moved / SHARE),
        transcendentals=int(trans / SHARE),
    )


def stats_of(value):
    width = value.shape[1]
    average = jnp.sum(value, axis=1, keepdims=True) / width
    centred = value - average
    variance = jnp.sum(centred * centred, axis=1, keepdims=True) / width
    inv_root = lax.rsqrt(variance + EPSILON)
    return centred * inv_root, inv_root


def norm_first(stream, gain, shift):
    rows, width = stream.shape
    block = rows // 4

    def body(x_ref, gain_ref, shift_ref, low_ref):
        xhat, unused = stats_of(x_ref[...].astype(F32))
        low_ref[...] = (xhat * gain_ref[...] + shift_ref[...]).astype(BF16)

    row = pl.BlockSpec((block, width), lambda i: (i, 0))
    flat = pl.BlockSpec((1, width), lambda i: (0, 0))
    return pl.pallas_call(
        body,
        grid=(4,),
        in_specs=[row, flat, flat],
        out_specs=row,
        out_shape=jax.ShapeDtypeStruct((rows, width), BF16),
        compiler_params=params(6),
        cost_estimate=cost(rows * width * 10, rows * width * 4),
        name="norm_first",
    )(stream, gain, shift)


def norm_second(stream, terms, gain, shift):
    rows, width = stream.shape
    block = rows // 4

    def body(x_ref, a_ref, b_ref, c_ref, gain_ref, shift_ref, res_ref, low_ref):
        residual = (
            x_ref[...].astype(F32)
            + a_ref[...].astype(F32)
            + b_ref[...].astype(F32)
            + c_ref[...].astype(F32)
        )
        res_ref[...] = residual
        xhat, unused = stats_of(residual)
        low_ref[...] = (xhat * gain_ref[...] + shift_ref[...]).astype(BF16)

    row = pl.BlockSpec((block, width), lambda i: (i, 0))
    flat = pl.BlockSpec((1, width), lambda i: (0, 0))
    return pl.pallas_call(
        body,
        grid=(4,),
        in_specs=[row] * 4 + [flat, flat],
        out_specs=[row, row],
        out_shape=[
            jax.ShapeDtypeStruct((rows, width), F32),
            jax.ShapeDtypeStruct((rows, width), BF16),
        ],
        compiler_params=params(6),
        cost_estimate=cost(rows * width * 12, rows * width * 14),
        name="norm_second",
    )(stream, *terms, gain, shift)


def norm_back(stream, terms, upper, gain, both):
    rows, width = stream.shape
    block = rows // 4

    def body(x_ref, a_ref, b_ref, c_ref, up_ref, gain_ref, low_ref, sums_ref, *full_ref):
        xhat, inv_root = stats_of(x_ref[...].astype(F32))
        grad = a_ref[...].astype(F32) + b_ref[...].astype(F32) + c_ref[...].astype(F32)
        scaled = grad * gain_ref[...]
        mean_scaled = jnp.sum(scaled, axis=1, keepdims=True) / width
        mean_cross = jnp.sum(scaled * xhat, axis=1, keepdims=True) / width
        result = up_ref[...].astype(F32) + inv_root * (scaled - mean_scaled - xhat * mean_cross)
        low_ref[...] = result.astype(BF16)
        if full_ref:
            full_ref[0][...] = result

        @pl.when(pl.program_id(0) == 0)
        def _():
            sums_ref[...] = jnp.zeros_like(sums_ref)

        sums_ref[...] += jnp.concatenate(
            [
                jnp.sum(grad * xhat, axis=0, keepdims=True),
                jnp.sum(grad, axis=0, keepdims=True),
            ],
            axis=0,
        )

    row = pl.BlockSpec((block, width), lambda i: (i, 0))
    flat = pl.BlockSpec((1, width), lambda i: (0, 0))
    sums = pl.BlockSpec((2, width), lambda i: (0, 0))
    return pl.pallas_call(
        body,
        grid=(4,),
        in_specs=[row] * 5 + [flat],
        out_specs=[row, sums] + [row] * both,
        out_shape=[
            jax.ShapeDtypeStruct((rows, width), BF16),
            jax.ShapeDtypeStruct((2, width), F32),
        ]
        + [jax.ShapeDtypeStruct((rows, width), F32)] * both,
        compiler_params=params(10),
        cost_estimate=cost(rows * width * 20, rows * width * 18),
        name="norm_back",
    )(stream, *terms, upper, gain)


def cuts_of(sizes):
    ends = [sum(sizes[: i + 1]) for i in range(len(sizes))]
    return [(end - size, end) for end, size in zip(ends, sizes)]


def roll_lanes(value, shift):
    return pltpu.roll(value, shift % value.shape[1], 1)


def turn(value, table, sign):
    times = value.shape[1] // LANES
    wide = [jnp.concatenate([table[i]] * times, axis=1) for i in range(3)]
    ahead = roll_lanes(value, -(ROT // 2))
    behind = roll_lanes(value, ROT // 2)
    moved = ahead * wide[1] + behind * wide[2]
    return value * wide[0] + (moved if sign > 0 else -moved)


def qkv_columns(tokens, pieces, bias, table, half):
    rows, width = tokens.shape
    columns = pieces[0].shape[2] // 2
    cuts = cuts_of([p.shape[1] for p in pieces])

    def body(half_ref, x_ref, *refs):
        bias_ref, table_ref, out_ref = refs[-3:]
        which = pl.program_id(0)
        acc = bias_ref[0]
        for w_ref, (low, high) in zip(refs, cuts):
            acc = acc + jnp.dot(x_ref[:, low:high], w_ref[0], preferred_element_type=F32)

        @pl.when(which < 2)
        def _():
            out_ref[0] = turn(acc, table_ref, 1).astype(BF16)

        @pl.when(which == 2)
        def _():
            out_ref[0] = acc.astype(BF16)

    return pl.pallas_call(
        body,
        grid_spec=pltpu.PrefetchScalarGridSpec(
            num_scalar_prefetch=1,
            grid=(3,),
            in_specs=[pl.BlockSpec((rows, width), lambda j, h: (0, 0))]
            + [pl.BlockSpec((1, p.shape[1], columns), lambda j, h: (j, 0, h[0])) for p in pieces]
            + [
                pl.BlockSpec((1, 1, columns), lambda j, h: (j, 0, h[0])),
                pl.BlockSpec((3, rows, LANES), lambda j, h: (0, 0, 0)),
            ],
            out_specs=pl.BlockSpec((1, rows, columns), lambda j, h: (j, 0, 0)),
        ),
        out_shape=jax.ShapeDtypeStruct((3, rows, columns), BF16),
        compiler_params=params(16),
        cost_estimate=cost(6 * rows * width * columns, 2 * (rows * width + 3 * columns * width)),
        name="qkv_columns",
    )(half, tokens, *pieces, bias, table)


def place_of(order_ref, slot, core, rows):
    return pl.multiple_of((order_ref[1 + slot] * 2 + core) * rows, rows)


CHUNK = 256


def score_chunk(query, key, first):
    scores = lax.dot_general(query, key, (((1,), (1,)), ((), ())), preferred_element_type=F32)
    last = scores[:, first:]
    at_query = lax.broadcasted_iota(jnp.int32, last.shape, 0)
    at_key = lax.broadcasted_iota(jnp.int32, last.shape, 1)
    last = jnp.where(at_query >= at_key, last, -jnp.inf)
    return last if first == 0 else jnp.concatenate([scores[:, :first], last], axis=1)


def attend(mine, other, order, factor):
    unused, rows, columns = mine.shape
    slots = order.shape[0] - 1
    piece = rows // slots
    length = 2 * rows

    def body(order_ref, mine_ref, other_ref, out_mine, out_other, lse_ref, whole, result):
        core = order_ref[0]
        for slot in range(slots):
            here = slice(slot * piece, (slot + 1) * piece)
            whole[:, pl.ds(place_of(order_ref, slot, core, piece), piece), :] = mine_ref[:, here, :]
            whole[:, pl.ds(place_of(order_ref, slot, 1 - core, piece), piece), :] = other_ref[
                :, here, :
            ]
        for head in range(LANES // HEAD_DIM):
            lanes = slice(head * HEAD_DIM, (head + 1) * HEAD_DIM)
            for first in range(0, length, CHUNK):
                upto = first + CHUNK
                query = whole[0, first:upto, lanes] * jnp.bfloat16(factor)
                scores = score_chunk(query, whole[1, :upto, lanes], first)
                highest = jnp.max(scores, axis=1, keepdims=True)
                exponent = jnp.exp(scores - highest)
                summed = jnp.sum(exponent, axis=1, keepdims=True)
                mixed = jnp.dot(
                    exponent.astype(BF16), whole[2, :upto, lanes], preferred_element_type=F32
                )
                result[first:upto, lanes] = (mixed * (1.0 / summed)).astype(BF16)
                lse_ref[0, first:upto, head : head + 1] = highest + jnp.log(summed)
        for slot in range(slots):
            here = slice(slot * piece, (slot + 1) * piece)
            out_mine[here, :] = result[pl.ds(place_of(order_ref, slot, core, piece), piece), :]
            out_other[here, :] = result[pl.ds(place_of(order_ref, slot, 1 - core, piece), piece), :]

    groups = columns // LANES
    three = pl.BlockSpec((3, rows, LANES), lambda g, o: (0, 0, g))
    one = pl.BlockSpec((rows, LANES), lambda g, o: (0, g))
    return pl.pallas_call(
        body,
        grid_spec=pltpu.PrefetchScalarGridSpec(
            num_scalar_prefetch=1,
            grid=(groups,),
            in_specs=[three, three],
            out_specs=[one, one, pl.BlockSpec((1, length, 2), lambda g, o: (g, 0, 0))],
            scratch_shapes=[
                pltpu.VMEM((3, length, LANES), BF16),
                pltpu.VMEM((length, LANES), BF16),
            ],
        ),
        out_shape=[
            jax.ShapeDtypeStruct((rows, columns), BF16),
            jax.ShapeDtypeStruct((rows, columns), BF16),
            jax.ShapeDtypeStruct((groups, length, 2), F32),
        ],
        compiler_params=params(20),
        cost_estimate=cost(
            4 * length * length * columns, 16 * rows * columns, columns * length * length / 128
        ),
        name="attend",
    )(order, mine, other)


def attend_back(mine, other, grad_mine, grad_other, lse, table_mine, table_other, order, factor):
    unused, rows, columns = mine.shape
    slots = order.shape[0] - 1
    piece = rows // slots
    length = 2 * rows
    across = (((1,), (1,)), ((), ()))
    down = (((0,), (0,)), ((), ()))

    def body(
        order_ref,
        mine_ref,
        other_ref,
        gm_ref,
        go_ref,
        lse_ref,
        tm_ref,
        to_ref,
        out_mine,
        out_other,
        bias_ref,
        whole,
        grads,
        dq_ref,
        dkv_ref,
    ):
        core = order_ref[0]
        for slot in range(slots):
            here = slice(slot * piece, (slot + 1) * piece)
            one = pl.ds(place_of(order_ref, slot, core, piece), piece)
            two = pl.ds(place_of(order_ref, slot, 1 - core, piece), piece)
            whole[:, one, :] = mine_ref[:, here, :]
            whole[:, two, :] = other_ref[:, here, :]
            grads[one, :] = gm_ref[here, :]
            grads[two, :] = go_ref[here, :]
        heads = LANES // HEAD_DIM
        for head in range(heads):
            lanes = slice(head * HEAD_DIM, (head + 1) * HEAD_DIM)
            for first in reversed(range(0, length, CHUNK)):
                upto = first + CHUNK
                query = whole[0, first:upto, lanes] * jnp.bfloat16(factor)
                key = whole[1, :upto, lanes]
                value = whole[2, :upto, lanes]
                grad = grads[first:upto, lanes]
                scores = score_chunk(query, key, first)
                probs = jnp.exp(scores - lse_ref[0, first:upto, head : head + 1])
                probs_grad = lax.dot_general(grad, value, across, preferred_element_type=F32)
                shift = jnp.sum(probs * probs_grad, axis=1, keepdims=True)
                scores_grad = (probs * (probs_grad - shift)).astype(BF16)
                dq_ref[first:upto, lanes] = (
                    jnp.dot(scores_grad, key, preferred_element_type=F32) * factor
                )
                dk = lax.dot_general(scores_grad, query, down, preferred_element_type=F32)
                dv = lax.dot_general(
                    probs.astype(BF16), grad, down, preferred_element_type=F32
                )
                if upto == length:
                    dkv_ref[0, :, lanes] = dk
                    dkv_ref[1, :, lanes] = dv
                else:
                    dkv_ref[0, :upto, lanes] += dk
                    dkv_ref[1, :upto, lanes] += dv
        total = [jnp.zeros((1, LANES), F32) for _ in range(3)]
        for slot in range(slots):
            here = slice(slot * piece, (slot + 1) * piece)
            for at, table, out in (
                (core, tm_ref, out_mine),
                (1 - core, to_ref, out_other),
            ):
                rows_at = pl.ds(place_of(order_ref, slot, at, piece), piece)
                angles = table[:, here, :]
                parts = (
                    turn(dq_ref[rows_at, :], angles, -1).astype(BF16),
                    turn(dkv_ref[0, rows_at, :], angles, -1).astype(BF16),
                    dkv_ref[1, rows_at, :].astype(BF16),
                )
                for i in range(3):
                    out[i, here, :] = parts[i]
                    total[i] += jnp.sum(parts[i].astype(F32), axis=0, keepdims=True)
        for i in range(3):
            bias_ref[i] = total[i]

    groups = columns // LANES
    three = pl.BlockSpec((3, rows, LANES), lambda g, o: (0, 0, g))
    one = pl.BlockSpec((rows, LANES), lambda g, o: (0, g))
    full = pl.BlockSpec((3, rows, LANES), lambda g, o: (0, 0, 0))
    return pl.pallas_call(
        body,
        grid_spec=pltpu.PrefetchScalarGridSpec(
            num_scalar_prefetch=1,
            grid=(groups,),
            in_specs=[
                three,
                three,
                one,
                one,
                pl.BlockSpec((1, length, 2), lambda g, o: (g, 0, 0)),
                full,
                full,
            ],
            out_specs=[three, three, pl.BlockSpec((3, 1, LANES), lambda g, o: (0, 0, g))],
            scratch_shapes=[
                pltpu.VMEM((3, length, LANES), BF16),
                pltpu.VMEM((length, LANES), BF16),
                pltpu.VMEM((length, LANES), F32),
                pltpu.VMEM((2, length, LANES), F32),
            ],
        ),
        out_shape=[
            jax.ShapeDtypeStruct((3, rows, columns), BF16),
            jax.ShapeDtypeStruct((3, rows, columns), BF16),
            jax.ShapeDtypeStruct((3, 1, columns), F32),
        ],
        compiler_params=params(20),
        cost_estimate=cost(
            10 * length * length * columns, 40 * rows * columns, columns * length * length / 128
        ),
        name="attend_back",
    )(order, mine, other, grad_mine, grad_other, lse, table_mine, table_other)


ACROSS = (((1,), (1,)), ((), ()))
DOWN = (((0,), (0,)), ((), ()))


def feed_forward(tokens, pieces, hidden_grad):
    rows, width = tokens.shape
    units = pieces[0].shape[2]
    block = 256 if units > 256 else units
    cuts = cuts_of([p.shape[1] for p in pieces])

    def body(x_ref, *refs):
        hg_ref, hidden_ref, grad_ref = refs[-3:]
        gate_up = 0.0
        for w_ref, (low, high) in zip(refs, cuts):
            both = jnp.concatenate([w_ref[0], w_ref[1]], axis=1)
            gate_up += jnp.dot(x_ref[:, low:high], both, preferred_element_type=F32)
        gate, up = gate_up[:, :block], gate_up[:, block:]
        sigma = jax.nn.sigmoid(gate)
        silu = gate * sigma
        hidden_ref[...] = (silu * up).astype(BF16)
        grad = hg_ref[...].astype(F32)
        grad_ref[0] = (grad * up * (sigma + silu * (1.0 - sigma))).astype(BF16)
        grad_ref[1] = (grad * silu).astype(BF16)

    return pl.pallas_call(
        body,
        grid=(pl.cdiv(units, block),),
        in_specs=[pl.BlockSpec((rows, width), lambda j: (0, 0))]
        + [pl.BlockSpec((2, p.shape[1], block), lambda j: (0, 0, j)) for p in pieces]
        + [pl.BlockSpec((rows, block), lambda j: (0, j))],
        out_specs=[
            pl.BlockSpec((rows, block), lambda j: (0, j)),
            pl.BlockSpec((2, rows, block), lambda j: (0, 0, j)),
        ],
        out_shape=[
            jax.ShapeDtypeStruct((rows, units), BF16),
            jax.ShapeDtypeStruct((2, rows, units), BF16),
        ],
        compiler_params=params(20),
        cost_estimate=cost(
            4 * rows * width * units, 4 * width * units + 2 * rows * width, rows * units
        ),
        name="feed_forward",
    )(tokens, *pieces, hidden_grad)


def to_features(values, pieces, across):
    count, rows, units = values.shape
    axis = 1 if across else 2
    sizes = [p.shape[axis] for p in pieces]
    block = sizes[-1]
    width = sum(sizes)
    owner = [i for i, size in enumerate(sizes) for _ in range(size // block)]
    starts = [owner.index(i) for i in range(len(pieces))]
    dims = ACROSS if across else (((1,), (0,)), ((), ()))

    def body(v_ref, *refs):
        step = pl.program_id(0)
        for i, w_ref in enumerate(refs[:-1]):

            @pl.when((step >= starts[i]) & (step < starts[i] + sizes[i] // block))
            def _():
                total = 0.0
                for n in range(count):
                    total += lax.dot_general(v_ref[n], w_ref[n], dims, preferred_element_type=F32)
                refs[-1][...] = total.astype(BF16)

    def spec(i):
        last = sizes[i] // block - 1
        at = lambda j: jnp.clip(j - starts[i], 0, last)
        if across:
            return pl.BlockSpec((count, block, units), lambda j: (0, at(j), 0))
        return pl.BlockSpec((count, units, block), lambda j: (0, 0, at(j)))

    return pl.pallas_call(
        body,
        grid=(width // block,),
        in_specs=[pl.BlockSpec((count, rows, units), lambda j: (0, 0, 0))]
        + [spec(i) for i in range(len(pieces))],
        out_specs=pl.BlockSpec((rows, block), lambda j: (0, j)),
        out_shape=jax.ShapeDtypeStruct((rows, width), BF16),
        compiler_params=params(32),
        cost_estimate=cost(
            2 * count * rows * width * units, 2 * count * (width + rows) * units + 2 * rows * width
        ),
        name="to_features",
    )(values, *pieces)


def from_features(index, tokens, pieces, block):
    rows, width = tokens.shape
    cuts = cuts_of([p.shape[1] for p in pieces])
    count = index.shape[0]

    def body(index_ref, x_ref, *refs):
        total = 0.0
        for w_ref, (low, high) in zip(refs, cuts):
            total += lax.dot_general(
                x_ref[:, low:high], w_ref[...], ACROSS, preferred_element_type=F32
            )
        refs[-1][0] = total.astype(BF16)

    out = pl.pallas_call(
        body,
        grid_spec=pltpu.PrefetchScalarGridSpec(
            num_scalar_prefetch=1,
            grid=(count,),
            in_specs=[pl.BlockSpec((rows, width), lambda j, q: (0, 0))]
            + [pl.BlockSpec((block, p.shape[1]), lambda j, q: (q[j], 0)) for p in pieces],
            out_specs=pl.BlockSpec((1, rows, block), lambda j, q: (j, 0, 0)),
        ),
        out_shape=jax.ShapeDtypeStruct((count, rows, block), BF16),
        compiler_params=params(16),
        cost_estimate=cost(
            2 * rows * width * block * count, 2 * width * (rows + block * count)
        ),
        name="from_features",
    )(index, tokens, *pieces)
    return out


def grad_quarters(quarters, tokens, others, adds, rows_first, first=0, count=None):
    rows, width = tokens.shape
    units = others.shape[2]
    count = others.shape[0] if count is None else count
    quarter = width // 4
    k = quarters.shape[0]
    form = (quarter, units) if rows_first else (units, quarter)

    def body(q_ref, x_ref, y_ref, *refs):
        x, y = x_ref[...], y_ref[0]
        left, right = (x, y) if rows_first else (y, x)
        total = lax.dot_general(left, right, DOWN, preferred_element_type=F32)
        for ref in refs[:-1]:
            total += ref[0, 0].astype(F32)
        refs[-1][0, 0] = total.astype(BF16)

    def shifted(at_k, at_n):
        return pl.BlockSpec((1, 1, *form), lambda i, j, q: (i + at_k, j + at_n, 0, 0))

    return pl.pallas_call(
        body,
        grid_spec=pltpu.PrefetchScalarGridSpec(
            num_scalar_prefetch=1,
            grid=(k, count),
            in_specs=[
                pl.BlockSpec((rows, quarter), lambda i, j, q: (0, q[i])),
                pl.BlockSpec((1, rows, units), lambda i, j, q: (j + first, 0, 0)),
            ]
            + [shifted(at_k, at_n) for unused, at_k, at_n in adds],
            out_specs=shifted(0, 0),
        ),
        out_shape=jax.ShapeDtypeStruct((k, count, *form), BF16),
        compiler_params=params(20, 2),
        cost_estimate=cost(
            2 * k * count * rows * quarter * units,
            2 * k * count * quarter * units * (1 + len(adds)) + 2 * rows * (width + count * units),
        ),
        name="grad_quarters",
    )(quarters, tokens, others, *[add[0] for add in adds])


def join_pairs(core, parts, rests):
    rows, units = parts[0].shape[1:]
    block = 128 if rows % 128 == 0 else rows
    steps = rows // block

    def body(core_ref, *refs):
        half = pl.program_id(0)
        out_ref = refs[-1]
        for i in range(2):

            @pl.when(half == core_ref[0])
            def _():
                out_ref[:, i, :] = refs[i][0].astype(F32)

            @pl.when(half != core_ref[0])
            def _():
                out_ref[:, i, :] = refs[2 + i][0].astype(F32)

    def spec(same):
        def at(h, j, c):
            wanted = (h == c[0]) if same else (h != c[0])
            return (0, jnp.where(wanted, j, 0), 0)

        return pl.BlockSpec((1, block, units), at)

    return pl.pallas_call(
        body,
        grid_spec=pltpu.PrefetchScalarGridSpec(
            num_scalar_prefetch=1,
            grid=(2, steps),
            in_specs=[spec(True), spec(True), spec(False), spec(False)],
            out_specs=pl.BlockSpec((block, 2, units), lambda h, j, c: (h * steps + j, 0, 0)),
        ),
        out_shape=jax.ShapeDtypeStruct((2 * rows, 2, units), F32),
        compiler_params=params(16, 2),
        cost_estimate=cost(rows * units, 24 * rows * units),
        name="join_pairs",
    )(core, *parts, *rests)


def rotary_table(position):
    half = ROT // 2
    lane = jnp.arange(LANES) % HEAD_DIM
    frequency = 10000.0 ** (-((lane % half).astype(F32) * 2.0 / ROT))
    angles = position.astype(F32)[:, None] * frequency[None, :]
    lane = lane[None, :]
    cosine = jnp.where(lane < ROT, jnp.cos(angles), 1.0)
    sine = jnp.sin(angles)
    return jnp.stack(
        [
            cosine,
            jnp.where(lane < half, -sine, 0.0),
            jnp.where((lane >= half) & (lane < ROT), sine, 0.0),
        ]
    )


def local(
    inputs,
    first_gain,
    first_shift,
    project_in,
    project_bias,
    project_out,
    second_gain,
    second_shift,
    gate_weight,
    down_weight,
    cotangent,
):
    y_count = lax.axis_size("y")
    slots = lax.axis_size("col")
    y = lax.axis_index("y")
    core = lax.axis_index("core")
    row = lax.axis_index("row")
    place = lax.axis_index("col")
    factor = 1.0 / math.sqrt(HEAD_DIM)
    half_rows = inputs.shape[0] // 2
    wide = inputs.shape[1]
    width = 2 * wide

    def take(x, start, size, axis):
        return lax.dynamic_slice_in_dim(x, start, size, axis)

    straight = [(0, 0), (1, 2), (2, 1), (3, 3)]
    crossed = [(0, 2), (1, 0), (2, 3), (3, 1)]
    aligned = core == row

    def order_features(own, oth):
        low, high = oth[..., : wide // 2], oth[..., wide // 2 :]
        return jnp.concatenate(
            [own, jnp.where(core == 0, low, high), jnp.where(core == 0, high, low)], axis=-1
        )

    def natural(oth):
        low, high = oth[..., : wide // 2], oth[..., wide // 2 :]
        return jnp.concatenate(
            [jnp.where(core == 0, low, high), jnp.where(core == 0, high, low)], axis=-1
        )

    def to_sequence(x):
        a = lax.ppermute(take(x, row * half_rows, half_rows, 0), ("core", "row"), straight)
        b = lax.ppermute(take(x, (1 - row) * half_rows, half_rows, 0), ("core", "row"), crossed)
        return order_features(jnp.where(aligned, a, b), jnp.where(aligned, b, a))

    def from_sequence(x):
        own, oth = x[:, :wide], natural(x[:, wide:])
        a = jnp.where(aligned, own, oth)
        b = jnp.where(aligned, oth, own)
        a = lax.ppermute(a, ("core", "row"), [(j, i) for i, j in straight])
        b = lax.ppermute(b, ("core", "row"), [(j, i) for i, j in crossed])
        top = jnp.where(row == 0, a, b)
        bottom = jnp.where(row == 0, b, a)
        return jnp.concatenate([top, bottom], axis=0)

    order = slot_order(place, slots)
    table_of = jnp.concatenate([core[None], order]).astype(jnp.int32)
    inside = jnp.arange(half_rows)
    position = lambda c: ((order[:, None] * 2 + c) * half_rows + inside[None, :]).reshape(-1)
    rotary_mine = rotary_table(position(core))
    rotary_other = rotary_table(position(1 - core))

    stream = to_sequence(inputs)
    vectors = jnp.concatenate([first_gain, first_shift, second_gain, second_shift], axis=0)
    vectors = order_features(vectors, swap(vectors, "row"))
    gain_a, shift_a, gain_b, shift_b = (vectors[i : i + 1] for i in range(4))

    def part_of(w, axis):
        part = w.shape[axis] // 2
        return take(w, core * part, part, axis)

    w_in = jnp.transpose(project_in[0], (1, 0, 2))
    w_out, w_down = project_out[0], down_weight[0]
    w_gate = jnp.transpose(gate_weight[0], (1, 0, 2))
    fixed = 0 * core

    def quarters(*q):
        return jnp.stack(q).astype(jnp.int32)

    def for_core(tokens, others, rows_first, **span):
        return grad_quarters(quarters(1 - core, 3 + fixed), tokens, others, (), rows_first, **span)

    def for_row(tokens, others, rows_first, got, at=0, **span):
        return grad_quarters(
            quarters(2 + fixed), tokens, others, ((got, 1, at),), rows_first, **span
        )

    def for_y(tokens, others, rows_first, got, arrived, at=0, **span):
        adds = ((got, 0, at), (arrived, 0, 0))
        return grad_quarters(quarters(core), tokens, others, adds, rows_first, **span)[0]

    def y_swap(own):
        return swap(own, "y") if y_count == 2 else lax.psum(own, "y")

    def y_total(own, other):
        return (own.astype(F32) + other.astype(F32)).astype(BF16) if y_count == 2 else other

    def join(total, rest, axis):
        return jnp.concatenate(
            [jnp.where(core == 0, total, rest), jnp.where(core == 0, rest, total)], axis=axis
        ).astype(F32)

    low_a = norm_first(stream, gain_a, shift_a)
    in_half = swap(after(part_of(w_in, 1), stream), "row")
    cot = to_sequence(after(cotangent, low_a))
    hops = Gather(low_a, slots)
    rotary_mine = sync([hops], rotary_mine)
    hops.hop()
    rotary_other, out_part, down_part = sync(
        [hops], rotary_other, part_of(w_out, 1), part_of(w_down, 1)
    )
    hops.hop()
    out_half = swap(out_part, "row")
    w_gate, gate_part, in_half, cot = sync([hops], w_gate, part_of(w_gate, 1), in_half, cot)
    tokens_a = hops.rows()
    pieces_in = (w_in, in_half, swap(in_half, "core"))
    cot_hops = Gather(cot, slots)
    down_half = swap(after(down_part, cot), "row")
    bias = project_bias[0][:, None, :]
    qkv_other = qkv_columns(tokens_a, pieces_in, bias, rotary_mine, (1 - core)[None])
    qkv_from = swap(qkv_other, "core")
    qkv_mine = qkv_columns(tokens_a, pieces_in, bias, rotary_mine, core[None])
    out_mine, out_other, lse = attend(qkv_mine, qkv_from, table_of, factor)
    out_mine, out_other, out_half = sync([cot_hops], out_mine, out_other, out_half)
    cot_hops.hop()
    pieces_out = (w_out, out_half, swap(out_half, "core"))
    out_from = swap(out_other, "core")
    attended = jnp.concatenate(
        [jnp.where(core == 0, out_mine, out_from), jnp.where(core == 0, out_from, out_mine)], axis=1
    )
    part_out = to_features(attended[None], [p[None] for p in pieces_out], False)
    part_out, gate_part = sync([], part_out, gate_part)
    hops = Scatter(part_out, slots)
    down_half = sync([hops, cot_hops], down_half)
    hops.hop()
    cot_hops.hop()
    gate_half = swap(after(gate_part, down_half), "row")
    down_rest = sync([hops, cot_hops], swap(down_half, "core"))
    hops.hop()
    pieces_down = (w_down, down_half, down_rest)
    units = w_down.shape[0]
    ways = 2 if units % 32 == 0 else 1
    grad_rows = cot_hops.rows()
    hidden_grad = from_features(
        jnp.arange(ways, dtype=jnp.int32), grad_rows, pieces_down, units // ways
    )
    hidden_grad = jnp.concatenate([hidden_grad[i] for i in range(ways)], axis=1)
    grad_rows, hidden_grad = sync([hops], grad_rows, hidden_grad)
    residual, low_b = norm_second(stream, hops.terms(), gain_b, shift_b)

    hops = Gather(low_b, slots)
    sync([hops], low_b)
    hops.hop()
    gate_half = sync([hops], gate_half)
    hops.hop()
    gate_half, gate_rest = sync([hops], gate_half, swap(gate_half, "core"))
    tokens_b = hops.rows()
    pieces_gate = (w_gate, gate_half, gate_rest)
    hidden, pair = feed_forward(tokens_b, pieces_gate, hidden_grad)
    part_b = to_features(pair, pieces_gate, True)
    part_b, hidden, pair = sync([], part_b, hidden, pair)

    hops = Scatter(part_b, slots)
    down_sent = for_core(grad_rows, hidden[None], False)
    gate_sent = for_core(tokens_b, pair, True)
    down_sent, gate_sent = sync([hops], down_sent, gate_sent)
    hops.hop()
    down_got = swap(down_sent, "core")
    gate_got = swap(gate_sent, "core")
    down_oth = for_row(grad_rows, hidden[None], False, down_got)
    down_oth, gate_got = sync([hops], down_oth, gate_got)
    hops.hop()
    down_arrived = swap(down_oth, "row")
    gate_oth = [
        for_row(tokens_b, pair, True, gate_got, at=i, first=i, count=1) for i in range(2)
    ]
    gate_oth = list(sync([hops], *gate_oth))
    g2_low, sums_b, g2 = norm_back(residual, hops.terms(), cot, gain_b, 1)

    hops = Gather(g2_low, slots)
    gate_arrived = [swap(gate_oth[0], "row"), None]
    part_down = to_features(hidden[None], [p[None] for p in pieces_down], False)
    part_down, down_arrived = sync([hops], part_down, down_arrived)
    hops.hop()
    down_own = for_y(grad_rows, hidden[None], False, down_got, down_arrived)
    down_own, part_down = sync([hops], down_own, part_down)
    hops.hop()
    down_other = y_swap(down_own)
    gate_arrived[0], gate_oth[1] = sync([hops], gate_arrived[0], gate_oth[1])
    gate_arrived[1] = swap(gate_oth[1], "row")
    g2_rows = hops.rows()
    columns = w_out.shape[0] // 2
    grad_other = from_features((1 - core)[None], g2_rows, pieces_out, columns)[0]
    grad_from = swap(grad_other, "core")
    grad_mine = from_features(core[None], g2_rows, pieces_out, columns)[0]
    gate_own = [
        for_y(tokens_b, pair, True, gate_got, gate_arrived[0], at=0, first=0, count=1),
        None,
    ]
    out_sent = for_core(g2_rows, attended[None], False)
    grad_from, grad_mine, out_sent, gate_own[0], part_down, down_other = sync(
        [], grad_from, grad_mine, out_sent, gate_own[0], part_down, down_other
    )
    down_hops = Scatter(part_down, slots)
    gate_other = [y_swap(gate_own[0]), None]
    out_got = swap(out_sent, "core")
    mixed_mine, mixed_other, bias_part = attend_back(
        qkv_mine, qkv_from, grad_mine, grad_from, lse, rotary_mine, rotary_other, table_of, factor
    )
    mixed_mine, mixed_other, out_got, gate_arrived[1] = sync(
        [down_hops], mixed_mine, mixed_other, out_got, gate_arrived[1]
    )
    down_hops.hop()
    mixed_from = swap(mixed_other, "core")
    out_oth = for_row(g2_rows, attended[None], False, out_got)
    gate_own[1] = for_y(tokens_b, pair, True, gate_got, gate_arrived[1], at=1, first=1, count=1)
    mixed = jnp.concatenate(
        [
            jnp.where(core == 0, mixed_mine, mixed_from),
            jnp.where(core == 0, mixed_from, mixed_mine),
        ],
        axis=2,
    )
    in_sent = for_core(tokens_a, mixed, True)
    in_sent, mixed, gate_own[1], gate_other[0], out_oth = sync(
        [], in_sent, mixed, gate_own[1], gate_other[0], out_oth
    )
    in_got = swap(in_sent, "core")
    out_arrived = swap(out_oth, "row")
    gate_other[1] = y_swap(gate_own[1])
    part_a = to_features(mixed, pieces_in, True)
    part_a, in_got, out_arrived = sync([], part_a, in_got, out_arrived)
    hops = Scatter(part_a, slots)
    spans = (dict(at=0, first=0, count=2), dict(at=2, first=2, count=1))
    in_oth = [for_row(tokens_a, mixed, True, in_got, **span) for span in spans]
    in_arrived = [swap(x, "row") for x in in_oth]
    out_own = for_y(g2_rows, attended[None], False, out_got, out_arrived)
    *in_oth, out_own = sync([hops, down_hops], *in_oth, out_own)
    hops.hop()
    down_total = y_total(down_own, down_other)
    gate_total = [y_total(gate_own[0], gate_other[0]), None]
    in_arrived[0], gate_other[1], down_total, gate_total[0] = sync(
        [hops], in_arrived[0], gate_other[1], down_total, gate_total[0]
    )
    hops.hop()
    out_other_y = y_swap(out_own)
    in_own = [for_y(tokens_a, mixed, True, in_got, in_arrived[0], **spans[0])]
    gate_total[1] = y_total(gate_own[1], gate_other[1])
    in_own[0], gate_total[1], in_arrived[1], out_other_y = sync(
        [hops], in_own[0], gate_total[1], in_arrived[1], out_other_y
    )
    in_other = [y_swap(in_own[0])]
    input_low, sums_a = norm_back(stream, hops.terms(), g2, gain_a, 0)
    down_rest = swap(down_total, "core")
    gate_rest = [swap(x, "core") for x in gate_total]
    out_total = y_total(out_own, out_other_y)
    out_rest = swap(out_total, "core")
    in_own.append(for_y(tokens_a, mixed, True, in_got, in_arrived[1], **spans[1]))
    input_low, sums_a, in_own[1], down_rest, out_rest, *gate_rest = sync(
        [], input_low, sums_a, in_own[1], down_rest, out_rest, *gate_rest
    )

    bias_all = jnp.zeros((3, 2 * slots * columns), F32)
    bias_all = lax.dynamic_update_slice(
        bias_all, bias_part[:, 0, :], (jnp.int32(0), (place * 2 + core) * columns)
    ).reshape(-1, wide)
    sums = jnp.concatenate([sums_a, sums_b], axis=0)
    own, oth = sums[:, :wide], natural(sums[:, wide:])
    total = jnp.concatenate([own, bias_all, oth], axis=0)

    in_other.append(y_swap(in_own[1]))
    input_grad = from_sequence(input_low)
    down_grad = join(down_total, down_rest, 2)[0]
    if slots == 4:
        arrived = lax.ppermute(total, "col", PAIR)
        arrived, input_grad, down_grad = sync([], arrived, input_grad, down_grad)
        total = total + arrived
        arrived = sync([], lax.ppermute(total, "col", MID))
        total = total + arrived
        outer, in_other[0], gate_total[0] = sync(
            [], lax.ppermute(total, "col", OUT), in_other[0], gate_total[0]
        )
        total = jnp.where((place == 0) | (place == 3), outer, total)
        down_hops.flying = list(tie(down_hops.flying, outer))
        down_hops.hop()
        arrived = swap(total, "core")
        gate_grad = join_pairs(core[None], gate_total, gate_rest)
        arrived, gate_grad, in_other[1] = sync([down_hops], arrived, gate_grad, in_other[1])
        total = total + arrived
    else:
        gate_grad = join_pairs(core[None], gate_total, gate_rest)
        total = lax.psum(total, "col")
        total = total + swap(total, "core")
    cut = own.shape[0] + bias_all.shape[0]
    arrived = swap(jnp.concatenate([total[cut:], total[own.shape[0] : cut]], axis=0), "row")
    layer_low = (residual + sum(t.astype(F32) for t in down_hops.terms())).astype(BF16)
    in_total = [y_total(x, o) for x, o in zip(in_own, in_other)]
    in_rest = [swap(x, "core") for x in in_total]
    arrived, layer_low, *in_rest = sync([], arrived, layer_low, *in_rest)
    total = total[:cut] + arrived
    vectors = lax.psum(total, "y") if y_count != 2 else total + swap(total, "y")
    layer_out = from_sequence(layer_low)
    out_grad = join(out_total, out_rest, 2)[0]
    in_grad = jnp.concatenate([join(x, r, 1) for x, r in zip(in_total, in_rest)], axis=0)
    bias_grad = take(vectors[4:].reshape(3, -1), place * 2 * columns, 2 * columns, 1)
    input_grad = input_grad.astype(F32)
    return (
        layer_out[None],
        input_grad,
        vectors[0:1],
        vectors[1:2],
        jnp.transpose(in_grad, (1, 0, 2))[None],
        bias_grad[None],
        out_grad[None],
        vectors[2:3],
        vectors[3:4],
        gate_grad[None],
        down_grad[None],
    )


def solution(mesh):
    dp, rows, cols = (mesh.shape[a] for a in ("dp", "row", "col"))
    split = Mesh(mesh.devices.reshape(dp // 2, 2, rows, cols), ("y", "core", "row", "col"))
    tokens = ("y", "core", "col")
    return jax.shard_map(
        local,
        mesh=split,
        in_specs=(
            P(tokens, "row"),
            P(None, "row"),
            P(None, "row"),
            P(None, "row", None, "col"),
            P(None, None, "col"),
            P(None, "col", "row"),
            P(None, "row"),
            P(None, "row"),
            P(None, "row", None, "col"),
            P(None, "col", "row"),
            P(tokens, "row"),
        ),
        out_specs=(
            P(None, tokens, "row"),
            P(tokens, "row"),
            P(None, "row"),
            P(None, "row"),
            P(None, "row", None, "col"),
            P(None, None, "col"),
            P(None, "col", "row"),
            P(None, "row"),
            P(None, "row"),
            P(None, "row", None, "col"),
            P(None, "col", "row"),
        ),
        check_vma=False,
    )
```

```python
import functools
import math

import jax
import jax.numpy as jnp
from jax import lax
from jax.experimental import pallas as pl
from jax.experimental.pallas import tpu as pltpu
from jax.sharding import Mesh
from jax.sharding import PartitionSpec as P

HEAD_DIM = 64
ROT = 16
LENGTH = 1024
EPSILON = 1e-05
F32 = jnp.float32
BF16 = jnp.bfloat16
LANES = 128
MIB = 1 << 20


def swap(x, axis):
    return lax.ppermute(x, axis, [(0, 1), (1, 0)])


PAIR = [(0, 1), (1, 0), (2, 3), (3, 2)]
MID = [(1, 2), (2, 1)]
OUT = [(1, 0), (2, 3)]
IN = [(0, 1), (3, 2)]
ORDER4 = ((0, 1, 2, 3), (1, 0, 2, 3), (2, 3, 1, 0), (3, 2, 1, 0))


def slot_order(place, count):
    if count == 4:
        return jnp.array(ORDER4, jnp.int32)[place]
    return jnp.arange(count, dtype=jnp.int32)


def tie(values, *behind):
    return lax.optimization_barrier((tuple(values), behind))[0]


def after(x, *behind):
    return tie((x,), *behind)[0] if behind else x


class Gather:
    def __init__(self, own, count):
        self.own, self.count, self.got = own, count, []
        self.flying = []
        if count == 4:
            self.flying = [lax.ppermute(own, "col", PAIR), lax.ppermute(own, "col", MID)]

    def hop(self):
        if self.count != 4:
            return
        if not self.got:
            one, mid = self.flying
            self.got = [one, mid]
            self.flying = [lax.ppermute(one, "col", MID), lax.ppermute(mid, "col", OUT)]
        else:
            far, mid_out = self.flying
            self.got += [far, mid_out]
            self.flying = [lax.ppermute(far, "col", OUT)]

    def rows(self):
        if self.count != 4:
            return lax.all_gather(self.own, "col", axis=0, tiled=True)
        one, mid, far, mid_out = self.got
        return jnp.concatenate([self.own, one, mid + mid_out, far + self.flying[0]], axis=0)


class Scatter:
    def __init__(self, parts, count):
        self.count, self.step, self.parts = count, 0, parts
        self.flying, self.two = [], None
        if count == 4:
            rows = parts.shape[0] // count
            self.part = [parts[i * rows : (i + 1) * rows] for i in range(4)]
            self.flying = [lax.ppermute(self.part[3], "col", IN)]
            self.two = lax.ppermute(self.part[2], "col", IN)

    def hop(self):
        if self.count != 4:
            return
        if self.step == 0:
            three = self.part[3] + self.flying[0]
            self.flying = [lax.ppermute(three, "col", MID), self.two]
        else:
            one, two = self.part[1] + self.flying[0], self.part[2] + self.flying[1]
            self.flying = [lax.ppermute(one, "col", PAIR), lax.ppermute(two, "col", MID)]
        self.step += 1

    def terms(self):
        if self.count != 4:
            mine = lax.psum_scatter(self.parts, "col", scatter_dimension=0, tiled=True)
            return (mine, jnp.zeros_like(mine), jnp.zeros_like(mine))
        return (self.part[0], *self.flying)


def sync(moving, *values):
    flat = [x for m in moving for x in m.flying] + list(values)
    flat = list(lax.optimization_barrier(tuple(flat)))
    for m in moving:
        count = len(m.flying)
        m.flying, flat = flat[:count], flat[count:]
    return flat[0] if len(flat) == 1 else flat


def params(mib, axes=1):
    return pltpu.CompilerParams(
        vmem_limit_bytes=mib * MIB, dimension_semantics=("arbitrary",) * axes
    )


SHARE = 8


def cost(flops, moved, trans=0):
    return pl.CostEstimate(
        flops=int(flops / SHARE),
        bytes_accessed=int(moved / SHARE),
        transcendentals=int(trans / SHARE),
    )


def stats_of(value):
    width = value.shape[1]
    average = jnp.sum(value, axis=1, keepdims=True) / width
    centred = value - average
    variance = jnp.sum(centred * centred, axis=1, keepdims=True) / width
    inv_root = lax.rsqrt(variance + EPSILON)
    return centred * inv_root, inv_root


def norm_first(stream, gain, shift):
    rows, width = stream.shape
    block = rows // 4

    def body(x_ref, gain_ref, shift_ref, low_ref):
        xhat, unused = stats_of(x_ref[...].astype(F32))
        low_ref[...] = (xhat * gain_ref[...] + shift_ref[...]).astype(BF16)

    row = pl.BlockSpec((block, width), lambda i: (i, 0))
    flat = pl.BlockSpec((1, width), lambda i: (0, 0))
    return pl.pallas_call(
        body,
        grid=(4,),
        in_specs=[row, flat, flat],
        out_specs=row,
        out_shape=jax.ShapeDtypeStruct((rows, width), BF16),
        compiler_params=params(6),
        cost_estimate=cost(rows * width * 10, rows * width * 4),
        name="norm_first",
    )(stream, gain, shift)


def norm_second(stream, terms, gain, shift):
    rows, width = stream.shape
    block = rows // 4

    def body(x_ref, a_ref, b_ref, c_ref, gain_ref, shift_ref, res_ref, low_ref):
        residual = (
            x_ref[...].astype(F32)
            + a_ref[...].astype(F32)
            + b_ref[...].astype(F32)
            + c_ref[...].astype(F32)
        )
        res_ref[...] = residual
        xhat, unused = stats_of(residual)
        low_ref[...] = (xhat * gain_ref[...] + shift_ref[...]).astype(BF16)

    row = pl.BlockSpec((block, width), lambda i: (i, 0))
    flat = pl.BlockSpec((1, width), lambda i: (0, 0))
    return pl.pallas_call(
        body,
        grid=(4,),
        in_specs=[row] * 4 + [flat, flat],
        out_specs=[row, row],
        out_shape=[
            jax.ShapeDtypeStruct((rows, width), F32),
            jax.ShapeDtypeStruct((rows, width), BF16),
        ],
        compiler_params=params(6),
        cost_estimate=cost(rows * width * 12, rows * width * 14),
        name="norm_second",
    )(stream, *terms, gain, shift)


def norm_back(stream, terms, upper, gain, both):
    rows, width = stream.shape
    block = rows // 4

    def body(x_ref, a_ref, b_ref, c_ref, up_ref, gain_ref, low_ref, sums_ref, *full_ref):
        xhat, inv_root = stats_of(x_ref[...].astype(F32))
        grad = a_ref[...].astype(F32) + b_ref[...].astype(F32) + c_ref[...].astype(F32)
        scaled = grad * gain_ref[...]
        mean_scaled = jnp.sum(scaled, axis=1, keepdims=True) / width
        mean_cross = jnp.sum(scaled * xhat, axis=1, keepdims=True) / width
        result = up_ref[...].astype(F32) + inv_root * (scaled - mean_scaled - xhat * mean_cross)
        low_ref[...] = result.astype(BF16)
        if full_ref:
            full_ref[0][...] = result

        @pl.when(pl.program_id(0) == 0)
        def _():
            sums_ref[...] = jnp.zeros_like(sums_ref)

        sums_ref[...] += jnp.concatenate(
            [
                jnp.sum(grad * xhat, axis=0, keepdims=True),
                jnp.sum(grad, axis=0, keepdims=True),
            ],
            axis=0,
        )

    row = pl.BlockSpec((block, width), lambda i: (i, 0))
    flat = pl.BlockSpec((1, width), lambda i: (0, 0))
    sums = pl.BlockSpec((2, width), lambda i: (0, 0))
    return pl.pallas_call(
        body,
        grid=(4,),
        in_specs=[row] * 5 + [flat],
        out_specs=[row, sums] + [row] * both,
        out_shape=[
            jax.ShapeDtypeStruct((rows, width), BF16),
            jax.ShapeDtypeStruct((2, width), F32),
        ]
        + [jax.ShapeDtypeStruct((rows, width), F32)] * both,
        compiler_params=params(10),
        cost_estimate=cost(rows * width * 20, rows * width * 18),
        name="norm_back",
    )(stream, *terms, upper, gain)


def cuts_of(sizes):
    ends = [sum(sizes[: i + 1]) for i in range(len(sizes))]
    return [(end - size, end) for end, size in zip(ends, sizes)]


def roll_lanes(value, shift):
    return pltpu.roll(value, shift % value.shape[1], 1)


def turn(value, table, sign):
    times = value.shape[1] // LANES
    wide = [jnp.concatenate([table[i]] * times, axis=1) for i in range(3)]
    ahead = roll_lanes(value, -(ROT // 2))
    behind = roll_lanes(value, ROT // 2)
    moved = ahead * wide[1] + behind * wide[2]
    return value * wide[0] + (moved if sign > 0 else -moved)


def qkv_columns(tokens, pieces, bias, table, half):
    rows, width = tokens.shape
    columns = pieces[0].shape[2] // 2
    cuts = cuts_of([p.shape[1] for p in pieces])

    def body(half_ref, x_ref, *refs):
        bias_ref, table_ref, out_ref = refs[-3:]
        which = pl.program_id(0)
        acc = bias_ref[0]
        for w_ref, (low, high) in zip(refs, cuts):
            acc = acc + jnp.dot(x_ref[:, low:high], w_ref[0], preferred_element_type=F32)

        @pl.when(which < 2)
        def _():
            out_ref[0] = turn(acc, table_ref, 1).astype(BF16)

        @pl.when(which == 2)
        def _():
            out_ref[0] = acc.astype(BF16)

    return pl.pallas_call(
        body,
        grid_spec=pltpu.PrefetchScalarGridSpec(
            num_scalar_prefetch=1,
            grid=(3,),
            in_specs=[pl.BlockSpec((rows, width), lambda j, h: (0, 0))]
            + [pl.BlockSpec((1, p.shape[1], columns), lambda j, h: (j, 0, h[0])) for p in pieces]
            + [
                pl.BlockSpec((1, 1, columns), lambda j, h: (j, 0, h[0])),
                pl.BlockSpec((3, rows, LANES), lambda j, h: (0, 0, 0)),
            ],
            out_specs=pl.BlockSpec((1, rows, columns), lambda j, h: (j, 0, 0)),
        ),
        out_shape=jax.ShapeDtypeStruct((3, rows, columns), BF16),
        compiler_params=params(16),
        cost_estimate=cost(6 * rows * width * columns, 2 * (rows * width + 3 * columns * width)),
        name="qkv_columns",
    )(half, tokens, *pieces, bias, table)


def place_of(order_ref, slot, core, rows):
    return pl.multiple_of((order_ref[1 + slot] * 2 + core) * rows, rows)


CHUNK = 256


def score_chunk(query, key, first):
    scores = lax.dot_general(query, key, (((1,), (1,)), ((), ())), preferred_element_type=F32)
    last = scores[:, first:]
    at_query = lax.broadcasted_iota(jnp.int32, last.shape, 0)
    at_key = lax.broadcasted_iota(jnp.int32, last.shape, 1)
    last = jnp.where(at_query >= at_key, last, -jnp.inf)
    return last if first == 0 else jnp.concatenate([scores[:, :first], last], axis=1)


def attend(mine, other, order, factor):
    unused, rows, columns = mine.shape
    slots = order.shape[0] - 1
    piece = rows // slots
    length = 2 * rows

    def body(order_ref, mine_ref, other_ref, out_mine, out_other, lse_ref, whole, result):
        core = order_ref[0]
        for slot in range(slots):
            here = slice(slot * piece, (slot + 1) * piece)
            whole[:, pl.ds(place_of(order_ref, slot, core, piece), piece), :] = mine_ref[:, here, :]
            whole[:, pl.ds(place_of(order_ref, slot, 1 - core, piece), piece), :] = other_ref[
                :, here, :
            ]
        for head in range(LANES // HEAD_DIM):
            lanes = slice(head * HEAD_DIM, (head + 1) * HEAD_DIM)
            for first in range(0, length, CHUNK):
                upto = first + CHUNK
                query = whole[0, first:upto, lanes] * jnp.bfloat16(factor)
                scores = score_chunk(query, whole[1, :upto, lanes], first)
                highest = jnp.max(scores, axis=1, keepdims=True)
                exponent = jnp.exp(scores - highest)
                summed = jnp.sum(exponent, axis=1, keepdims=True)
                mixed = jnp.dot(
                    exponent.astype(BF16), whole[2, :upto, lanes], preferred_element_type=F32
                )
                result[first:upto, lanes] = (mixed * (1.0 / summed)).astype(BF16)
                lse_ref[0, first:upto, head : head + 1] = highest + jnp.log(summed)
        for slot in range(slots):
            here = slice(slot * piece, (slot + 1) * piece)
            out_mine[here, :] = result[pl.ds(place_of(order_ref, slot, core, piece), piece), :]
            out_other[here, :] = result[pl.ds(place_of(order_ref, slot, 1 - core, piece), piece), :]

    groups = columns // LANES
    three = pl.BlockSpec((3, rows, LANES), lambda g, o: (0, 0, g))
    one = pl.BlockSpec((rows, LANES), lambda g, o: (0, g))
    return pl.pallas_call(
        body,
        grid_spec=pltpu.PrefetchScalarGridSpec(
            num_scalar_prefetch=1,
            grid=(groups,),
            in_specs=[three, three],
            out_specs=[one, one, pl.BlockSpec((1, length, 2), lambda g, o: (g, 0, 0))],
            scratch_shapes=[
                pltpu.VMEM((3, length, LANES), BF16),
                pltpu.VMEM((length, LANES), BF16),
            ],
        ),
        out_shape=[
            jax.ShapeDtypeStruct((rows, columns), BF16),
            jax.ShapeDtypeStruct((rows, columns), BF16),
            jax.ShapeDtypeStruct((groups, length, 2), F32),
        ],
        compiler_params=params(20),
        cost_estimate=cost(
            4 * length * length * columns, 16 * rows * columns, columns * length * length / 128
        ),
        name="attend",
    )(order, mine, other)


def attend_back(mine, other, grad_mine, grad_other, lse, table_mine, table_other, order, factor):
    unused, rows, columns = mine.shape
    slots = order.shape[0] - 1
    piece = rows // slots
    length = 2 * rows
    across = (((1,), (1,)), ((), ()))
    down = (((0,), (0,)), ((), ()))

    def body(
        order_ref,
        mine_ref,
        other_ref,
        gm_ref,
        go_ref,
        lse_ref,
        tm_ref,
        to_ref,
        out_mine,
        out_other,
        bias_ref,
        whole,
        grads,
        dq_ref,
        dkv_ref,
    ):
        core = order_ref[0]
        for slot in range(slots):
            here = slice(slot * piece, (slot + 1) * piece)
            one = pl.ds(place_of(order_ref, slot, core, piece), piece)
            two = pl.ds(place_of(order_ref, slot, 1 - core, piece), piece)
            whole[:, one, :] = mine_ref[:, here, :]
            whole[:, two, :] = other_ref[:, here, :]
            grads[one, :] = gm_ref[here, :]
            grads[two, :] = go_ref[here, :]
        heads = LANES // HEAD_DIM
        for head in range(heads):
            lanes = slice(head * HEAD_DIM, (head + 1) * HEAD_DIM)
            for first in reversed(range(0, length, CHUNK)):
                upto = first + CHUNK
                query = whole[0, first:upto, lanes] * jnp.bfloat16(factor)
                key = whole[1, :upto, lanes]
                value = whole[2, :upto, lanes]
                grad = grads[first:upto, lanes]
                scores = score_chunk(query, key, first)
                probs = jnp.exp(scores - lse_ref[0, first:upto, head : head + 1])
                probs_grad = lax.dot_general(grad, value, across, preferred_element_type=F32)
                shift = jnp.sum(probs * probs_grad, axis=1, keepdims=True)
                scores_grad = (probs * (probs_grad - shift)).astype(BF16)
                dq_ref[first:upto, lanes] = (
                    jnp.dot(scores_grad, key, preferred_element_type=F32) * factor
                )
                dk = lax.dot_general(scores_grad, query, down, preferred_element_type=F32)
                dv = lax.dot_general(
                    probs.astype(BF16), grad, down, preferred_element_type=F32
                )
                if upto == length:
                    dkv_ref[0, :, lanes] = dk
                    dkv_ref[1, :, lanes] = dv
                else:
                    dkv_ref[0, :upto, lanes] += dk
                    dkv_ref[1, :upto, lanes] += dv
        total = [jnp.zeros((1, LANES), F32) for _ in range(3)]
        for slot in range(slots):
            here = slice(slot * piece, (slot + 1) * piece)
            for at, table, out in (
                (core, tm_ref, out_mine),
                (1 - core, to_ref, out_other),
            ):
                rows_at = pl.ds(place_of(order_ref, slot, at, piece), piece)
                angles = table[:, here, :]
                parts = (
                    turn(dq_ref[rows_at, :], angles, -1).astype(BF16),
                    turn(dkv_ref[0, rows_at, :], angles, -1).astype(BF16),
                    dkv_ref[1, rows_at, :].astype(BF16),
                )
                for i in range(3):
                    out[i, here, :] = parts[i]
                    total[i] += jnp.sum(parts[i].astype(F32), axis=0, keepdims=True)
        for i in range(3):
            bias_ref[i] = total[i]

    groups = columns // LANES
    three = pl.BlockSpec((3, rows, LANES), lambda g, o: (0, 0, g))
    one = pl.BlockSpec((rows, LANES), lambda g, o: (0, g))
    full = pl.BlockSpec((3, rows, LANES), lambda g, o: (0, 0, 0))
    return pl.pallas_call(
        body,
        grid_spec=pltpu.PrefetchScalarGridSpec(
            num_scalar_prefetch=1,
            grid=(groups,),
            in_specs=[
                three,
                three,
                one,
                one,
                pl.BlockSpec((1, length, 2), lambda g, o: (g, 0, 0)),
                full,
                full,
            ],
            out_specs=[three, three, pl.BlockSpec((3, 1, LANES), lambda g, o: (0, 0, g))],
            scratch_shapes=[
                pltpu.VMEM((3, length, LANES), BF16),
                pltpu.VMEM((length, LANES), BF16),
                pltpu.VMEM((length, LANES), F32),
                pltpu.VMEM((2, length, LANES), F32),
            ],
        ),
        out_shape=[
            jax.ShapeDtypeStruct((3, rows, columns), BF16),
            jax.ShapeDtypeStruct((3, rows, columns), BF16),
            jax.ShapeDtypeStruct((3, 1, columns), F32),
        ],
        compiler_params=params(20),
        cost_estimate=cost(
            10 * length * length * columns, 40 * rows * columns, columns * length * length / 128
        ),
        name="attend_back",
    )(order, mine, other, grad_mine, grad_other, lse, table_mine, table_other)


ACROSS = (((1,), (1,)), ((), ()))
DOWN = (((0,), (0,)), ((), ()))


def feed_forward(tokens, pieces, hidden_grad):
    rows, width = tokens.shape
    units = pieces[0].shape[2]
    block = 256 if units > 256 else units
    cuts = cuts_of([p.shape[1] for p in pieces])

    def body(x_ref, *refs):
        hg_ref, hidden_ref, grad_ref = refs[-3:]
        gate_up = 0.0
        for w_ref, (low, high) in zip(refs, cuts):
            both = jnp.concatenate([w_ref[0], w_ref[1]], axis=1)
            gate_up += jnp.dot(x_ref[:, low:high], both, preferred_element_type=F32)
        gate, up = gate_up[:, :block], gate_up[:, block:]
        sigma = jax.nn.sigmoid(gate)
        silu = gate * sigma
        hidden_ref[...] = (silu * up).astype(BF16)
        grad = hg_ref[...].astype(F32)
        grad_ref[0] = (grad * up * (sigma + silu * (1.0 - sigma))).astype(BF16)
        grad_ref[1] = (grad * silu).astype(BF16)

    return pl.pallas_call(
        body,
        grid=(pl.cdiv(units, block),),
        in_specs=[pl.BlockSpec((rows, width), lambda j: (0, 0))]
        + [pl.BlockSpec((2, p.shape[1], block), lambda j: (0, 0, j)) for p in pieces]
        + [pl.BlockSpec((rows, block), lambda j: (0, j))],
        out_specs=[
            pl.BlockSpec((rows, block), lambda j: (0, j)),
            pl.BlockSpec((2, rows, block), lambda j: (0, 0, j)),
        ],
        out_shape=[
            jax.ShapeDtypeStruct((rows, units), BF16),
            jax.ShapeDtypeStruct((2, rows, units), BF16),
        ],
        compiler_params=params(20),
        cost_estimate=cost(
            4 * rows * width * units, 4 * width * units + 2 * rows * width, rows * units
        ),
        name="feed_forward",
    )(tokens, *pieces, hidden_grad)


def to_features(values, pieces, across):
    count, rows, units = values.shape
    axis = 1 if across else 2
    sizes = [p.shape[axis] for p in pieces]
    block = sizes[-1]
    width = sum(sizes)
    owner = [i for i, size in enumerate(sizes) for _ in range(size // block)]
    starts = [owner.index(i) for i in range(len(pieces))]
    dims = ACROSS if across else (((1,), (0,)), ((), ()))

    def body(v_ref, *refs):
        step = pl.program_id(0)
        for i, w_ref in enumerate(refs[:-1]):

            @pl.when((step >= starts[i]) & (step < starts[i] + sizes[i] // block))
            def _():
                total = 0.0
                for n in range(count):
                    total += lax.dot_general(v_ref[n], w_ref[n], dims, preferred_element_type=F32)
                refs[-1][...] = total.astype(BF16)

    def spec(i):
        last = sizes[i] // block - 1
        at = lambda j: jnp.clip(j - starts[i], 0, last)
        if across:
            return pl.BlockSpec((count, block, units), lambda j: (0, at(j), 0))
        return pl.BlockSpec((count, units, block), lambda j: (0, 0, at(j)))

    return pl.pallas_call(
        body,
        grid=(width // block,),
        in_specs=[pl.BlockSpec((count, rows, units), lambda j: (0, 0, 0))]
        + [spec(i) for i in range(len(pieces))],
        out_specs=pl.BlockSpec((rows, block), lambda j: (0, j)),
        out_shape=jax.ShapeDtypeStruct((rows, width), BF16),
        compiler_params=params(32),
        cost_estimate=cost(
            2 * count * rows * width * units, 2 * count * (width + rows) * units + 2 * rows * width
        ),
        name="to_features",
    )(values, *pieces)


def from_features(index, tokens, pieces, block):
    rows, width = tokens.shape
    cuts = cuts_of([p.shape[1] for p in pieces])
    count = index.shape[0]

    def body(index_ref, x_ref, *refs):
        total = 0.0
        for w_ref, (low, high) in zip(refs, cuts):
            total += lax.dot_general(
                x_ref[:, low:high], w_ref[...], ACROSS, preferred_element_type=F32
            )
        refs[-1][0] = total.astype(BF16)

    out = pl.pallas_call(
        body,
        grid_spec=pltpu.PrefetchScalarGridSpec(
            num_scalar_prefetch=1,
            grid=(count,),
            in_specs=[pl.BlockSpec((rows, width), lambda j, q: (0, 0))]
            + [pl.BlockSpec((block, p.shape[1]), lambda j, q: (q[j], 0)) for p in pieces],
            out_specs=pl.BlockSpec((1, rows, block), lambda j, q: (j, 0, 0)),
        ),
        out_shape=jax.ShapeDtypeStruct((count, rows, block), BF16),
        compiler_params=params(16),
        cost_estimate=cost(
            2 * rows * width * block * count, 2 * width * (rows + block * count)
        ),
        name="from_features",
    )(index, tokens, *pieces)
    return out


def grad_quarters(quarters, tokens, others, adds, rows_first, first=0, count=None):
    rows, width = tokens.shape
    units = others.shape[2]
    count = others.shape[0] if count is None else count
    quarter = width // 4
    k = quarters.shape[0]
    form = (quarter, units) if rows_first else (units, quarter)

    def body(q_ref, x_ref, y_ref, *refs):
        x, y = x_ref[...], y_ref[0]
        left, right = (x, y) if rows_first else (y, x)
        total = lax.dot_general(left, right, DOWN, preferred_element_type=F32)
        for ref in refs[:-1]:
            total += ref[0, 0].astype(F32)
        refs[-1][0, 0] = total.astype(BF16)

    def shifted(at_k, at_n):
        return pl.BlockSpec((1, 1, *form), lambda i, j, q: (i + at_k, j + at_n, 0, 0))

    return pl.pallas_call(
        body,
        grid_spec=pltpu.PrefetchScalarGridSpec(
            num_scalar_prefetch=1,
            grid=(k, count),
            in_specs=[
                pl.BlockSpec((rows, quarter), lambda i, j, q: (0, q[i])),
                pl.BlockSpec((1, rows, units), lambda i, j, q: (j + first, 0, 0)),
            ]
            + [shifted(at_k, at_n) for unused, at_k, at_n in adds],
            out_specs=shifted(0, 0),
        ),
        out_shape=jax.ShapeDtypeStruct((k, count, *form), BF16),
        compiler_params=params(20, 2),
        cost_estimate=cost(
            2 * k * count * rows * quarter * units,
            2 * k * count * quarter * units * (1 + len(adds)) + 2 * rows * (width + count * units),
        ),
        name="grad_quarters",
    )(quarters, tokens, others, *[add[0] for add in adds])


def join_pairs(core, parts, rests):
    rows, units = parts[0].shape[1:]
    block = 128 if rows % 128 == 0 else rows
    steps = rows // block

    def body(core_ref, *refs):
        half = pl.program_id(0)
        out_ref = refs[-1]
        for i in range(2):

            @pl.when(half == core_ref[0])
            def _():
                out_ref[:, i, :] = refs[i][0].astype(F32)

            @pl.when(half != core_ref[0])
            def _():
                out_ref[:, i, :] = refs[2 + i][0].astype(F32)

    def spec(same):
        def at(h, j, c):
            wanted = (h == c[0]) if same else (h != c[0])
            return (0, jnp.where(wanted, j, 0), 0)

        return pl.BlockSpec((1, block, units), at)

    return pl.pallas_call(
        body,
        grid_spec=pltpu.PrefetchScalarGridSpec(
            num_scalar_prefetch=1,
            grid=(2, steps),
            in_specs=[spec(True), spec(True), spec(False), spec(False)],
            out_specs=pl.BlockSpec((block, 2, units), lambda h, j, c: (h * steps + j, 0, 0)),
        ),
        out_shape=jax.ShapeDtypeStruct((2 * rows, 2, units), F32),
        compiler_params=params(16, 2),
        cost_estimate=cost(rows * units, 24 * rows * units),
        name="join_pairs",
    )(core, *parts, *rests)


def rotary_table(position):
    half = ROT // 2
    lane = jnp.arange(LANES) % HEAD_DIM
    frequency = 10000.0 ** (-((lane % half).astype(F32) * 2.0 / ROT))
    angles = position.astype(F32)[:, None] * frequency[None, :]
    lane = lane[None, :]
    cosine = jnp.where(lane < ROT, jnp.cos(angles), 1.0)
    sine = jnp.sin(angles)
    return jnp.stack(
        [
            cosine,
            jnp.where(lane < half, -sine, 0.0),
            jnp.where((lane >= half) & (lane < ROT), sine, 0.0),
        ]
    )


def local(
    inputs,
    first_gain,
    first_shift,
    project_in,
    project_bias,
    project_out,
    second_gain,
    second_shift,
    gate_weight,
    down_weight,
    cotangent,
):
    y_count = lax.axis_size("y")
    slots = lax.axis_size("col")
    y = lax.axis_index("y")
    core = lax.axis_index("core")
    row = lax.axis_index("row")
    place = lax.axis_index("col")
    factor = 1.0 / math.sqrt(HEAD_DIM)
    half_rows = inputs.shape[0] // 2
    wide = inputs.shape[1]
    width = 2 * wide

    def take(x, start, size, axis):
        return lax.dynamic_slice_in_dim(x, start, size, axis)

    straight = [(0, 0), (1, 2), (2, 1), (3, 3)]
    crossed = [(0, 2), (1, 0), (2, 3), (3, 1)]
    aligned = core == row

    def order_features(own, oth):
        low, high = oth[..., : wide // 2], oth[..., wide // 2 :]
        return jnp.concatenate(
            [own, jnp.where(core == 0, low, high), jnp.where(core == 0, high, low)], axis=-1
        )

    def natural(oth):
        low, high = oth[..., : wide // 2], oth[..., wide // 2 :]
        return jnp.concatenate(
            [jnp.where(core == 0, low, high), jnp.where(core == 0, high, low)], axis=-1
        )

    def to_sequence(x):
        a = lax.ppermute(take(x, row * half_rows, half_rows, 0), ("core", "row"), straight)
        b = lax.ppermute(take(x, (1 - row) * half_rows, half_rows, 0), ("core", "row"), crossed)
        return order_features(jnp.where(aligned, a, b), jnp.where(aligned, b, a))

    def from_sequence(x):
        own, oth = x[:, :wide], natural(x[:, wide:])
        a = jnp.where(aligned, own, oth)
        b = jnp.where(aligned, oth, own)
        a = lax.ppermute(a, ("core", "row"), [(j, i) for i, j in straight])
        b = lax.ppermute(b, ("core", "row"), [(j, i) for i, j in crossed])
        top = jnp.where(row == 0, a, b)
        bottom = jnp.where(row == 0, b, a)
        return jnp.concatenate([top, bottom], axis=0)

    order = slot_order(place, slots)
    table_of = jnp.concatenate([core[None], order]).astype(jnp.int32)
    inside = jnp.arange(half_rows)
    position = lambda c: ((order[:, None] * 2 + c) * half_rows + inside[None, :]).reshape(-1)
    rotary_mine = rotary_table(position(core))
    rotary_other = rotary_table(position(1 - core))

    stream = to_sequence(inputs)
    vectors = jnp.concatenate([first_gain, first_shift, second_gain, second_shift], axis=0)
    vectors = order_features(vectors, swap(vectors, "row"))
    gain_a, shift_a, gain_b, shift_b = (vectors[i : i + 1] for i in range(4))

    def part_of(w, axis):
        part = w.shape[axis] // 2
        return take(w, core * part, part, axis)

    w_in = jnp.transpose(project_in[0], (1, 0, 2))
    w_out, w_down = project_out[0], down_weight[0]
    w_gate = jnp.transpose(gate_weight[0], (1, 0, 2))
    fixed = 0 * core

    def quarters(*q):
        return jnp.stack(q).astype(jnp.int32)

    def for_core(tokens, others, rows_first, **span):
        return grad_quarters(quarters(1 - core, 3 + fixed), tokens, others, (), rows_first, **span)

    def for_row(tokens, others, rows_first, got, at=0, **span):
        return grad_quarters(
            quarters(2 + fixed), tokens, others, ((got, 1, at),), rows_first, **span
        )

    def for_y(tokens, others, rows_first, got, arrived, at=0, **span):
        adds = ((got, 0, at), (arrived, 0, 0))
        return grad_quarters(quarters(core), tokens, others, adds, rows_first, **span)[0]

    def y_swap(own):
        return swap(own, "y") if y_count == 2 else lax.psum(own, "y")

    def y_total(own, other):
        return (own.astype(F32) + other.astype(F32)).astype(BF16) if y_count == 2 else other

    def join(total, rest, axis):
        return jnp.concatenate(
            [jnp.where(core == 0, total, rest), jnp.where(core == 0, rest, total)], axis=axis
        ).astype(F32)

    low_a = norm_first(stream, gain_a, shift_a)
    in_half = swap(after(part_of(w_in, 1), stream), "row")
    cot = to_sequence(after(cotangent, low_a))
    hops = Gather(low_a, slots)
    rotary_mine = sync([hops], rotary_mine)
    hops.hop()
    rotary_other, out_part, down_part = sync(
        [hops], rotary_other, part_of(w_out, 1), part_of(w_down, 1)
    )
    hops.hop()
    out_half = swap(out_part, "row")
    w_gate, gate_part, in_half, cot = sync([hops], w_gate, part_of(w_gate, 1), in_half, cot)
    tokens_a = hops.rows()
    pieces_in = (w_in, in_half, swap(in_half, "core"))
    cot_hops = Gather(cot, slots)
    down_half = swap(after(down_part, cot), "row")
    bias = project_bias[0][:, None, :]
    qkv_other = qkv_columns(tokens_a, pieces_in, bias, rotary_mine, (1 - core)[None])
    qkv_from = swap(qkv_other, "core")
    qkv_mine = qkv_columns(tokens_a, pieces_in, bias, rotary_mine, core[None])
    out_mine, out_other, lse = attend(qkv_mine, qkv_from, table_of, factor)
    out_mine, out_other, out_half = sync([cot_hops], out_mine, out_other, out_half)
    cot_hops.hop()
    pieces_out = (w_out, out_half, swap(out_half, "core"))
    out_from = swap(out_other, "core")
    attended = jnp.concatenate(
        [jnp.where(core == 0, out_mine, out_from), jnp.where(core == 0, out_from, out_mine)], axis=1
    )
    part_out = to_features(attended[None], [p[None] for p in pieces_out], False)
    part_out, gate_part = sync([], part_out, gate_part)
    hops = Scatter(part_out, slots)
    down_half = sync([hops, cot_hops], down_half)
    hops.hop()
    cot_hops.hop()
    gate_half = swap(after(gate_part, down_half), "row")
    down_rest = sync([hops, cot_hops], swap(down_half, "core"))
    hops.hop()
    pieces_down = (w_down, down_half, down_rest)
    units = w_down.shape[0]
    ways = 2 if units % 32 == 0 else 1
    grad_rows = cot_hops.rows()
    hidden_grad = from_features(
        jnp.arange(ways, dtype=jnp.int32), grad_rows, pieces_down, units // ways
    )
    hidden_grad = jnp.concatenate([hidden_grad[i] for i in range(ways)], axis=1)
    grad_rows, hidden_grad = sync([hops], grad_rows, hidden_grad)
    residual, low_b = norm_second(stream, hops.terms(), gain_b, shift_b)

    hops = Gather(low_b, slots)
    sync([hops], low_b)
    hops.hop()
    gate_half = sync([hops], gate_half)
    hops.hop()
    gate_half, gate_rest = sync([hops], gate_half, swap(gate_half, "core"))
    tokens_b = hops.rows()
    pieces_gate = (w_gate, gate_half, gate_rest)
    hidden, pair = feed_forward(tokens_b, pieces_gate, hidden_grad)
    part_b = to_features(pair, pieces_gate, True)
    part_b, hidden, pair = sync([], part_b, hidden, pair)

    hops = Scatter(part_b, slots)
    down_sent = for_core(grad_rows, hidden[None], False)
    gate_sent = for_core(tokens_b, pair, True)
    down_sent, gate_sent = sync([hops], down_sent, gate_sent)
    hops.hop()
    down_got = swap(down_sent, "core")
    gate_got = swap(gate_sent, "core")
    down_oth = for_row(grad_rows, hidden[None], False, down_got)
    down_oth, gate_got = sync([hops], down_oth, gate_got)
    hops.hop()
    down_arrived = swap(down_oth, "row")
    gate_oth = [
        for_row(tokens_b, pair, True, gate_got, at=i, first=i, count=1) for i in range(2)
    ]
    gate_oth = list(sync([hops], *gate_oth))
    g2_low, sums_b, g2 = norm_back(residual, hops.terms(), cot, gain_b, 1)

    hops = Gather(g2_low, slots)
    gate_arrived = [swap(gate_oth[0], "row"), None]
    part_down = to_features(hidden[None], [p[None] for p in pieces_down], False)
    part_down, down_arrived = sync([hops], part_down, down_arrived)
    hops.hop()
    down_own = for_y(grad_rows, hidden[None], False, down_got, down_arrived)
    down_own, part_down = sync([hops], down_own, part_down)
    hops.hop()
    down_other = y_swap(down_own)
    gate_arrived[0], gate_oth[1] = sync([hops], gate_arrived[0], gate_oth[1])
    gate_arrived[1] = swap(gate_oth[1], "row")
    g2_rows = hops.rows()
    columns = w_out.shape[0] // 2
    grad_other = from_features((1 - core)[None], g2_rows, pieces_out, columns)[0]
    grad_from = swap(grad_other, "core")
    grad_mine = from_features(core[None], g2_rows, pieces_out, columns)[0]
    gate_own = [
        for_y(tokens_b, pair, True, gate_got, gate_arrived[0], at=0, first=0, count=1),
        None,
    ]
    out_sent = for_core(g2_rows, attended[None], False)
    grad_from, grad_mine, out_sent, gate_own[0], part_down, down_other = sync(
        [], grad_from, grad_mine, out_sent, gate_own[0], part_down, down_other
    )
    down_hops = Scatter(part_down, slots)
    gate_other = [y_swap(gate_own[0]), None]
    out_got = swap(out_sent, "core")
    mixed_mine, mixed_other, bias_part = attend_back(
        qkv_mine, qkv_from, grad_mine, grad_from, lse, rotary_mine, rotary_other, table_of, factor
    )
    mixed_mine, mixed_other, out_got, gate_arrived[1] = sync(
        [down_hops], mixed_mine, mixed_other, out_got, gate_arrived[1]
    )
    down_hops.hop()
    mixed_from = swap(mixed_other, "core")
    out_oth = for_row(g2_rows, attended[None], False, out_got)
    gate_own[1] = for_y(tokens_b, pair, True, gate_got, gate_arrived[1], at=1, first=1, count=1)
    mixed = jnp.concatenate(
        [
            jnp.where(core == 0, mixed_mine, mixed_from),
            jnp.where(core == 0, mixed_from, mixed_mine),
        ],
        axis=2,
    )
    in_sent = for_core(tokens_a, mixed, True)
    part_a = to_features(mixed, pieces_in, True)
    part_a, in_sent, mixed, gate_own[1], gate_other[0], out_oth = sync(
        [], part_a, in_sent, mixed, gate_own[1], gate_other[0], out_oth
    )
    in_got = swap(in_sent, "core")
    out_arrived = swap(out_oth, "row")
    gate_other[1] = y_swap(gate_own[1])
    part_a, in_got, out_arrived = sync([], part_a, in_got, out_arrived)
    hops = Scatter(part_a, slots)
    spans = (dict(at=0, first=0, count=2), dict(at=2, first=2, count=1))
    in_oth = [for_row(tokens_a, mixed, True, in_got, **span) for span in spans]
    in_arrived = [swap(x, "row") for x in in_oth]
    out_own = for_y(g2_rows, attended[None], False, out_got, out_arrived)
    *in_oth, out_own = sync([hops, down_hops], *in_oth, out_own)
    hops.hop()
    down_total = y_total(down_own, down_other)
    gate_total = [y_total(gate_own[0], gate_other[0]), None]
    in_arrived[0], gate_other[1], down_total, gate_total[0] = sync(
        [hops], in_arrived[0], gate_other[1], down_total, gate_total[0]
    )
    hops.hop()
    out_other_y = y_swap(out_own)
    in_own = [for_y(tokens_a, mixed, True, in_got, in_arrived[0], **spans[0])]
    gate_total[1] = y_total(gate_own[1], gate_other[1])
    in_own[0], gate_total[1], in_arrived[1], out_other_y = sync(
        [hops], in_own[0], gate_total[1], in_arrived[1], out_other_y
    )
    in_other = [y_swap(in_own[0])]
    input_low, sums_a = norm_back(stream, hops.terms(), g2, gain_a, 0)
    down_rest = swap(down_total, "core")
    gate_rest = [swap(x, "core") for x in gate_total]
    out_total = y_total(out_own, out_other_y)
    out_rest = swap(out_total, "core")
    in_own.append(for_y(tokens_a, mixed, True, in_got, in_arrived[1], **spans[1]))
    input_low, sums_a, in_own[1], down_rest, out_rest, *gate_rest = sync(
        [], input_low, sums_a, in_own[1], down_rest, out_rest, *gate_rest
    )

    bias_all = jnp.zeros((3, 2 * slots * columns), F32)
    bias_all = lax.dynamic_update_slice(
        bias_all, bias_part[:, 0, :], (jnp.int32(0), (place * 2 + core) * columns)
    ).reshape(-1, wide)
    sums = jnp.concatenate([sums_a, sums_b], axis=0)
    own, oth = sums[:, :wide], natural(sums[:, wide:])
    total = jnp.concatenate([own, bias_all, oth], axis=0)

    in_other.append(y_swap(in_own[1]))
    input_grad = from_sequence(input_low)
    down_grad = join(down_total, down_rest, 2)[0]
    if slots == 4:
        arrived = lax.ppermute(total, "col", PAIR)
        arrived, input_grad, down_grad = sync([], arrived, input_grad, down_grad)
        total = total + arrived
        arrived = sync([], lax.ppermute(total, "col", MID))
        total = total + arrived
        outer, in_other[0], gate_total[0] = sync(
            [], lax.ppermute(total, "col", OUT), in_other[0], gate_total[0]
        )
        total = jnp.where((place == 0) | (place == 3), outer, total)
        down_hops.flying = list(tie(down_hops.flying, outer))
        down_hops.hop()
        arrived = swap(total, "core")
        gate_grad = join_pairs(core[None], gate_total, gate_rest)
        arrived, gate_grad, in_other[1] = sync([down_hops], arrived, gate_grad, in_other[1])
        total = total + arrived
    else:
        gate_grad = join_pairs(core[None], gate_total, gate_rest)
        total = lax.psum(total, "col")
        total = total + swap(total, "core")
    cut = own.shape[0] + bias_all.shape[0]
    arrived = swap(jnp.concatenate([total[cut:], total[own.shape[0] : cut]], axis=0), "row")
    layer_low = (residual + sum(t.astype(F32) for t in down_hops.terms())).astype(BF16)
    in_total = [y_total(x, o) for x, o in zip(in_own, in_other)]
    in_rest = [swap(x, "core") for x in in_total]
    arrived, layer_low, *in_rest = sync([], arrived, layer_low, *in_rest)
    total = total[:cut] + arrived
    vectors = lax.psum(total, "y") if y_count != 2 else total + swap(total, "y")
    layer_out = from_sequence(layer_low)
    out_grad = join(out_total, out_rest, 2)[0]
    in_grad = jnp.concatenate([join(x, r, 1) for x, r in zip(in_total, in_rest)], axis=0)
    bias_grad = take(vectors[4:].reshape(3, -1), place * 2 * columns, 2 * columns, 1)
    input_grad = input_grad.astype(F32)
    return (
        layer_out[None],
        input_grad,
        vectors[0:1],
        vectors[1:2],
        jnp.transpose(in_grad, (1, 0, 2))[None],
        bias_grad[None],
        out_grad[None],
        vectors[2:3],
        vectors[3:4],
        gate_grad[None],
        down_grad[None],
    )


def solution(mesh):
    dp, rows, cols = (mesh.shape[a] for a in ("dp", "row", "col"))
    split = Mesh(mesh.devices.reshape(dp // 2, 2, rows, cols), ("y", "core", "row", "col"))
    tokens = ("y", "core", "col")
    return jax.shard_map(
        local,
        mesh=split,
        in_specs=(
            P(tokens, "row"),
            P(None, "row"),
            P(None, "row"),
            P(None, "row", None, "col"),
            P(None, None, "col"),
            P(None, "col", "row"),
            P(None, "row"),
            P(None, "row"),
            P(None, "row", None, "col"),
            P(None, "col", "row"),
            P(tokens, "row"),
        ),
        out_specs=(
            P(None, tokens, "row"),
            P(tokens, "row"),
            P(None, "row"),
            P(None, "row"),
            P(None, "row", None, "col"),
            P(None, None, "col"),
            P(None, "col", "row"),
            P(None, "row"),
            P(None, "row"),
            P(None, "row", None, "col"),
            P(None, "col", "row"),
        ),
        check_vma=False,
    )
```

```python
import functools
import math

import jax
import jax.numpy as jnp
from jax import lax
from jax.experimental import pallas as pl
from jax.experimental.pallas import tpu as pltpu
from jax.sharding import Mesh
from jax.sharding import PartitionSpec as P

HEAD_DIM = 64
ROT = 16
LENGTH = 1024
EPSILON = 1e-05
F32 = jnp.float32
BF16 = jnp.bfloat16
LANES = 128
MIB = 1 << 20


def swap(x, axis):
    return lax.ppermute(x, axis, [(0, 1), (1, 0)])


PAIR = [(0, 1), (1, 0), (2, 3), (3, 2)]
MID = [(1, 2), (2, 1)]
OUT = [(1, 0), (2, 3)]
IN = [(0, 1), (3, 2)]
ORDER4 = ((0, 1, 2, 3), (1, 0, 2, 3), (2, 3, 1, 0), (3, 2, 1, 0))


def slot_order(place, count):
    if count == 4:
        return jnp.array(ORDER4, jnp.int32)[place]
    return jnp.arange(count, dtype=jnp.int32)


def tie(values, *behind):
    return lax.optimization_barrier((tuple(values), behind))[0]


def after(x, *behind):
    return tie((x,), *behind)[0] if behind else x


class Gather:
    def __init__(self, own, count):
        self.own, self.count, self.got = own, count, []
        self.flying = []
        if count == 4:
            self.flying = [lax.ppermute(own, "col", PAIR), lax.ppermute(own, "col", MID)]

    def hop(self):
        if self.count != 4:
            return
        if not self.got:
            one, mid = self.flying
            self.got = [one, mid]
            self.flying = [lax.ppermute(one, "col", MID), lax.ppermute(mid, "col", OUT)]
        else:
            far, mid_out = self.flying
            self.got += [far, mid_out]
            self.flying = [lax.ppermute(far, "col", OUT)]

    def rows(self):
        if self.count != 4:
            return lax.all_gather(self.own, "col", axis=0, tiled=True)
        one, mid, far, mid_out = self.got
        return jnp.concatenate([self.own, one, mid + mid_out, far + self.flying[0]], axis=0)


class Scatter:
    def __init__(self, parts, count):
        self.count, self.step, self.parts = count, 0, parts
        self.flying, self.two = [], None
        if count == 4:
            rows = parts.shape[0] // count
            self.part = [parts[i * rows : (i + 1) * rows] for i in range(4)]
            self.flying = [lax.ppermute(self.part[3], "col", IN)]
            self.two = lax.ppermute(self.part[2], "col", IN)

    def hop(self):
        if self.count != 4:
            return
        if self.step == 0:
            three = self.part[3] + self.flying[0]
            self.flying = [lax.ppermute(three, "col", MID), self.two]
        else:
            one, two = self.part[1] + self.flying[0], self.part[2] + self.flying[1]
            self.flying = [lax.ppermute(one, "col", PAIR), lax.ppermute(two, "col", MID)]
        self.step += 1

    def terms(self):
        if self.count != 4:
            mine = lax.psum_scatter(self.parts, "col", scatter_dimension=0, tiled=True)
            return (mine, jnp.zeros_like(mine), jnp.zeros_like(mine))
        return (self.part[0], *self.flying)


def sync(moving, *values):
    flat = [x for m in moving for x in m.flying] + list(values)
    flat = list(lax.optimization_barrier(tuple(flat)))
    for m in moving:
        count = len(m.flying)
        m.flying, flat = flat[:count], flat[count:]
    return flat[0] if len(flat) == 1 else flat


def params(mib, axes=1):
    return pltpu.CompilerParams(
        vmem_limit_bytes=mib * MIB, dimension_semantics=("arbitrary",) * axes
    )


SHARE = 8


def cost(flops, moved, trans=0):
    return pl.CostEstimate(
        flops=int(flops / SHARE),
        bytes_accessed=int(moved / SHARE),
        transcendentals=int(trans / SHARE),
    )


def stats_of(value):
    width = value.shape[1]
    average = jnp.sum(value, axis=1, keepdims=True) / width
    centred = value - average
    variance = jnp.sum(centred * centred, axis=1, keepdims=True) / width
    inv_root = lax.rsqrt(variance + EPSILON)
    return centred * inv_root, inv_root


def norm_first(stream, gain, shift):
    rows, width = stream.shape
    block = rows // 4

    def body(x_ref, gain_ref, shift_ref, low_ref):
        xhat, unused = stats_of(x_ref[...].astype(F32))
        low_ref[...] = (xhat * gain_ref[...] + shift_ref[...]).astype(BF16)

    row = pl.BlockSpec((block, width), lambda i: (i, 0))
    flat = pl.BlockSpec((1, width), lambda i: (0, 0))
    return pl.pallas_call(
        body,
        grid=(4,),
        in_specs=[row, flat, flat],
        out_specs=row,
        out_shape=jax.ShapeDtypeStruct((rows, width), BF16),
        compiler_params=params(6),
        cost_estimate=cost(rows * width * 10, rows * width * 4),
        name="norm_first",
    )(stream, gain, shift)


def norm_second(stream, terms, gain, shift):
    rows, width = stream.shape
    block = rows // 4

    def body(x_ref, a_ref, b_ref, c_ref, gain_ref, shift_ref, res_ref, low_ref):
        residual = (
            x_ref[...].astype(F32)
            + a_ref[...].astype(F32)
            + b_ref[...].astype(F32)
            + c_ref[...].astype(F32)
        )
        res_ref[...] = residual
        xhat, unused = stats_of(residual)
        low_ref[...] = (xhat * gain_ref[...] + shift_ref[...]).astype(BF16)

    row = pl.BlockSpec((block, width), lambda i: (i, 0))
    flat = pl.BlockSpec((1, width), lambda i: (0, 0))
    return pl.pallas_call(
        body,
        grid=(4,),
        in_specs=[row] * 4 + [flat, flat],
        out_specs=[row, row],
        out_shape=[
            jax.ShapeDtypeStruct((rows, width), F32),
            jax.ShapeDtypeStruct((rows, width), BF16),
        ],
        compiler_params=params(6),
        cost_estimate=cost(rows * width * 12, rows * width * 14),
        name="norm_second",
    )(stream, *terms, gain, shift)


def norm_back(stream, terms, upper, gain, both):
    rows, width = stream.shape
    block = rows // 4

    def body(x_ref, a_ref, b_ref, c_ref, up_ref, gain_ref, low_ref, sums_ref, *full_ref):
        xhat, inv_root = stats_of(x_ref[...].astype(F32))
        grad = a_ref[...].astype(F32) + b_ref[...].astype(F32) + c_ref[...].astype(F32)
        scaled = grad * gain_ref[...]
        mean_scaled = jnp.sum(scaled, axis=1, keepdims=True) / width
        mean_cross = jnp.sum(scaled * xhat, axis=1, keepdims=True) / width
        result = up_ref[...].astype(F32) + inv_root * (scaled - mean_scaled - xhat * mean_cross)
        low_ref[...] = result.astype(BF16)
        if full_ref:
            full_ref[0][...] = result

        @pl.when(pl.program_id(0) == 0)
        def _():
            sums_ref[...] = jnp.zeros_like(sums_ref)

        sums_ref[...] += jnp.concatenate(
            [
                jnp.sum(grad * xhat, axis=0, keepdims=True),
                jnp.sum(grad, axis=0, keepdims=True),
            ],
            axis=0,
        )

    row = pl.BlockSpec((block, width), lambda i: (i, 0))
    flat = pl.BlockSpec((1, width), lambda i: (0, 0))
    sums = pl.BlockSpec((2, width), lambda i: (0, 0))
    return pl.pallas_call(
        body,
        grid=(4,),
        in_specs=[row] * 5 + [flat],
        out_specs=[row, sums] + [row] * both,
        out_shape=[
            jax.ShapeDtypeStruct((rows, width), BF16),
            jax.ShapeDtypeStruct((2, width), F32),
        ]
        + [jax.ShapeDtypeStruct((rows, width), F32)] * both,
        compiler_params=params(10),
        cost_estimate=cost(rows * width * 20, rows * width * 18),
        name="norm_back",
    )(stream, *terms, upper, gain)


def cuts_of(sizes):
    ends = [sum(sizes[: i + 1]) for i in range(len(sizes))]
    return [(end - size, end) for end, size in zip(ends, sizes)]


def roll_lanes(value, shift):
    return pltpu.roll(value, shift % value.shape[1], 1)


def turn(value, table, sign):
    times = value.shape[1] // LANES
    wide = [jnp.concatenate([table[i]] * times, axis=1) for i in range(3)]
    ahead = roll_lanes(value, -(ROT // 2))
    behind = roll_lanes(value, ROT // 2)
    moved = ahead * wide[1] + behind * wide[2]
    return value * wide[0] + (moved if sign > 0 else -moved)


def qkv_columns(tokens, pieces, bias, table, half):
    rows, width = tokens.shape
    columns = pieces[0].shape[2] // 2
    cuts = cuts_of([p.shape[1] for p in pieces])

    def body(half_ref, x_ref, *refs):
        bias_ref, table_ref, out_ref = refs[-3:]
        which = pl.program_id(0)
        acc = bias_ref[0]
        for w_ref, (low, high) in zip(refs, cuts):
            acc = acc + jnp.dot(x_ref[:, low:high], w_ref[0], preferred_element_type=F32)

        @pl.when(which < 2)
        def _():
            out_ref[0] = turn(acc, table_ref, 1).astype(BF16)

        @pl.when(which == 2)
        def _():
            out_ref[0] = acc.astype(BF16)

    return pl.pallas_call(
        body,
        grid_spec=pltpu.PrefetchScalarGridSpec(
            num_scalar_prefetch=1,
            grid=(3,),
            in_specs=[pl.BlockSpec((rows, width), lambda j, h: (0, 0))]
            + [pl.BlockSpec((1, p.shape[1], columns), lambda j, h: (j, 0, h[0])) for p in pieces]
            + [
                pl.BlockSpec((1, 1, columns), lambda j, h: (j, 0, h[0])),
                pl.BlockSpec((3, rows, LANES), lambda j, h: (0, 0, 0)),
            ],
            out_specs=pl.BlockSpec((1, rows, columns), lambda j, h: (j, 0, 0)),
        ),
        out_shape=jax.ShapeDtypeStruct((3, rows, columns), BF16),
        compiler_params=params(16),
        cost_estimate=cost(6 * rows * width * columns, 2 * (rows * width + 3 * columns * width)),
        name="qkv_columns",
    )(half, tokens, *pieces, bias, table)


def place_of(order_ref, slot, core, rows):
    return pl.multiple_of((order_ref[1 + slot] * 2 + core) * rows, rows)


CHUNK = 256


def score_chunk(query, key, first):
    scores = lax.dot_general(query, key, (((1,), (1,)), ((), ())), preferred_element_type=F32)
    last = scores[:, first:]
    at_query = lax.broadcasted_iota(jnp.int32, last.shape, 0)
    at_key = lax.broadcasted_iota(jnp.int32, last.shape, 1)
    last = jnp.where(at_query >= at_key, last, -jnp.inf)
    return last if first == 0 else jnp.concatenate([scores[:, :first], last], axis=1)


def attend(mine, other, order, factor):
    unused, rows, columns = mine.shape
    slots = order.shape[0] - 1
    piece = rows // slots
    length = 2 * rows

    def body(order_ref, mine_ref, other_ref, out_mine, out_other, lse_ref, whole, result):
        core = order_ref[0]
        for slot in range(slots):
            here = slice(slot * piece, (slot + 1) * piece)
            whole[:, pl.ds(place_of(order_ref, slot, core, piece), piece), :] = mine_ref[:, here, :]
            whole[:, pl.ds(place_of(order_ref, slot, 1 - core, piece), piece), :] = other_ref[
                :, here, :
            ]
        for head in range(LANES // HEAD_DIM):
            lanes = slice(head * HEAD_DIM, (head + 1) * HEAD_DIM)
            for first in range(0, length, CHUNK):
                upto = first + CHUNK
                query = whole[0, first:upto, lanes] * jnp.bfloat16(factor)
                scores = score_chunk(query, whole[1, :upto, lanes], first)
                highest = jnp.max(scores, axis=1, keepdims=True)
                exponent = jnp.exp(scores - highest)
                summed = jnp.sum(exponent, axis=1, keepdims=True)
                mixed = jnp.dot(
                    exponent.astype(BF16), whole[2, :upto, lanes], preferred_element_type=F32
                )
                result[first:upto, lanes] = (mixed * (1.0 / summed)).astype(BF16)
                lse_ref[0, first:upto, head : head + 1] = highest + jnp.log(summed)
        for slot in range(slots):
            here = slice(slot * piece, (slot + 1) * piece)
            out_mine[here, :] = result[pl.ds(place_of(order_ref, slot, core, piece), piece), :]
            out_other[here, :] = result[pl.ds(place_of(order_ref, slot, 1 - core, piece), piece), :]

    groups = columns // LANES
    three = pl.BlockSpec((3, rows, LANES), lambda g, o: (0, 0, g))
    one = pl.BlockSpec((rows, LANES), lambda g, o: (0, g))
    return pl.pallas_call(
        body,
        grid_spec=pltpu.PrefetchScalarGridSpec(
            num_scalar_prefetch=1,
            grid=(groups,),
            in_specs=[three, three],
            out_specs=[one, one, pl.BlockSpec((1, length, 2), lambda g, o: (g, 0, 0))],
            scratch_shapes=[
                pltpu.VMEM((3, length, LANES), BF16),
                pltpu.VMEM((length, LANES), BF16),
            ],
        ),
        out_shape=[
            jax.ShapeDtypeStruct((rows, columns), BF16),
            jax.ShapeDtypeStruct((rows, columns), BF16),
            jax.ShapeDtypeStruct((groups, length, 2), F32),
        ],
        compiler_params=params(20),
        cost_estimate=cost(
            4 * length * length * columns, 16 * rows * columns, columns * length * length / 128
        ),
        name="attend",
    )(order, mine, other)


def attend_back(mine, other, grad_mine, grad_other, lse, table_mine, table_other, order, factor):
    unused, rows, columns = mine.shape
    slots = order.shape[0] - 1
    piece = rows // slots
    length = 2 * rows
    across = (((1,), (1,)), ((), ()))
    down = (((0,), (0,)), ((), ()))

    def body(
        order_ref,
        mine_ref,
        other_ref,
        gm_ref,
        go_ref,
        lse_ref,
        tm_ref,
        to_ref,
        out_mine,
        out_other,
        bias_ref,
        whole,
        grads,
        dq_ref,
        dkv_ref,
    ):
        core = order_ref[0]
        for slot in range(slots):
            here = slice(slot * piece, (slot + 1) * piece)
            one = pl.ds(place_of(order_ref, slot, core, piece), piece)
            two = pl.ds(place_of(order_ref, slot, 1 - core, piece), piece)
            whole[:, one, :] = mine_ref[:, here, :]
            whole[:, two, :] = other_ref[:, here, :]
            grads[one, :] = gm_ref[here, :]
            grads[two, :] = go_ref[here, :]
        heads = LANES // HEAD_DIM
        for head in range(heads):
            lanes = slice(head * HEAD_DIM, (head + 1) * HEAD_DIM)
            for first in reversed(range(0, length, CHUNK)):
                upto = first + CHUNK
                query = whole[0, first:upto, lanes] * jnp.bfloat16(factor)
                key = whole[1, :upto, lanes]
                value = whole[2, :upto, lanes]
                grad = grads[first:upto, lanes]
                scores = score_chunk(query, key, first)
                probs = jnp.exp(scores - lse_ref[0, first:upto, head : head + 1])
                probs_grad = lax.dot_general(grad, value, across, preferred_element_type=F32)
                shift = jnp.sum(probs * probs_grad, axis=1, keepdims=True)
                scores_grad = (probs * (probs_grad - shift)).astype(BF16)
                dq_ref[first:upto, lanes] = (
                    jnp.dot(scores_grad, key, preferred_element_type=F32) * factor
                )
                dk = lax.dot_general(scores_grad, query, down, preferred_element_type=F32)
                dv = lax.dot_general(
                    probs.astype(BF16), grad, down, preferred_element_type=F32
                )
                if upto == length:
                    dkv_ref[0, :, lanes] = dk
                    dkv_ref[1, :, lanes] = dv
                else:
                    dkv_ref[0, :upto, lanes] += dk
                    dkv_ref[1, :upto, lanes] += dv
        total = [jnp.zeros((1, LANES), F32) for _ in range(3)]
        for slot in range(slots):
            here = slice(slot * piece, (slot + 1) * piece)
            for at, table, out in (
                (core, tm_ref, out_mine),
                (1 - core, to_ref, out_other),
            ):
                rows_at = pl.ds(place_of(order_ref, slot, at, piece), piece)
                angles = table[:, here, :]
                parts = (
                    turn(dq_ref[rows_at, :], angles, -1).astype(BF16),
                    turn(dkv_ref[0, rows_at, :], angles, -1).astype(BF16),
                    dkv_ref[1, rows_at, :].astype(BF16),
                )
                for i in range(3):
                    out[i, here, :] = parts[i]
                    total[i] += jnp.sum(parts[i].astype(F32), axis=0, keepdims=True)
        for i in range(3):
            bias_ref[i] = total[i]

    groups = columns // LANES
    three = pl.BlockSpec((3, rows, LANES), lambda g, o: (0, 0, g))
    one = pl.BlockSpec((rows, LANES), lambda g, o: (0, g))
    full = pl.BlockSpec((3, rows, LANES), lambda g, o: (0, 0, 0))
    return pl.pallas_call(
        body,
        grid_spec=pltpu.PrefetchScalarGridSpec(
            num_scalar_prefetch=1,
            grid=(groups,),
            in_specs=[
                three,
                three,
                one,
                one,
                pl.BlockSpec((1, length, 2), lambda g, o: (g, 0, 0)),
                full,
                full,
            ],
            out_specs=[three, three, pl.BlockSpec((3, 1, LANES), lambda g, o: (0, 0, g))],
            scratch_shapes=[
                pltpu.VMEM((3, length, LANES), BF16),
                pltpu.VMEM((length, LANES), BF16),
                pltpu.VMEM((length, LANES), F32),
                pltpu.VMEM((2, length, LANES), F32),
            ],
        ),
        out_shape=[
            jax.ShapeDtypeStruct((3, rows, columns), BF16),
            jax.ShapeDtypeStruct((3, rows, columns), BF16),
            jax.ShapeDtypeStruct((3, 1, columns), F32),
        ],
        compiler_params=params(20),
        cost_estimate=cost(
            10 * length * length * columns, 40 * rows * columns, columns * length * length / 128
        ),
        name="attend_back",
    )(order, mine, other, grad_mine, grad_other, lse, table_mine, table_other)


ACROSS = (((1,), (1,)), ((), ()))
DOWN = (((0,), (0,)), ((), ()))


def feed_forward(tokens, pieces, hidden_grad):
    rows, width = tokens.shape
    units = pieces[0].shape[2]
    block = 256 if units > 256 else units
    cuts = cuts_of([p.shape[1] for p in pieces])

    def body(x_ref, *refs):
        hg_ref, hidden_ref, grad_ref = refs[-3:]
        gate_up = 0.0
        for w_ref, (low, high) in zip(refs, cuts):
            both = jnp.concatenate([w_ref[0], w_ref[1]], axis=1)
            gate_up += jnp.dot(x_ref[:, low:high], both, preferred_element_type=F32)
        gate, up = gate_up[:, :block], gate_up[:, block:]
        sigma = jax.nn.sigmoid(gate)
        silu = gate * sigma
        hidden_ref[...] = (silu * up).astype(BF16)
        grad = hg_ref[...].astype(F32)
        grad_ref[0] = (grad * up * (sigma + silu * (1.0 - sigma))).astype(BF16)
        grad_ref[1] = (grad * silu).astype(BF16)

    return pl.pallas_call(
        body,
        grid=(pl.cdiv(units, block),),
        in_specs=[pl.BlockSpec((rows, width), lambda j: (0, 0))]
        + [pl.BlockSpec((2, p.shape[1], block), lambda j: (0, 0, j)) for p in pieces]
        + [pl.BlockSpec((rows, block), lambda j: (0, j))],
        out_specs=[
            pl.BlockSpec((rows, block), lambda j: (0, j)),
            pl.BlockSpec((2, rows, block), lambda j: (0, 0, j)),
        ],
        out_shape=[
            jax.ShapeDtypeStruct((rows, units), BF16),
            jax.ShapeDtypeStruct((2, rows, units), BF16),
        ],
        compiler_params=params(20),
        cost_estimate=cost(
            4 * rows * width * units, 4 * width * units + 2 * rows * width, rows * units
        ),
        name="feed_forward",
    )(tokens, *pieces, hidden_grad)


def to_features(values, pieces, across):
    count, rows, units = values.shape
    axis = 1 if across else 2
    sizes = [p.shape[axis] for p in pieces]
    block = sizes[-1]
    width = sum(sizes)
    owner = [i for i, size in enumerate(sizes) for _ in range(size // block)]
    starts = [owner.index(i) for i in range(len(pieces))]
    dims = ACROSS if across else (((1,), (0,)), ((), ()))

    def body(v_ref, *refs):
        step = pl.program_id(0)
        for i, w_ref in enumerate(refs[:-1]):

            @pl.when((step >= starts[i]) & (step < starts[i] + sizes[i] // block))
            def _():
                total = 0.0
                for n in range(count):
                    total += lax.dot_general(v_ref[n], w_ref[n], dims, preferred_element_type=F32)
                refs[-1][...] = total.astype(BF16)

    def spec(i):
        last = sizes[i] // block - 1
        at = lambda j: jnp.clip(j - starts[i], 0, last)
        if across:
            return pl.BlockSpec((count, block, units), lambda j: (0, at(j), 0))
        return pl.BlockSpec((count, units, block), lambda j: (0, 0, at(j)))

    return pl.pallas_call(
        body,
        grid=(width // block,),
        in_specs=[pl.BlockSpec((count, rows, units), lambda j: (0, 0, 0))]
        + [spec(i) for i in range(len(pieces))],
        out_specs=pl.BlockSpec((rows, block), lambda j: (0, j)),
        out_shape=jax.ShapeDtypeStruct((rows, width), BF16),
        compiler_params=params(32),
        cost_estimate=cost(
            2 * count * rows * width * units, 2 * count * (width + rows) * units + 2 * rows * width
        ),
        name="to_features",
    )(values, *pieces)


def from_features(index, tokens, pieces, block):
    rows, width = tokens.shape
    cuts = cuts_of([p.shape[1] for p in pieces])
    count = index.shape[0]

    def body(index_ref, x_ref, *refs):
        total = 0.0
        for w_ref, (low, high) in zip(refs, cuts):
            total += lax.dot_general(
                x_ref[:, low:high], w_ref[...], ACROSS, preferred_element_type=F32
            )
        refs[-1][0] = total.astype(BF16)

    out = pl.pallas_call(
        body,
        grid_spec=pltpu.PrefetchScalarGridSpec(
            num_scalar_prefetch=1,
            grid=(count,),
            in_specs=[pl.BlockSpec((rows, width), lambda j, q: (0, 0))]
            + [pl.BlockSpec((block, p.shape[1]), lambda j, q: (q[j], 0)) for p in pieces],
            out_specs=pl.BlockSpec((1, rows, block), lambda j, q: (j, 0, 0)),
        ),
        out_shape=jax.ShapeDtypeStruct((count, rows, block), BF16),
        compiler_params=params(16),
        cost_estimate=cost(
            2 * rows * width * block * count, 2 * width * (rows + block * count)
        ),
        name="from_features",
    )(index, tokens, *pieces)
    return out


def grad_quarters(quarters, tokens, others, adds, rows_first, first=0, count=None):
    rows, width = tokens.shape
    units = others.shape[2]
    count = others.shape[0] if count is None else count
    quarter = width // 4
    k = quarters.shape[0]
    form = (quarter, units) if rows_first else (units, quarter)

    def body(q_ref, x_ref, y_ref, *refs):
        x, y = x_ref[...], y_ref[0]
        left, right = (x, y) if rows_first else (y, x)
        total = lax.dot_general(left, right, DOWN, preferred_element_type=F32)
        for ref in refs[:-1]:
            total += ref[0, 0].astype(F32)
        refs[-1][0, 0] = total.astype(BF16)

    def shifted(at_k, at_n):
        return pl.BlockSpec((1, 1, *form), lambda i, j, q: (i + at_k, j + at_n, 0, 0))

    return pl.pallas_call(
        body,
        grid_spec=pltpu.PrefetchScalarGridSpec(
            num_scalar_prefetch=1,
            grid=(k, count),
            in_specs=[
                pl.BlockSpec((rows, quarter), lambda i, j, q: (0, q[i])),
                pl.BlockSpec((1, rows, units), lambda i, j, q: (j + first, 0, 0)),
            ]
            + [shifted(at_k, at_n) for unused, at_k, at_n in adds],
            out_specs=shifted(0, 0),
        ),
        out_shape=jax.ShapeDtypeStruct((k, count, *form), BF16),
        compiler_params=params(20, 2),
        cost_estimate=cost(
            2 * k * count * rows * quarter * units,
            2 * k * count * quarter * units * (1 + len(adds)) + 2 * rows * (width + count * units),
        ),
        name="grad_quarters",
    )(quarters, tokens, others, *[add[0] for add in adds])


def join_pairs(core, parts, rests):
    rows, units = parts[0].shape[1:]
    block = 64 if rows % 64 == 0 else rows
    steps = rows // block

    def body(core_ref, *refs):
        half = pl.program_id(0)
        out_ref = refs[-1]
        for i in range(2):

            @pl.when(half == core_ref[0])
            def _():
                out_ref[:, i, :] = refs[i][0].astype(F32)

            @pl.when(half != core_ref[0])
            def _():
                out_ref[:, i, :] = refs[2 + i][0].astype(F32)

    def spec(same):
        def at(h, j, c):
            wanted = (h == c[0]) if same else (h != c[0])
            return (0, jnp.where(wanted, j, 0), 0)

        return pl.BlockSpec((1, block, units), at)

    return pl.pallas_call(
        body,
        grid_spec=pltpu.PrefetchScalarGridSpec(
            num_scalar_prefetch=1,
            grid=(2, steps),
            in_specs=[spec(True), spec(True), spec(False), spec(False)],
            out_specs=pl.BlockSpec((block, 2, units), lambda h, j, c: (h * steps + j, 0, 0)),
        ),
        out_shape=jax.ShapeDtypeStruct((2 * rows, 2, units), F32),
        compiler_params=params(8, 2),
        cost_estimate=cost(rows * units, 24 * rows * units),
        name="join_pairs",
    )(core, *parts, *rests)


def rotary_table(position):
    half = ROT // 2
    lane = jnp.arange(LANES) % HEAD_DIM
    frequency = 10000.0 ** (-((lane % half).astype(F32) * 2.0 / ROT))
    angles = position.astype(F32)[:, None] * frequency[None, :]
    lane = lane[None, :]
    cosine = jnp.where(lane < ROT, jnp.cos(angles), 1.0)
    sine = jnp.sin(angles)
    return jnp.stack(
        [
            cosine,
            jnp.where(lane < half, -sine, 0.0),
            jnp.where((lane >= half) & (lane < ROT), sine, 0.0),
        ]
    )


def local(
    inputs,
    first_gain,
    first_shift,
    project_in,
    project_bias,
    project_out,
    second_gain,
    second_shift,
    gate_weight,
    down_weight,
    cotangent,
):
    y_count = lax.axis_size("y")
    slots = lax.axis_size("col")
    y = lax.axis_index("y")
    core = lax.axis_index("core")
    row = lax.axis_index("row")
    place = lax.axis_index("col")
    factor = 1.0 / math.sqrt(HEAD_DIM)
    half_rows = inputs.shape[0] // 2
    wide = inputs.shape[1]
    width = 2 * wide

    def take(x, start, size, axis):
        return lax.dynamic_slice_in_dim(x, start, size, axis)

    straight = [(0, 0), (1, 2), (2, 1), (3, 3)]
    crossed = [(0, 2), (1, 0), (2, 3), (3, 1)]
    aligned = core == row

    def order_features(own, oth):
        low, high = oth[..., : wide // 2], oth[..., wide // 2 :]
        return jnp.concatenate(
            [own, jnp.where(core == 0, low, high), jnp.where(core == 0, high, low)], axis=-1
        )

    def natural(oth):
        low, high = oth[..., : wide // 2], oth[..., wide // 2 :]
        return jnp.concatenate(
            [jnp.where(core == 0, low, high), jnp.where(core == 0, high, low)], axis=-1
        )

    def to_sequence(x):
        a = lax.ppermute(take(x, row * half_rows, half_rows, 0), ("core", "row"), straight)
        b = lax.ppermute(take(x, (1 - row) * half_rows, half_rows, 0), ("core", "row"), crossed)
        return order_features(jnp.where(aligned, a, b), jnp.where(aligned, b, a))

    def from_sequence(x):
        own, oth = x[:, :wide], natural(x[:, wide:])
        a = jnp.where(aligned, own, oth)
        b = jnp.where(aligned, oth, own)
        a = lax.ppermute(a, ("core", "row"), [(j, i) for i, j in straight])
        b = lax.ppermute(b, ("core", "row"), [(j, i) for i, j in crossed])
        top = jnp.where(row == 0, a, b)
        bottom = jnp.where(row == 0, b, a)
        return jnp.concatenate([top, bottom], axis=0)

    order = slot_order(place, slots)
    table_of = jnp.concatenate([core[None], order]).astype(jnp.int32)
    inside = jnp.arange(half_rows)
    position = lambda c: ((order[:, None] * 2 + c) * half_rows + inside[None, :]).reshape(-1)
    rotary_mine = rotary_table(position(core))
    rotary_other = rotary_table(position(1 - core))

    stream = to_sequence(inputs)
    vectors = jnp.concatenate([first_gain, first_shift, second_gain, second_shift], axis=0)
    vectors = order_features(vectors, swap(vectors, "row"))
    gain_a, shift_a, gain_b, shift_b = (vectors[i : i + 1] for i in range(4))

    def part_of(w, axis):
        part = w.shape[axis] // 2
        return take(w, core * part, part, axis)

    w_in = jnp.transpose(project_in[0], (1, 0, 2))
    w_out, w_down = project_out[0], down_weight[0]
    w_gate = jnp.transpose(gate_weight[0], (1, 0, 2))
    fixed = 0 * core

    def quarters(*q):
        return jnp.stack(q).astype(jnp.int32)

    def for_core(tokens, others, rows_first, **span):
        return grad_quarters(quarters(1 - core, 3 + fixed), tokens, others, (), rows_first, **span)

    def for_row(tokens, others, rows_first, got, at=0, **span):
        return grad_quarters(
            quarters(2 + fixed), tokens, others, ((got, 1, at),), rows_first, **span
        )

    def for_y(tokens, others, rows_first, got, arrived, at=0, **span):
        adds = ((got, 0, at), (arrived, 0, 0))
        return grad_quarters(quarters(core), tokens, others, adds, rows_first, **span)[0]

    def y_swap(own):
        return swap(own, "y") if y_count == 2 else lax.psum(own, "y")

    def y_total(own, other):
        return (own.astype(F32) + other.astype(F32)).astype(BF16) if y_count == 2 else other

    def join(total, rest, axis):
        return jnp.concatenate(
            [jnp.where(core == 0, total, rest), jnp.where(core == 0, rest, total)], axis=axis
        ).astype(F32)

    low_a = norm_first(stream, gain_a, shift_a)
    in_half = swap(after(part_of(w_in, 1), stream), "row")
    cot = to_sequence(after(cotangent, low_a))
    hops = Gather(low_a, slots)
    rotary_mine = sync([hops], rotary_mine)
    hops.hop()
    rotary_other, out_part, down_part = sync(
        [hops], rotary_other, part_of(w_out, 1), part_of(w_down, 1)
    )
    hops.hop()
    out_half = swap(out_part, "row")
    w_gate, gate_part, in_half, cot = sync([hops], w_gate, part_of(w_gate, 1), in_half, cot)
    tokens_a = hops.rows()
    pieces_in = (w_in, in_half, swap(in_half, "core"))
    cot_hops = Gather(cot, slots)
    down_half = swap(after(down_part, cot), "row")
    bias = project_bias[0][:, None, :]
    qkv_other = qkv_columns(tokens_a, pieces_in, bias, rotary_mine, (1 - core)[None])
    qkv_from = swap(qkv_other, "core")
    qkv_mine = qkv_columns(tokens_a, pieces_in, bias, rotary_mine, core[None])
    out_mine, out_other, lse = attend(qkv_mine, qkv_from, table_of, factor)
    out_mine, out_other, out_half = sync([cot_hops], out_mine, out_other, out_half)
    cot_hops.hop()
    pieces_out = (w_out, out_half, swap(out_half, "core"))
    out_from = swap(out_other, "core")
    attended = jnp.concatenate(
        [jnp.where(core == 0, out_mine, out_from), jnp.where(core == 0, out_from, out_mine)], axis=1
    )
    part_out = to_features(attended[None], [p[None] for p in pieces_out], False)
    part_out, gate_part = sync([], part_out, gate_part)
    hops = Scatter(part_out, slots)
    down_half = sync([hops, cot_hops], down_half)
    hops.hop()
    cot_hops.hop()
    gate_half = swap(after(gate_part, down_half), "row")
    down_rest = sync([hops, cot_hops], swap(down_half, "core"))
    hops.hop()
    pieces_down = (w_down, down_half, down_rest)
    units = w_down.shape[0]
    ways = 2 if units % 32 == 0 else 1
    grad_rows = cot_hops.rows()
    hidden_grad = from_features(
        jnp.arange(ways, dtype=jnp.int32), grad_rows, pieces_down, units // ways
    )
    hidden_grad = jnp.concatenate([hidden_grad[i] for i in range(ways)], axis=1)
    grad_rows, hidden_grad = sync([hops], grad_rows, hidden_grad)
    residual, low_b = norm_second(stream, hops.terms(), gain_b, shift_b)

    hops = Gather(low_b, slots)
    sync([hops], low_b)
    hops.hop()
    gate_half = sync([hops], gate_half)
    hops.hop()
    gate_half, gate_rest = sync([hops], gate_half, swap(gate_half, "core"))
    tokens_b = hops.rows()
    pieces_gate = (w_gate, gate_half, gate_rest)
    hidden, pair = feed_forward(tokens_b, pieces_gate, hidden_grad)
    part_b = to_features(pair, pieces_gate, True)
    part_b, hidden, pair = sync([], part_b, hidden, pair)

    hops = Scatter(part_b, slots)
    down_sent = for_core(grad_rows, hidden[None], False)
    gate_sent = for_core(tokens_b, pair, True)
    down_sent, gate_sent = sync([hops], down_sent, gate_sent)
    hops.hop()
    down_got = swap(down_sent, "core")
    gate_got = swap(gate_sent, "core")
    down_oth = for_row(grad_rows, hidden[None], False, down_got)
    down_oth, gate_got = sync([hops], down_oth, gate_got)
    hops.hop()
    down_arrived = swap(down_oth, "row")
    gate_oth = [
        for_row(tokens_b, pair, True, gate_got, at=i, first=i, count=1) for i in range(2)
    ]
    gate_oth = list(sync([hops], *gate_oth))
    g2_low, sums_b, g2 = norm_back(residual, hops.terms(), cot, gain_b, 1)

    hops = Gather(g2_low, slots)
    gate_arrived = [swap(gate_oth[0], "row"), None]
    part_down = to_features(hidden[None], [p[None] for p in pieces_down], False)
    part_down, down_arrived = sync([hops], part_down, down_arrived)
    hops.hop()
    down_own = for_y(grad_rows, hidden[None], False, down_got, down_arrived)
    down_own, part_down = sync([hops], down_own, part_down)
    hops.hop()
    down_other = y_swap(down_own)
    gate_arrived[0], gate_oth[1] = sync([hops], gate_arrived[0], gate_oth[1])
    gate_arrived[1] = swap(gate_oth[1], "row")
    g2_rows = hops.rows()
    columns = w_out.shape[0] // 2
    grad_other = from_features((1 - core)[None], g2_rows, pieces_out, columns)[0]
    grad_from = swap(grad_other, "core")
    grad_mine = from_features(core[None], g2_rows, pieces_out, columns)[0]
    gate_own = [
        for_y(tokens_b, pair, True, gate_got, gate_arrived[0], at=0, first=0, count=1),
        None,
    ]
    out_sent = for_core(g2_rows, attended[None], False)
    grad_from, grad_mine, out_sent, gate_own[0], part_down, down_other = sync(
        [], grad_from, grad_mine, out_sent, gate_own[0], part_down, down_other
    )
    down_hops = Scatter(part_down, slots)
    gate_other = [y_swap(gate_own[0]), None]
    out_got = swap(out_sent, "core")
    mixed_mine, mixed_other, bias_part = attend_back(
        qkv_mine, qkv_from, grad_mine, grad_from, lse, rotary_mine, rotary_other, table_of, factor
    )
    mixed_mine, mixed_other, out_got, gate_arrived[1] = sync(
        [down_hops], mixed_mine, mixed_other, out_got, gate_arrived[1]
    )
    down_hops.hop()
    mixed_from = swap(mixed_other, "core")
    out_oth = for_row(g2_rows, attended[None], False, out_got)
    gate_own[1] = for_y(tokens_b, pair, True, gate_got, gate_arrived[1], at=1, first=1, count=1)
    mixed = jnp.concatenate(
        [
            jnp.where(core == 0, mixed_mine, mixed_from),
            jnp.where(core == 0, mixed_from, mixed_mine),
        ],
        axis=2,
    )
    in_sent = for_core(tokens_a, mixed, True)
    part_a = to_features(mixed, pieces_in, True)
    part_a, in_sent, mixed, gate_own[1], gate_other[0], out_oth = sync(
        [], part_a, in_sent, mixed, gate_own[1], gate_other[0], out_oth
    )
    in_got = swap(in_sent, "core")
    out_arrived = swap(out_oth, "row")
    gate_other[1] = y_swap(gate_own[1])
    part_a, in_got, out_arrived = sync([], part_a, in_got, out_arrived)
    hops = Scatter(part_a, slots)
    spans = (dict(at=0, first=0, count=2), dict(at=2, first=2, count=1))
    in_oth = [for_row(tokens_a, mixed, True, in_got, **span) for span in spans]
    in_arrived = [swap(x, "row") for x in in_oth]
    out_own = for_y(g2_rows, attended[None], False, out_got, out_arrived)
    *in_oth, out_own = sync([hops, down_hops], *in_oth, out_own)
    hops.hop()
    down_total = y_total(down_own, down_other)
    gate_total = [y_total(gate_own[0], gate_other[0]), None]
    in_arrived[0], gate_other[1], down_total, gate_total[0] = sync(
        [hops], in_arrived[0], gate_other[1], down_total, gate_total[0]
    )
    hops.hop()
    out_other_y = y_swap(out_own)
    in_own = [for_y(tokens_a, mixed, True, in_got, in_arrived[0], **spans[0])]
    gate_total[1] = y_total(gate_own[1], gate_other[1])
    in_own[0], gate_total[1], in_arrived[1], out_other_y = sync(
        [hops], in_own[0], gate_total[1], in_arrived[1], out_other_y
    )
    in_other = [y_swap(in_own[0])]
    input_low, sums_a = norm_back(stream, hops.terms(), g2, gain_a, 0)
    down_rest = swap(down_total, "core")
    gate_rest = [swap(x, "core") for x in gate_total]
    out_total = y_total(out_own, out_other_y)
    out_rest = swap(out_total, "core")
    in_own.append(for_y(tokens_a, mixed, True, in_got, in_arrived[1], **spans[1]))
    input_low, sums_a, in_own[1], down_rest, out_rest, *gate_rest = sync(
        [], input_low, sums_a, in_own[1], down_rest, out_rest, *gate_rest
    )

    bias_all = jnp.zeros((3, 2 * slots * columns), F32)
    bias_all = lax.dynamic_update_slice(
        bias_all, bias_part[:, 0, :], (jnp.int32(0), (place * 2 + core) * columns)
    ).reshape(-1, wide)
    sums = jnp.concatenate([sums_a, sums_b], axis=0)
    own, oth = sums[:, :wide], natural(sums[:, wide:])
    total = jnp.concatenate([own, bias_all, oth], axis=0)

    in_other.append(y_swap(in_own[1]))
    input_grad = from_sequence(input_low)
    down_grad = join(down_total, down_rest, 2)[0]
    if slots == 4:
        arrived = lax.ppermute(total, "col", PAIR)
        arrived, input_grad, down_grad = sync([], arrived, input_grad, down_grad)
        total = total + arrived
        arrived = sync([], lax.ppermute(total, "col", MID))
        total = total + arrived
        outer, in_other[0], gate_total[0] = sync(
            [], lax.ppermute(total, "col", OUT), in_other[0], gate_total[0]
        )
        total = jnp.where((place == 0) | (place == 3), outer, total)
        down_hops.flying = list(tie(down_hops.flying, outer))
        down_hops.hop()
        arrived = swap(total, "core")
        gate_grad = join_pairs(core[None], gate_total, gate_rest)
        arrived, gate_grad, in_other[1] = sync([down_hops], arrived, gate_grad, in_other[1])
        total = total + arrived
    else:
        gate_grad = join_pairs(core[None], gate_total, gate_rest)
        total = lax.psum(total, "col")
        total = total + swap(total, "core")
    cut = own.shape[0] + bias_all.shape[0]
    arrived = swap(jnp.concatenate([total[cut:], total[own.shape[0] : cut]], axis=0), "row")
    layer_low = (residual + sum(t.astype(F32) for t in down_hops.terms())).astype(BF16)
    in_total = [y_total(x, o) for x, o in zip(in_own, in_other)]
    in_rest = [swap(x, "core") for x in in_total]
    arrived, layer_low, *in_rest = sync([], arrived, layer_low, *in_rest)
    total = total[:cut] + arrived
    vectors = lax.psum(total, "y") if y_count != 2 else total + swap(total, "y")
    layer_out = from_sequence(layer_low)
    out_grad = join(out_total, out_rest, 2)[0]
    in_grad = jnp.concatenate([join(x, r, 1) for x, r in zip(in_total, in_rest)], axis=0)
    bias_grad = take(vectors[4:].reshape(3, -1), place * 2 * columns, 2 * columns, 1)
    input_grad = input_grad.astype(F32)
    return (
        layer_out[None],
        input_grad,
        vectors[0:1],
        vectors[1:2],
        jnp.transpose(in_grad, (1, 0, 2))[None],
        bias_grad[None],
        out_grad[None],
        vectors[2:3],
        vectors[3:4],
        gate_grad[None],
        down_grad[None],
    )


def solution(mesh):
    dp, rows, cols = (mesh.shape[a] for a in ("dp", "row", "col"))
    split = Mesh(mesh.devices.reshape(dp // 2, 2, rows, cols), ("y", "core", "row", "col"))
    tokens = ("y", "core", "col")
    return jax.shard_map(
        local,
        mesh=split,
        in_specs=(
            P(tokens, "row"),
            P(None, "row"),
            P(None, "row"),
            P(None, "row", None, "col"),
            P(None, None, "col"),
            P(None, "col", "row"),
            P(None, "row"),
            P(None, "row"),
            P(None, "row", None, "col"),
            P(None, "col", "row"),
            P(tokens, "row"),
        ),
        out_specs=(
            P(None, tokens, "row"),
            P(tokens, "row"),
            P(None, "row"),
            P(None, "row"),
            P(None, "row", None, "col"),
            P(None, None, "col"),
            P(None, "col", "row"),
            P(None, "row"),
            P(None, "row"),
            P(None, "row", None, "col"),
            P(None, "col", "row"),
        ),
        check_vma=False,
    )
```
